128 devices in a mesh: row: 16 (over x, y), col: 8 (over z, core).
Axes of the slice: x: 4, y: 4, z: 4, core: 2. Of those that a mesh axis runs over, the one named last changes fastest.
Arguments:
- node_feats: bfloat16 [32768, 512], P('row', 'col'), may hold values from -6 to 6
- hidden_act: bfloat16 [32768, 512], P('row', 'col'), may hold values from 0 to 2
- grad_out: bfloat16 [32768, 512], P('row', 'col'), may hold values from -6 to 6
- relu_mask: int32 [32768, 512], P('row', 'col'), may hold values 0 or 1
- edge_tiles: bfloat16 [256, 20, 128, 128], P('row'), may hold values from -0.125 to 0.125
- block_cols: int32 [256, 20], P('row'), may hold values from 0 to 255
- weight_one: bfloat16 [512, 512], P('col'), may hold values from -0.25 to 0.25
- weight_two: bfloat16 [512, 512], P('col'), may hold values from -0.25 to 0.25
Outputs:
- input_grad: bfloat16 [32768, 512], P('row', 'col')
- first_grad: float32 [512, 512], P('col')
- second_grad: float32 [512, 512], P('col')
The draws below stay inside these ranges and needn't reach their ends.
All inputs are finite; a program needn't handle non-finite values. No bound on the sum of `relu_mask` on one device may be relied on, other than what follows from the above.
Results may differ from the reference program's by a relative error of at most 0.03.
Values may be sent and summed in bfloat16 or wider, within the bound.
A program may use at most 128 MiB of HBM per device.

```python
import math
import jax
import jax.numpy as jnp
import numpy as np
from jax import lax

D = 512
BS = 128
K = 20
ROWB_DEV = 16
NB = 256
N = 32768


def plant(values, key, smallest, top_value):
    longest = values.shape.index(max(values.shape))
    spots = []
    for shift in (0, 1):
        where = [jax.random.randint(jax.random.fold_in(key, axis), (), 0, length) for axis, length in enumerate(values.shape)]
        where[longest] = (where[longest] + shift) % values.shape[longest]
        spots.append(tuple(where))
    return values.at[spots[0]].set(smallest).at[spots[1]].set(top_value)


def block_levels(stream_key, extent, split, smallest, top_value):
    factor_of = 1.0
    for axis_at, blocks in split:
        draws = jax.random.uniform(jax.random.fold_in(jax.random.fold_in(stream_key, 6), axis_at), (blocks,), jnp.float32, smallest / len(split), top_value / len(split))
        factor_of = factor_of * jnp.repeat(jnp.exp(draws), extent[axis_at] // blocks).reshape((-1,) + (1,) * (len(extent) - 1 - axis_at))
    return factor_of


def rank_table(count, slope):
    loads = [(1 << 20) // math.isqrt(rank ** slope) + 1 for rank in range(1, count + 1)]
    scale = 1 + sum(loads) // (1 << 30)
    return np.cumsum(np.array([max(1, weight // scale) for weight in loads]))


def ranked_ids(key, dims, amount, skew):
    grid = rank_table(amount, skew)
    pick = jax.random.randint(jax.random.fold_in(key, 1), dims, 0, int(grid[amount - 1]))
    standing = jnp.searchsorted(jnp.asarray(grid, jnp.int32), pick, side="right")
    return jax.random.permutation(jax.random.fold_in(key, 2), amount)[standing].astype(jnp.int32)


def scatter_about(own_key, shape, width, limit, cuts=(), held_as=jnp.bfloat16):
    drawn = jax.random.normal(own_key, shape, jnp.float32) * width
    if len(cuts) > 0:
        drawn = block_levels(own_key, shape, cuts, -0.22, 0.18) * drawn
    return jnp.clip(drawn, min=-limit, max=limit).astype(held_as)


def setup_inputs(seed: int = 0) -> dict:
    seeds = jax.random.split(jax.random.key(seed), 9)
    return {
        "node_feats": scatter_about(seeds[0], (N, D), 1.0, 6.0, ((0, 16), (1, 8))),
        "hidden_act": jnp.clip(2.0 * jax.random.uniform(seeds[1], (N, D), jnp.float32) ** block_levels(seeds[1], (N, D), ((0, 16), (1, 8)), -0.2, 0.2), 0.0, 2.0).astype(jnp.bfloat16),
        "grad_out": scatter_about(seeds[2], (N, D), 1.0, 6.0, ((0, 16), (1, 8))),
        "relu_mask": plant((jax.random.randint(seeds[3], (N, D), 0, 2) < 1).astype(jnp.int32), jax.random.fold_in(seeds[3], 1), 0, 1),
        "edge_tiles": scatter_about(seeds[4], (NB, K, BS, BS), (K * BS) ** -0.5, 0.125, ((0, 16),)),
        "block_cols": plant(ranked_ids(seeds[5], (NB, K), NB, 1), jax.random.fold_in(seeds[5], 3), 0, NB - 1).astype(jnp.int32),
        "weight_one": scatter_about(seeds[6], (D, D), D ** -0.5, 0.25, ((0, 8),)),
        "weight_two": scatter_about(seeds[7], (D, D), D ** -0.5, 0.25, ((0, 8),)),
    }


def aggregate(edge_tiles, block_cols, values):
    table = values.reshape(NB, BS, values.shape[1])

    def one_row(pair):
        tiles_row, cols_row = pair
        picked = table[cols_row.astype(jnp.int32)]
        return jnp.einsum("kij,kjd->id", tiles_row.astype(jnp.float32), picked.astype(jnp.float32))

    summed = lax.map(one_row, (edge_tiles, block_cols))
    return summed.reshape(N, values.shape[1])


def spread(edge_tiles, block_cols, values):
    feat_cols = values.shape[1]
    blocks = values.reshape(NB, BS, feat_cols)

    def one_group(group, carry):
        first_row = (group * ROWB_DEV).astype(jnp.int32)
        tiles_group = lax.dynamic_slice_in_dim(edge_tiles, first_row, ROWB_DEV, 0)
        cols_group = lax.dynamic_slice_in_dim(block_cols, first_row, ROWB_DEV, 0)
        vals_group = lax.dynamic_slice_in_dim(blocks, first_row, ROWB_DEV, 0)
        terms = jnp.einsum("rkij,rid->rkjd", tiles_group.astype(jnp.float32), vals_group.astype(jnp.float32))
        partial_sum = jax.ops.segment_sum(terms.reshape(ROWB_DEV * K, BS, feat_cols), cols_group.reshape(-1), num_segments=NB)
        rounded = lax.optimization_barrier(partial_sum.astype(jnp.bfloat16))
        return carry + rounded.astype(jnp.float32)

    start_sum = jnp.zeros((NB, BS, feat_cols), jnp.float32)
    total = lax.fori_loop(0, NB // ROWB_DEV, one_group, start_sum)
    return total.reshape(N, feat_cols)


def reference(node_feats, hidden_act, grad_out, relu_mask, edge_tiles, block_cols, weight_one, weight_two):
    agg_feats = aggregate(edge_tiles, block_cols, node_feats).astype(jnp.bfloat16)
    agg_hidden = aggregate(edge_tiles, block_cols, hidden_act).astype(jnp.bfloat16)
    second_grad = jnp.dot(agg_hidden.T, grad_out, preferred_element_type=jnp.float32)
    d_hidden_agg = jnp.dot(grad_out, weight_two.T, preferred_element_type=jnp.float32).astype(jnp.bfloat16)
    hidden_grad = spread(edge_tiles, block_cols, d_hidden_agg)
    delta = (hidden_grad * relu_mask.astype(jnp.float32)).astype(jnp.bfloat16)
    first_grad = jnp.dot(agg_feats.T, delta, preferred_element_type=jnp.float32)
    d_feats_agg = jnp.dot(delta, weight_one.T, preferred_element_type=jnp.float32).astype(jnp.bfloat16)
    input_grad = spread(edge_tiles, block_cols, d_feats_agg).astype(jnp.bfloat16)
    return (input_grad, first_grad, second_grad)
```

```python
import functools
import jax
import jax.numpy as jnp
from jax import lax
from jax.experimental import pallas as pl
from jax.experimental.pallas import tpu as pltpu
from jax.sharding import PartitionSpec as P


def spread_kernel(cols_ref, vals_ref, tiles_ref, out_ref, acc_ref):
    step = pl.program_id(0)
    feats = vals_ref.shape[0]
    side = tiles_ref.shape[2]
    per_row = tiles_ref.shape[1]

    @pl.when(step == 0)
    def _():
        acc_ref[...] = jnp.zeros_like(acc_ref)

    vals = vals_ref[...]
    blank = jnp.zeros((feats, side), vals.dtype)
    left = jnp.concatenate(
        [
            jnp.concatenate([vals[:, :side], blank], axis=1),
            jnp.concatenate([blank, vals[:, side:]], axis=1),
        ],
        axis=0,
    )
    for k in range(0, per_row, 2):
        right = jnp.concatenate(
            [
                jnp.concatenate([tiles_ref[0, k], tiles_ref[0, k + 1]], axis=1),
                jnp.concatenate([tiles_ref[1, k], tiles_ref[1, k + 1]], axis=1),
            ],
            axis=0,
        )
        term = jnp.dot(left, right, preferred_element_type=jnp.float32)
        for row in range(2):
            for at in range(2):
                acc_ref[cols_ref[2 * step + row, k + at]] += term[
                    row * feats : (row + 1) * feats, at * side : (at + 1) * side
                ]

    @pl.when(step == pl.num_programs(0) - 1)
    def _():
        out_ref[...] = acc_ref[...].astype(out_ref.dtype)


def spread(block_cols, vals_t, edge_tiles, blocks):
    rows, per_row, side, _ = edge_tiles.shape
    feats = vals_t.shape[0]
    return pl.pallas_call(
        spread_kernel,
        out_shape=jax.ShapeDtypeStruct((blocks, feats, side), jnp.bfloat16),
        grid_spec=pltpu.PrefetchScalarGridSpec(
            num_scalar_prefetch=1,
            grid=(rows // 2,),
            in_specs=[
                pl.BlockSpec((feats, 2 * side), lambda i, c: (0, i)),
                pl.BlockSpec((2, per_row, side, side), lambda i, c: (i, 0, 0, 0)),
            ],
            out_specs=pl.BlockSpec((blocks, feats, side), lambda i, c: (0, 0, 0)),
            scratch_shapes=[pltpu.VMEM((blocks, feats, side), jnp.float32)],
        ),
        compiler_params=pltpu.CompilerParams(vmem_limit_bytes=48 << 20),
    )(block_cols, vals_t, edge_tiles)


def per_device(
    node_feats, hidden_act, grad_out, relu_mask, edge_tiles, block_cols, weight_one, weight_two
):
    rows_dev, feat_cols = node_feats.shape
    side = edge_tiles.shape[2]
    blocks_dev = rows_dev // side
    blocks = blocks_dev * lax.axis_size("row")

    def layer(vals_t, weight, acts):
        part = spread(block_cols, vals_t, edge_tiles, blocks)
        mine = lax.psum_scatter(part, "row", scatter_dimension=0, tiled=True)
        full = lax.all_gather(mine, "col", axis=1, tiled=True)
        acts_b = acts.T.reshape(feat_cols, blocks_dev, side)
        weight_grad = jnp.einsum("fbn,bgn->fg", acts_b, full, preferred_element_type=jnp.float32)
        value_grad = jnp.einsum("fg,bgn->fbn", weight, full, preferred_element_type=jnp.float32)
        weight_grad = lax.psum(weight_grad.astype(jnp.bfloat16), "row").astype(jnp.float32)
        return value_grad.reshape(feat_cols, rows_dev), weight_grad

    hidden_grad, second_grad = layer(grad_out.T, weight_two, hidden_act)
    delta_t = (hidden_grad * relu_mask.T.astype(jnp.float32)).astype(jnp.bfloat16)
    input_grad, first_grad = layer(delta_t, weight_one, node_feats)
    return (input_grad.astype(jnp.bfloat16).T, first_grad, second_grad)


def solution(mesh):
    in_specs = (
        P("row", "col"),
        P("row", "col"),
        P("row", "col"),
        P("row", "col"),
        P("row", None, None, None),
        P("row", None),
        P("col", None),
        P("col", None),
    )
    out_specs = (P("row", "col"), P("col", None), P("col", None))
    return jax.shard_map(
        per_device, mesh=mesh, in_specs=in_specs, out_specs=out_specs, check_vma=False
    )
```

```python
import functools
import jax
import jax.numpy as jnp
from jax import lax
from jax.experimental import pallas as pl
from jax.experimental.pallas import tpu as pltpu
from jax.sharding import PartitionSpec as P

RING = 4
MESH = pl.DeviceIdType.MESH


def spread_kernel(cols_ref, vals_ref, tiles_ref, out_ref, acc_ref):
    step = pl.program_id(0)
    feats = vals_ref.shape[0]
    side = tiles_ref.shape[2]
    per_row = tiles_ref.shape[1]

    @pl.when(step == 0)
    def _():
        acc_ref[...] = jnp.zeros_like(acc_ref)

    vals = vals_ref[...]
    blank = jnp.zeros((feats, side), vals.dtype)
    left = jnp.concatenate(
        [
            jnp.concatenate([vals[:, :side], blank], axis=1),
            jnp.concatenate([blank, vals[:, side:]], axis=1),
        ],
        axis=0,
    )
    for k in range(0, per_row, 2):
        right = jnp.concatenate(
            [
                jnp.concatenate([tiles_ref[0, k], tiles_ref[0, k + 1]], axis=1),
                jnp.concatenate([tiles_ref[1, k], tiles_ref[1, k + 1]], axis=1),
            ],
            axis=0,
        )
        term = jnp.dot(left, right, preferred_element_type=jnp.float32)
        for row in range(2):
            for at in range(2):
                acc_ref[cols_ref[2 * step + row, k + at]] += term[
                    row * feats : (row + 1) * feats, at * side : (at + 1) * side
                ]

    @pl.when(step == pl.num_programs(0) - 1)
    def _():
        per_dev = out_ref.shape[2]
        half = feats // 2
        for x in range(RING):
            for y in range(RING):
                got = acc_ref[pl.ds((x * RING + y) * per_dev, per_dev)].astype(out_ref.dtype)
                out_ref[0, x * RING + y] = got[:, :half]
                out_ref[1, y * RING + x] = got[:, half:]


def spread(block_cols, vals_t, edge_tiles):
    rows, per_row, side, _ = edge_tiles.shape
    feats = vals_t.shape[0]
    blocks = rows * RING * RING
    out = (2, RING * RING, rows, feats // 2, side)
    return pl.pallas_call(
        spread_kernel,
        out_shape=jax.ShapeDtypeStruct(out, jnp.bfloat16),
        grid_spec=pltpu.PrefetchScalarGridSpec(
            num_scalar_prefetch=1,
            grid=(rows // 2,),
            in_specs=[
                pl.BlockSpec((feats, 2 * side), lambda i, c: (0, i)),
                pl.BlockSpec((2, per_row, side, side), lambda i, c: (i, 0, 0, 0)),
            ],
            out_specs=pl.BlockSpec(out, lambda i, c: (0, 0, 0, 0, 0)),
            scratch_shapes=[pltpu.VMEM((blocks, feats, side), jnp.float32)],
        ),
        compiler_params=pltpu.CompilerParams(vmem_limit_bytes=28 << 20),
    )(block_cols, vals_t, edge_tiles)


def layer_kernel(masked, *refs):
    part_ref, weight_ref, acts_ref = refs[:3]
    refs = refs[3:]
    if masked:
        mask_ref, refs = refs[0], refs[1:]
    value_ref, grad_ref = refs[:2]
    (
        in1, mid, own, in2, full, mine, gather1, gather2,
        s1, r1, s2, r2, sz, rz, sf, rf, sc, rc, sg, rg, sb, rb,
    ) = refs[2:]
    blk = part_ref.shape[2]
    hb = blk // 2
    half = part_ref.shape[3]
    side = part_ref.shape[4]
    feats = 2 * half
    f32, bf16 = jnp.float32, jnp.bfloat16

    row, col = lax.axis_index("row"), lax.axis_index("col")
    pos = (row // RING, lax.rem(row, RING))
    z, core = col // 2, lax.rem(col, 2)

    def wrap(v):
        return lax.rem(v + RING, RING)

    step = (1, -1)

    def plane(axis, d):
        x, y = pos
        if axis == 0:
            return (wrap(x + step[d]) * RING + y, col)
        return (x * RING + wrap(y + step[d]), col)

    def along(d):
        return (row, wrap(z + step[d]) * 2 + core)

    sibling = (row, z * 2 + 1 - core)
    peers = [(lax.rem(row + off, RING * RING), col) for off in range(1, RING * RING)]

    barrier = pltpu.get_barrier_semaphore()
    met = peers + [along(0), along(1), sibling]
    for dev in met:
        pl.semaphore_signal(barrier, inc=1, device_id=dev, device_id_type=MESH)
    pl.semaphore_wait(barrier, len(met))

    def remote(src, dst, send, recv, dev):
        return pltpu.make_async_remote_copy(
            src_ref=src, dst_ref=dst, send_sem=send, recv_sem=recv, device_id=dev, device_id_type=MESH
        )

    def part_of(h, q1, q2, lo):
        return part_ref.at[h, q1 * RING + q2, pl.ds(lo * hb, hb)]

    started = []

    def go(copy):
        copy.start()
        started.append(copy)
        return copy

    order = (2, 1, -1, 0)
    far, near, both = {}, {}, {}

    def start_far(h, d, j):
        p1, p2 = pos[h], pos[1 - h]
        far[h, d, j] = go(remote(
            part_of(h, wrap(p1 + 2), wrap(p2 + order[j]), d),
            in1.at[h, d, 0, j], s1.at[h, d, 0, j], r1.at[h, d, 0, j], plane(h, d)))

    def start_near(h, d, j):
        p1, p2 = pos[h], pos[1 - h]
        near[h, d, j] = go(remote(
            part_of(h, wrap(p1 + step[d]), wrap(p2 + order[j]), 1 - d),
            in1.at[h, d, 1, j], s1.at[h, d, 1, j], r1.at[h, d, 1, j], plane(h, d)))

    def start_both(h, d, j):
        p1, p2 = pos[h], pos[1 - h]
        far[h, d, j].wait_recv()
        mine_part = part_of(h, wrap(p1 + step[d]), wrap(p2 + order[j]), d)
        got = in1.at[h, d, 0, j]
        got[...] = (got[...].astype(f32) + mine_part[...].astype(f32)).astype(bf16)
        both[h, d, j] = go(remote(
            got, in1.at[h, d, 2, j], s1.at[h, d, 2, j], r1.at[h, d, 2, j], plane(h, d)))

    far2, near2, both2 = {}, {}, {}

    def finish_first(h, j):
        p1, p2 = pos[h], pos[1 - h]
        for lo in range(2):
            both[h, lo, j].wait_recv()
            near[h, 1 - lo, j].wait_recv()
            total = part_of(h, p1, wrap(p2 + order[j]), lo)[...].astype(f32)
            total += in1[h, lo, 2, j].astype(f32)
            total += in1[h, 1 - lo, 1, j].astype(f32)
            if j == 3:
                own[h, pl.ds(lo * hb, hb)] = total
            else:
                mid[h, j, pl.ds(lo * hb, hb)] = total.astype(bf16)
        halves = [mid.at[h, min(j, 2), pl.ds(lo * hb, hb)] for lo in range(2)]
        if j == 0:
            for d in range(2):
                far2[h, d] = go(remote(
                    halves[d], in2.at[h, d, 0], s2.at[h, d, 0], r2.at[h, d, 0], plane(1 - h, d)))
        elif j < 3:
            d = j - 1
            near2[h, d] = go(remote(
                halves[1 - d], in2.at[h, d, 1], s2.at[h, d, 1], r2.at[h, d, 1], plane(1 - h, d)))

    def start_both2(h, d):
        far2[h, d].wait_recv()
        got = in2.at[h, d, 0]
        got[...] = (got[...].astype(f32) + mid[h, 1 + d, pl.ds(d * hb, hb)].astype(f32)).astype(bf16)
        both2[h, d] = go(remote(
            got, in2.at[h, d, 2], s2.at[h, d, 2], r2.at[h, d, 2], plane(1 - h, d)))

    for j in range(RING):
        for h in range(2):
            for d in range(2):
                start_far(h, d, j)
    for j in range(2):
        for h in range(2):
            for d in range(2):
                start_near(h, d, j)
    for j in range(RING):
        for h in range(2):
            for d in range(2):
                start_both(h, d, j)
                if j + 2 < RING:
                    start_near(h, d, j + 2)
        if j > 0:
            for h in range(2):
                finish_first(h, j - 1)
    for h in range(2):
        for d in range(2):
            start_both2(h, d)
    for h in range(2):
        finish_first(h, 3)

    def spot(c, h, lo):
        return full.at[c, h, pl.ds(lo * hb, hb)]

    hop, hand = {}, {}

    def give(c, h, lo, key):
        hand[key] = go(remote(spot(c, h, lo), spot(c, h, lo), sc.at[key], rc.at[key], sibling))

    for h in range(2):
        for lo in range(2):
            both2[h, lo].wait_recv()
            near2[h, 1 - lo].wait_recv()
            total = own[h, pl.ds(lo * hb, hb)]
            total += in2[h, lo, 2].astype(f32)
            total += in2[h, 1 - lo, 1].astype(f32)
            full[col, h, pl.ds(lo * hb, hb)] = total.astype(bf16)
            key = h * 2 + lo
            for d in range(2):
                hop[d, key] = go(remote(
                    spot(col, h, lo), spot(col, h, lo), sz.at[d, key], rz.at[d, key], along(d)))
            give(col, h, lo, key)
    relay = {}
    for h in range(2):
        for d in range(2):
            for lo in (d, 1 - d):
                key = h * 2 + lo
                hop[d, key].wait_recv()
                c = wrap(z - step[d]) * 2 + core
                if lo == d:
                    relay[d, h] = go(remote(
                        spot(c, h, lo), spot(c, h, lo), sf.at[d, h], rf.at[d, h], along(d)))
                give(c, h, lo, 4 + d * 4 + key)
    for h in range(2):
        for d in range(2):
            relay[d, h].wait_recv()
            c = wrap(z + 2) * 2 + core
            give(c, h, d, 12 + d * 2 + h)
    for key in range(16):
        hand[key].wait_recv()

    devs = full.shape[0]
    grad = jnp.zeros((feats, devs * feats), f32)
    for b in range(0, blk, 2):
        right = jnp.concatenate(
            [
                jnp.concatenate([full[c, h, b + at] for c in range(devs) for h in range(2)], axis=0)
                for at in range(2)
            ],
            axis=1,
        )
        at_b = pl.ds(b * side, 2 * side)
        value = jnp.dot(weight_ref[...], right, preferred_element_type=f32)
        if masked:
            value = value * mask_ref[:, at_b].astype(f32)
        value_ref[:, at_b] = value.astype(bf16)
        grad += lax.dot_general(
            acts_ref[:, at_b], right, (((1,), (1,)), ((), ())), preferred_element_type=f32
        )

    tall = feats // RING
    for piece in range(RING * RING):
        a, b = piece // RING, piece % RING
        mine[piece] = grad[a * tall : (a + 1) * tall, b * side : (b + 1) * side]
    out = []
    for i, dev in enumerate(peers):
        out.append(go(remote(mine.at[dev[0]], gather1.at[i], sg.at[i], rg.at[i], dev)))
    total = mine[row]
    for i in range(len(peers)):
        out[i].wait_recv()
        total += gather1[i]
    gather2[row] = total
    back = [go(remote(gather2.at[row], gather2.at[row], sb.at[i], rb.at[i], dev)) for i, dev in enumerate(peers)]
    for copy in back:
        copy.wait_recv()
    for piece in range(RING * RING):
        a, b = piece // RING, piece % RING
        grad_ref[a * tall : (a + 1) * tall, b * side : (b + 1) * side] = gather2[piece]
    for copy in started:
        copy.wait_send()


def layer(part, weight, acts_t, mask_t, collective_id):
    _, plane, blk, half, side = part.shape
    feats, rows = acts_t.shape
    devs = weight.shape[1] // feats
    hb = blk // 2
    masked = mask_t is not None
    vmem = pl.BlockSpec(memory_space=pltpu.VMEM)
    args = [part, weight, acts_t] + ([mask_t] if masked else [])
    dma = pltpu.SemaphoreType.DMA
    bf16, f32 = jnp.bfloat16, jnp.float32
    tall = feats // RING
    scratch = [
        pltpu.VMEM((2, 2, 3, RING, hb, half, side), bf16),
        pltpu.VMEM((2, 3, blk, half, side), bf16),
        pltpu.VMEM((2, blk, half, side), f32),
        pltpu.VMEM((2, 2, 3, hb, half, side), bf16),
        pltpu.VMEM((devs, 2, blk, half, side), bf16),
        pltpu.VMEM((plane, tall, side), f32),
        pltpu.VMEM((plane - 1, tall, side), f32),
        pltpu.VMEM((plane, tall, side), f32),
    ]
    for shape in ((2, 2, 3, RING), (2, 2, 3), (2, 4), (2, 2), (16,), (plane - 1,), (plane - 1,)):
        scratch += [dma(shape), dma(shape)]
    return pl.pallas_call(
        functools.partial(layer_kernel, masked),
        out_shape=(
            jax.ShapeDtypeStruct((feats, rows), bf16),
            jax.ShapeDtypeStruct((feats, devs * feats), f32),
        ),
        in_specs=[vmem] * len(args),
        out_specs=(vmem, vmem),
        scratch_shapes=scratch,
        compiler_params=pltpu.CompilerParams(
            collective_id=collective_id, has_side_effects=True, vmem_limit_bytes=32 << 20
        ),
    )(*args)


def per_device(
    node_feats, hidden_act, grad_out, relu_mask, edge_tiles, block_cols, weight_one, weight_two
):
    part = spread(block_cols, grad_out.T, edge_tiles)
    delta_t, second_grad = layer(part, weight_two, hidden_act.T, relu_mask.T, 0)
    part = spread(block_cols, delta_t, edge_tiles)
    input_grad_t, first_grad = layer(part, weight_one, node_feats.T, None, 1)
    return (input_grad_t.T, first_grad, second_grad)


def solution(mesh):
    in_specs = (
        P("row", "col"),
        P("row", "col"),
        P("row", "col"),
        P("row", "col"),
        P("row", None, None, None),
        P("row", None),
        P("col", None),
        P("col", None),
    )
    out_specs = (P("row", "col"), P("col", None), P("col", None))
    return jax.shard_map(
        per_device, mesh=mesh, in_specs=in_specs, out_specs=out_specs, check_vma=False
    )
```

```python
import functools
import jax
import jax.numpy as jnp
from jax import lax
from jax.experimental import pallas as pl
from jax.experimental.pallas import tpu as pltpu
from jax.sharding import PartitionSpec as P

RING = 4
ROWS = RING * RING
GROUPS = 4
MESH = pl.DeviceIdType.MESH
ORDER = (
    "f0 f1 o0 b0 o1 f2 b1 o2 f3 c0 b2 o3 d0 c1 e0 b3 d1 h0 c2 r0 e1 p0 d2 h1 c3 r1 d3 e2 p1 e3 h2 h3 r2 p2 r3 p3"
)


def add_terms(acc_ref, cols_ref, vals, tiles, first):
    feats = vals.shape[0]
    side = tiles.shape[2]
    blank = jnp.zeros((feats, side), vals.dtype)
    left = jnp.concatenate(
        [
            jnp.concatenate([vals[:, :side], blank], axis=1),
            jnp.concatenate([blank, vals[:, side:]], axis=1),
        ],
        axis=0,
    )
    for k in range(0, tiles.shape[1], 2):
        right = jnp.concatenate(
            [
                jnp.concatenate([tiles[0, k], tiles[0, k + 1]], axis=1),
                jnp.concatenate([tiles[1, k], tiles[1, k + 1]], axis=1),
            ],
            axis=0,
        )
        term = jnp.dot(left, right, preferred_element_type=jnp.float32)
        for row in range(2):
            for at in range(2):
                acc_ref[cols_ref[first + row, k + at]] += term[
                    row * feats : (row + 1) * feats, at * side : (at + 1) * side
                ]


def hand_out(acc_ref, out_ref):
    per_dev = out_ref.shape[3]
    half = out_ref.shape[4]
    for x in range(RING):
        for y in range(RING):
            got = acc_ref[pl.ds((x * RING + y) * per_dev, per_dev)].astype(out_ref.dtype)
            out_ref[0, x, y] = got[:, :half]
            out_ref[1, y, x] = got[:, half:]


def spread_kernel(cols_ref, vals_ref, tiles_ref, out_ref, acc_ref):
    step = pl.program_id(0)

    @pl.when(step == 0)
    def _():
        acc_ref[...] = jnp.zeros_like(acc_ref)

    add_terms(acc_ref, cols_ref, vals_ref[...], tiles_ref, 2 * step)

    @pl.when(step == pl.num_programs(0) - 1)
    def _():
        hand_out(acc_ref, out_ref)


def stream_kernel(cols_hbm, vals_hbm, tiles_hbm, out_ref, tiles_ref, acc_ref, cols_ref, vals_ref, sems):
    pairs = tiles_ref.shape[0] // 2
    side = tiles_ref.shape[2]
    small = [
        pltpu.make_async_copy(cols_hbm, cols_ref, sems.at[pairs]),
        pltpu.make_async_copy(vals_hbm, vals_ref, sems.at[pairs + 1]),
    ]
    for copy in small:
        copy.start()

    def tiles_copy(i):
        at = pl.ds(2 * i, 2)
        return pltpu.make_async_copy(tiles_hbm.at[at], tiles_ref.at[at], sems.at[i])

    for i in range(pairs):
        tiles_copy(i).start()
    acc_ref[...] = jnp.zeros_like(acc_ref)
    for copy in small:
        copy.wait()

    def body(i, carry):
        tiles_copy(i).wait()
        vals = vals_ref[:, pl.ds(pl.multiple_of(2 * side * i, 2 * side), 2 * side)]
        add_terms(acc_ref, cols_ref, vals, tiles_ref.at[pl.ds(2 * i, 2)], 2 * i)
        return carry

    lax.fori_loop(0, pairs, body, 0)
    hand_out(acc_ref, out_ref)


def spread(block_cols, vals_t, edge_tiles, stream):
    rows, per_row, side, _ = edge_tiles.shape
    feats = vals_t.shape[0]
    out = (2, RING, RING, rows, feats // 2, side)
    acc = pltpu.VMEM((rows * ROWS, feats, side), jnp.float32)
    out_shape = jax.ShapeDtypeStruct(out, jnp.bfloat16)
    if stream:
        hbm = pl.BlockSpec(memory_space=pltpu.HBM)
        return pl.pallas_call(
            stream_kernel,
            out_shape=(out_shape, jax.ShapeDtypeStruct(edge_tiles.shape, edge_tiles.dtype)),
            in_specs=[hbm] * 3,
            out_specs=[pl.BlockSpec(memory_space=pltpu.VMEM)] * 2,
            scratch_shapes=[
                acc,
                pltpu.SMEM(block_cols.shape, jnp.int32),
                pltpu.VMEM(vals_t.shape, vals_t.dtype),
                pltpu.SemaphoreType.DMA((rows // 2 + 2,)),
            ],
            compiler_params=pltpu.CompilerParams(vmem_limit_bytes=30 << 20),
        )(*(pltpu.with_memory_space_constraint(v, pltpu.HBM) for v in (block_cols, vals_t, edge_tiles)))
    return pl.pallas_call(
        spread_kernel,
        out_shape=out_shape,
        grid_spec=pltpu.PrefetchScalarGridSpec(
            num_scalar_prefetch=1,
            grid=(rows // 2,),
            in_specs=[
                pl.BlockSpec((feats, 2 * side), lambda i, c: (0, i)),
                pl.BlockSpec((2, per_row, side, side), lambda i, c: (i, 0, 0, 0)),
            ],
            out_specs=pl.BlockSpec(out, lambda i, c: (0,) * 6),
            scratch_shapes=[acc],
        ),
        compiler_params=pltpu.CompilerParams(vmem_limit_bytes=28 << 20),
    )(block_cols, vals_t, edge_tiles)


def to_pieces(grad, pieces_ref):
    _, tall, wide = pieces_ref.shape
    for p in range(ROWS):
        a, b = p // RING, p % RING
        pieces_ref[p] = grad[a * tall : (a + 1) * tall, b * wide : (b + 1) * wide].astype(pieces_ref.dtype)


def from_pieces(pieces_ref, grad_ref):
    _, tall, wide = pieces_ref.shape
    for p in range(ROWS):
        a, b = p // RING, p % RING
        grad_ref[a * tall : (a + 1) * tall, b * wide : (b + 1) * wide] = pieces_ref[p].astype(grad_ref.dtype)


def layer_kernel(first, *refs):
    if first:
        part_ref, weight_ref, acts_ref, mask_ref, value_ref, pieces_ref = refs[:6]
        in1, mid, in2, full, total_ref, s1, r1, s2, r2, sz, rz, sf, rf, sc, rc = refs[6:]
    else:
        part_ref, weight_ref, acts_ref, early_ref, value_ref, grad_ref, early_grad_ref = refs[:7]
        in1, mid, in2, full, total_ref, s1, r1, s2, r2, sz, rz, sf, rf, sc, rc = refs[7:22]
        pieces_ref, gather1, gather2, sg, rg, sb, rb = refs[22:]
    blk, half, side = part_ref.shape[3:]
    gb = blk // GROUPS
    hb = gb // 2
    feats = 2 * half
    devs = full.shape[0]
    f32, bf16 = jnp.float32, jnp.bfloat16

    row, col = lax.axis_index("row"), lax.axis_index("col")
    pos = (row // RING, lax.rem(row, RING))
    z, core = col // 2, lax.rem(col, 2)
    step = (1, -1)
    both_d = (0, 1)
    lanes = [(h, d) for h in range(2) for d in range(2)]

    def wrap(v):
        return lax.rem(v + RING, RING)

    def plane(axis, d):
        x, y = pos
        if axis == 0:
            return (wrap(x + step[d]) * RING + y, col)
        return (x * RING + wrap(y + step[d]), col)

    def along(d):
        return (row, wrap(z + step[d]) * 2 + core)

    sibling = (row, z * 2 + 1 - core)
    near_devs = [plane(a, d) for a, d in lanes]
    peers = [(lax.rem(row + off, ROWS), col) for off in range(1, ROWS)]

    barrier = pltpu.get_barrier_semaphore()
    met = (near_devs if first else peers) + [along(0), along(1), sibling]
    for dev in met:
        pl.semaphore_signal(barrier, inc=1, device_id=dev, device_id_type=MESH)
    pl.semaphore_wait(barrier, len(met))

    started = []

    def send(src, dst, send_sem, recv_sem, dev):
        copy = pltpu.make_async_remote_copy(
            src_ref=src, dst_ref=dst, send_sem=send_sem, recv_sem=recv_sem,
            device_id=dev, device_id_type=MESH,
        )
        copy.start()
        started.append(copy)
        return copy

    def blocks(g, lo):
        return pl.ds(g * gb + lo * hb, hb)

    far, near, both, far2, near2, both2, hop, relay, hand = ({} for _ in range(9))

    def send_far(g):
        for h, d in lanes:
            far[h, d, g] = send(
                part_ref.at[h, wrap(pos[h] + 2), :, blocks(g, d)],
                in1.at[h, d, 0, g], s1.at[h, d, 0, g], r1.at[h, d, 0, g], plane(h, d))

    def send_near(g):
        for h, d in lanes:
            near[h, d, g] = send(
                part_ref.at[h, wrap(pos[h] + step[d]), :, blocks(g, 1 - d)],
                in1.at[h, d, 1, g], s1.at[h, d, 1, g], r1.at[h, d, 1, g], plane(h, d))

    def send_both(g):
        for h, d in lanes:
            far[h, d, g].wait_recv()
            got = in1.at[h, d, 0, g]
            mine = part_ref[h, wrap(pos[h] + step[d]), :, blocks(g, d)]
            got[...] = (got[...].astype(f32) + mine.astype(f32)).astype(bf16)
            both[h, d, g] = send(
                got, in1.at[h, d, 2, g], s1.at[h, d, 2, g], r1.at[h, d, 2, g], plane(h, d))

    def second_ring(g):
        for h in range(2):
            other = pos[1 - h]
            for lo in range(2):
                both[h, lo, g].wait_recv()
                near[h, 1 - lo, g].wait_recv()
                total = part_ref[h, pos[h], :, blocks(g, lo)].astype(f32)
                total += in1[h, lo, 2, g].astype(f32)
                total += in1[h, 1 - lo, 1, g].astype(f32)
                mid[h, g, :, pl.ds(lo * hb, hb)] = total.astype(bf16)
            for d in both_d:
                far2[h, d, g] = send(
                    mid.at[h, g, wrap(other + 2), pl.ds(d * hb, hb)],
                    in2.at[h, d, 0, g], s2.at[h, d, 0, g], r2.at[h, d, 0, g], plane(1 - h, d))
            for d in both_d:
                near2[h, d, g] = send(
                    mid.at[h, g, wrap(other + step[d]), pl.ds((1 - d) * hb, hb)],
                    in2.at[h, d, 1, g], s2.at[h, d, 1, g], r2.at[h, d, 1, g], plane(1 - h, d))

    def send_both2(g):
        for h, d in lanes:
            far2[h, d, g].wait_recv()
            got = in2.at[h, d, 0, g]
            mine = mid[h, g, wrap(pos[1 - h] + step[d]), pl.ds(d * hb, hb)]
            got[...] = (got[...].astype(f32) + mine.astype(f32)).astype(bf16)
            both2[h, d, g] = send(
                got, in2.at[h, d, 2, g], s2.at[h, d, 2, g], r2.at[h, d, 2, g], plane(1 - h, d))

    def give(c, g, key, h=None):
        spot = full.at[c, g] if h is None else full.at[c, g, h]
        hand[key, g] = send(spot, spot, sc.at[key, g], rc.at[key, g], sibling)

    def finish(g):
        for h in range(2):
            for lo in range(2):
                both2[h, lo, g].wait_recv()
                near2[h, 1 - lo, g].wait_recv()
                other = pos[1 - h]
                total = part_ref[h, pos[h], other, blocks(g, lo)].astype(f32)
                total += in1[h, lo, 2, g, other].astype(f32)
                total += in1[h, 1 - lo, 1, g, other].astype(f32)
                total += in2[h, lo, 2, g].astype(f32)
                total += in2[h, 1 - lo, 1, g].astype(f32)
                full[col, g, h, pl.ds(lo * hb, hb)] = total.astype(bf16)
        for d in both_d:
            spot = full.at[col, g]
            hop[d, g] = send(spot, spot, sz.at[d, g], rz.at[d, g], along(d))
        give(col, g, 0)

    def pass_on(g):
        for d in both_d:
            hop[d, g].wait_recv()
            c = wrap(z - step[d]) * 2 + core
            spot = full.at[c, g, d]
            relay[d, g] = send(spot, spot, sf.at[d, g], rf.at[d, g], along(d))
            give(c, g, 1 + d)

    def last_hand(g):
        for d in both_d:
            relay[d, g].wait_recv()
            give(wrap(z + 2) * 2 + core, g, 3 + d, d)

    def products(g):
        for key in range(5):
            hand[key, g].wait_recv()
        right = jnp.concatenate(
            [
                jnp.concatenate([full[c, g, h, b] for c in range(devs) for h in range(2)], axis=0)
                for b in range(gb)
            ],
            axis=1,
        )
        at = pl.ds(g * gb * side, gb * side)
        value = jnp.dot(weight_ref[...], right, preferred_element_type=f32)
        if first:
            value = value * mask_ref[:, at].astype(f32)
        value_ref[:, at] = value.astype(bf16)
        grad = lax.dot_general(
            acts_ref[:, at], right, (((1,), (1,)), ((), ())), preferred_element_type=f32
        )
        if g > 0:
            grad += total_ref[...]
        if g < GROUPS - 1:
            total_ref[...] = grad
        else:
            to_pieces(grad, pieces_ref)

    out, back = {}, {}

    def send_pieces(n, src):
        for i, dev in enumerate(peers):
            out[n, i] = send(src.at[dev[0]], gather1.at[n, i], sg.at[n, i], rg.at[n, i], dev)

    def add_pieces(n, src):
        total = src[row].astype(f32)
        for i, dev in enumerate(peers):
            out[n, i].wait_recv()
            total += gather1[n, i].astype(f32)
        gather2[n, row] = total.astype(bf16)
        for i, dev in enumerate(peers):
            spot = gather2.at[n, row]
            back[n, i] = send(spot, spot, sb.at[n, i], rb.at[n, i], dev)

    def take_pieces(n, dst):
        for i in range(len(peers)):
            back[n, i].wait_recv()
        from_pieces(gather2.at[n], dst)

    stages = dict(
        f=send_far, o=send_near, b=send_both, c=second_ring, d=send_both2,
        e=finish, h=pass_on, r=last_hand, p=products,
    )
    for word in ORDER.split():
        stages[word[0]](int(word[1:]))
        if not first:
            if word == "b1":
                send_pieces(0, early_ref)
            if word == "c1":
                add_pieces(0, early_ref)
            if word == "e3":
                take_pieces(0, early_grad_ref)
    if not first:
        send_pieces(1, pieces_ref)
        add_pieces(1, pieces_ref)
        take_pieces(1, grad_ref)
    for copy in started:
        copy.wait_send()


def layer(part, weight, acts_t, extra, collective_id):
    first = collective_id == 0
    blk, half, side = part.shape[3:]
    feats, rows = acts_t.shape
    devs = weight.shape[1] // feats
    gb = blk // GROUPS
    hb = gb // 2
    vmem = pl.BlockSpec(memory_space=pltpu.VMEM)
    dma = pltpu.SemaphoreType.DMA
    bf16, f32 = jnp.bfloat16, jnp.float32
    grad = (feats, devs * feats)
    pieces = (ROWS, feats // RING, devs * feats // RING)
    scratch = [
        pltpu.VMEM((2, 2, 3, GROUPS, RING, hb, half, side), bf16),
        pltpu.VMEM((2, GROUPS, RING, gb, half, side), bf16),
        pltpu.VMEM((2, 2, 3, GROUPS, hb, half, side), bf16),
        pltpu.VMEM((devs, GROUPS, 2, gb, half, side), bf16),
        pltpu.VMEM(grad, f32),
    ]
    for shape in ((2, 2, 3), (2, 2, 3), (2,), (2,), (5,)):
        scratch += [dma(shape + (GROUPS,)), dma(shape + (GROUPS,))]
    out_shape = [jax.ShapeDtypeStruct((feats, rows), bf16)]
    if first:
        out_shape += [jax.ShapeDtypeStruct(pieces, bf16)]
    else:
        out_shape += [jax.ShapeDtypeStruct(grad, f32)] * 2
        scratch += [
            pltpu.VMEM(pieces, bf16),
            pltpu.VMEM((2, ROWS - 1) + pieces[1:], bf16),
            pltpu.VMEM((2,) + pieces, bf16),
        ]
        scratch += [dma((2, ROWS - 1))] * 4
    return pl.pallas_call(
        functools.partial(layer_kernel, first),
        out_shape=out_shape,
        in_specs=[vmem] * 4,
        out_specs=[vmem] * len(out_shape),
        scratch_shapes=scratch,
        compiler_params=pltpu.CompilerParams(
            collective_id=collective_id, has_side_effects=True, vmem_limit_bytes=32 << 20
        ),
    )(part, weight, acts_t, extra)


def per_device(
    node_feats, hidden_act, grad_out, relu_mask, edge_tiles, block_cols, weight_one, weight_two
):
    part, tiles = spread(block_cols, grad_out.T, edge_tiles, True)
    delta_t, pieces = layer(part, weight_two, hidden_act.T, relu_mask.T, 0)
    part = spread(block_cols, delta_t, tiles, False)
    input_grad_t, first_grad, second_grad = layer(part, weight_one, node_feats.T, pieces, 1)
    return (input_grad_t.T, first_grad, second_grad)


def solution(mesh):
    in_specs = (
        P("row", "col"),
        P("row", "col"),
        P("row", "col"),
        P("row", "col"),
        P("row", None, None, None),
        P("row", None),
        P("col", None),
        P("col", None),
    )
    out_specs = (P("row", "col"), P("col", None), P("col", None))
    return jax.shard_map(
        per_device, mesh=mesh, in_specs=in_specs, out_specs=out_specs, check_vma=False
    )
```

```python
import functools
import jax
import jax.numpy as jnp
from jax import lax
from jax.experimental import pallas as pl
from jax.experimental.pallas import tpu as pltpu
from jax.sharding import PartitionSpec as P

RING = 4
ROWS = RING * RING
GROUPS = (4, 4, 4, 4)
ORDER = "f0 o0 f1 o1 b0 f2 b1 o2 c0 f3 b2 o3 c1 e0 b3 h0 c2 e1 p0 c3 h1 e2 p1 e3 h2 p2 h3 p3"
MESH = pl.DeviceIdType.MESH


def add_terms(acc_ref, cols_ref, vals, tiles, first):
    feats = vals.shape[0]
    side = tiles.shape[2]
    blank = jnp.zeros((feats, side), vals.dtype)
    left = jnp.concatenate(
        [
            jnp.concatenate([vals[:, :side], blank], axis=1),
            jnp.concatenate([blank, vals[:, side:]], axis=1),
        ],
        axis=0,
    )
    for k in range(0, tiles.shape[1], 2):
        right = jnp.concatenate(
            [
                jnp.concatenate([tiles[0, k], tiles[0, k + 1]], axis=1),
                jnp.concatenate([tiles[1, k], tiles[1, k + 1]], axis=1),
            ],
            axis=0,
        )
        term = jnp.dot(left, right, preferred_element_type=jnp.float32)
        for row in range(2):
            for at in range(2):
                acc_ref[cols_ref[first + row, k + at]] += term[
                    row * feats : (row + 1) * feats, at * side : (at + 1) * side
                ]


def hand_out(acc_ref, out_ref):
    per_dev = out_ref.shape[3]
    half = out_ref.shape[4]
    for x in range(RING):
        for y in range(RING):
            got = acc_ref[pl.ds((x * RING + y) * per_dev, per_dev)].astype(out_ref.dtype)
            out_ref[0, x, y] = got[:, :half]
            out_ref[1, y, x] = got[:, half:]


def spread_kernel(cols_ref, vals_ref, tiles_ref, out_ref, acc_ref):
    step = pl.program_id(0)

    @pl.when(step == 0)
    def _():
        acc_ref[...] = jnp.zeros_like(acc_ref)

    add_terms(acc_ref, cols_ref, vals_ref[...], tiles_ref, 2 * step)

    @pl.when(step == pl.num_programs(0) - 1)
    def _():
        hand_out(acc_ref, out_ref)


def stream_kernel(cols_hbm, vals_hbm, tiles_hbm, out_ref, tiles_ref, acc_ref, cols_ref, vals_ref, sems):
    pairs = tiles_ref.shape[0] // 2
    side = tiles_ref.shape[2]
    small = [
        pltpu.make_async_copy(cols_hbm, cols_ref, sems.at[pairs]),
        pltpu.make_async_copy(vals_hbm, vals_ref, sems.at[pairs + 1]),
    ]
    for copy in small:
        copy.start()

    def tiles_copy(i):
        at = pl.ds(2 * i, 2)
        return pltpu.make_async_copy(tiles_hbm.at[at], tiles_ref.at[at], sems.at[i])

    for i in range(pairs):
        tiles_copy(i).start()
    acc_ref[...] = jnp.zeros_like(acc_ref)
    for copy in small:
        copy.wait()

    def body(i, carry):
        tiles_copy(i).wait()
        vals = vals_ref[:, pl.ds(pl.multiple_of(2 * side * i, 2 * side), 2 * side)]
        add_terms(acc_ref, cols_ref, vals, tiles_ref.at[pl.ds(2 * i, 2)], 2 * i)
        return carry

    lax.fori_loop(0, pairs, body, 0)
    hand_out(acc_ref, out_ref)


def spread(block_cols, vals_t, edge_tiles, stream):
    rows, per_row, side, _ = edge_tiles.shape
    feats = vals_t.shape[0]
    out = (2, RING, RING, rows, feats // 2, side)
    acc = pltpu.VMEM((rows * ROWS, feats, side), jnp.float32)
    out_shape = jax.ShapeDtypeStruct(out, jnp.bfloat16)
    if stream:
        hbm = pl.BlockSpec(memory_space=pltpu.HBM)
        return pl.pallas_call(
            stream_kernel,
            out_shape=(out_shape, jax.ShapeDtypeStruct(edge_tiles.shape, edge_tiles.dtype)),
            in_specs=[hbm] * 3,
            out_specs=[pl.BlockSpec(memory_space=pltpu.VMEM)] * 2,
            scratch_shapes=[
                acc,
                pltpu.SMEM(block_cols.shape, jnp.int32),
                pltpu.VMEM(vals_t.shape, vals_t.dtype),
                pltpu.SemaphoreType.DMA((rows // 2 + 2,)),
            ],
            compiler_params=pltpu.CompilerParams(vmem_limit_bytes=30 << 20),
        )(*(pltpu.with_memory_space_constraint(v, pltpu.HBM) for v in (block_cols, vals_t, edge_tiles)))
    return pl.pallas_call(
        spread_kernel,
        out_shape=out_shape,
        grid_spec=pltpu.PrefetchScalarGridSpec(
            num_scalar_prefetch=1,
            grid=(rows // 2,),
            in_specs=[
                pl.BlockSpec((feats, 2 * side), lambda i, c: (0, i)),
                pl.BlockSpec((2, per_row, side, side), lambda i, c: (i, 0, 0, 0)),
            ],
            out_specs=pl.BlockSpec(out, lambda i, c: (0,) * 6),
            scratch_shapes=[acc],
        ),
        compiler_params=pltpu.CompilerParams(vmem_limit_bytes=28 << 20),
    )(block_cols, vals_t, edge_tiles)


def to_pieces(grad, pieces_ref):
    _, tall, wide = pieces_ref.shape
    for p in range(ROWS):
        a, b = p // RING, p % RING
        pieces_ref[p] = grad[a * tall : (a + 1) * tall, b * wide : (b + 1) * wide].astype(pieces_ref.dtype)


def from_pieces(pieces_ref, grad_ref):
    _, tall, wide = pieces_ref.shape
    for p in range(ROWS):
        a, b = p // RING, p % RING
        grad_ref[a * tall : (a + 1) * tall, b * wide : (b + 1) * wide] = pieces_ref[p].astype(grad_ref.dtype)


def layer_kernel(first, *refs):
    if first:
        part_ref, weight_ref, acts_ref, mask_ref, value_ref, pieces_ref = refs[:6]
        in1, mid, in2, full, total_ref, s1, r1, s2, r2, sz, rz, sc, rc = refs[6:]
    else:
        part_ref, weight_ref, acts_ref, early_ref, value_ref, grad_ref, early_grad_ref = refs[:7]
        in1, mid, in2, full, total_ref, s1, r1, s2, r2, sz, rz, sc, rc = refs[7:20]
        pieces_ref, gather1, gather2, sg, rg, sb, rb = refs[20:]
    blk, half, side = part_ref.shape[3:]
    feats = 2 * half
    devs = full.shape[0]
    f32, bf16 = jnp.float32, jnp.bfloat16
    starts = [sum(GROUPS[:g]) for g in range(len(GROUPS))]

    row, col = lax.axis_index("row"), lax.axis_index("col")
    pos = (row // RING, lax.rem(row, RING))
    z, core = col // 2, lax.rem(col, 2)
    step = (1, -1, 2)
    lanes = [(h, d) for h in range(2) for d in range(2)]

    def wrap(v):
        return lax.rem(v + RING, RING)

    def plane(axis, d):
        x, y = pos
        if axis == 0:
            return (wrap(x + step[d]) * RING + y, col)
        return (x * RING + wrap(y + step[d]), col)

    def along(d):
        return (row, wrap(z + step[d]) * 2 + core)

    sibling = (row, z * 2 + 1 - core)
    peers = [(lax.rem(row + off, ROWS), col) for off in range(1, ROWS)]

    barrier = pltpu.get_barrier_semaphore()
    met = [plane(a, d) for a in range(2) for d in range(3)] if first else peers
    met = met + [along(0), along(1), along(2), sibling]
    for dev in met:
        pl.semaphore_signal(barrier, inc=1, device_id=dev, device_id_type=MESH)
    pl.semaphore_wait(barrier, len(met))

    started = []

    def send(src, dst, send_sem, recv_sem, dev):
        copy = pltpu.make_async_remote_copy(
            src_ref=src, dst_ref=dst, send_sem=send_sem, recv_sem=recv_sem,
            device_id=dev, device_id_type=MESH,
        )
        copy.start()
        started.append(copy)
        return copy

    def blocks(g, lo=None):
        if lo is None:
            return pl.ds(starts[g], GROUPS[g])
        return pl.ds(starts[g] + lo * (GROUPS[g] // 2), GROUPS[g] // 2)

    def slots(g):
        return pl.ds(starts[g] // 2, GROUPS[g] // 2)

    far, near, both, direct, hop, hand = ({} for _ in range(6))

    def send_far(g):
        for h, d in lanes:
            far[h, d, g] = send(
                part_ref.at[h, wrap(pos[h] + 2), :, blocks(g, d)],
                in1.at[h, d, 0, :, slots(g)], s1.at[h, d, 0, g], r1.at[h, d, 0, g], plane(h, d))

    def send_near(g):
        for h, d in lanes:
            near[h, d, g] = send(
                part_ref.at[h, wrap(pos[h] + step[d]), :, blocks(g, 1 - d)],
                in1.at[h, d, 1, :, slots(g)], s1.at[h, d, 1, g], r1.at[h, d, 1, g], plane(h, d))

    def send_both(g):
        for h, d in lanes:
            far[h, d, g].wait_recv()
            got = in1.at[h, d, 0, :, slots(g)]
            mine = part_ref[h, wrap(pos[h] + step[d]), :, blocks(g, d)]
            got[...] = (got[...].astype(f32) + mine.astype(f32)).astype(bf16)
            both[h, d, g] = send(
                got, in1.at[h, d, 2, :, slots(g)], s1.at[h, d, 2, g], r1.at[h, d, 2, g], plane(h, d))

    def second_ring(g):
        for h in range(2):
            other = pos[1 - h]
            for lo in range(2):
                both[h, lo, g].wait_recv()
                near[h, 1 - lo, g].wait_recv()
                total = part_ref[h, pos[h], :, blocks(g, lo)].astype(f32)
                total += in1[h, lo, 2, :, slots(g)].astype(f32)
                total += in1[h, 1 - lo, 1, :, slots(g)].astype(f32)
                mid[h, :, blocks(g, lo)] = total.astype(bf16)
            for d in (2, 0, 1):
                direct[h, d, g] = send(
                    mid.at[h, wrap(other + step[d]), blocks(g)],
                    in2.at[h, d, blocks(g)], s2.at[h, d, g], r2.at[h, d, g], plane(1 - h, d))

    def give(c, g, key):
        spot = full.at[c, :, blocks(g)]
        hand[key, g] = send(spot, spot, sc.at[key, g], rc.at[key, g], sibling)

    def finish(g):
        for h in range(2):
            other = pos[1 - h]
            total = mid[h, other, blocks(g)].astype(f32)
            for d in range(3):
                direct[h, d, g].wait_recv()
                total += in2[h, d, blocks(g)].astype(f32)
            full[col, h, blocks(g)] = total.astype(bf16)
        for d in (2, 0, 1):
            spot = full.at[col, :, blocks(g)]
            hop[d, g] = send(spot, spot, sz.at[d, g], rz.at[d, g], along(d))
        give(col, g, 3)

    def pass_on(g):
        for d in (0, 1, 2):
            hop[d, g].wait_recv()
            give(wrap(z - step[d]) * 2 + core, g, d)

    def products(g):
        for key in range(4):
            hand[key, g].wait_recv()
        right = jnp.concatenate(
            [
                jnp.concatenate([full[c, h, starts[g] + b] for c in range(devs) for h in range(2)], axis=0)
                for b in range(GROUPS[g])
            ],
            axis=1,
        )
        at = pl.ds(starts[g] * side, GROUPS[g] * side)
        value = jnp.dot(weight_ref[...], right, preferred_element_type=f32)
        if first:
            value = value * mask_ref[:, at].astype(f32)
        value_ref[:, at] = value.astype(bf16)
        grad = lax.dot_general(
            acts_ref[:, at], right, (((1,), (1,)), ((), ())), preferred_element_type=f32
        )
        if g > 0:
            grad += total_ref[...]
        if g < len(GROUPS) - 1:
            total_ref[...] = grad
        else:
            to_pieces(grad, pieces_ref)

    out, back = {}, {}

    def send_pieces(n, src):
        for i, dev in enumerate(peers):
            out[n, i] = send(src.at[dev[0]], gather1.at[n, i], sg.at[n, i], rg.at[n, i], dev)

    def add_pieces(n, src):
        total = src[row].astype(f32)
        for i, dev in enumerate(peers):
            out[n, i].wait_recv()
            total += gather1[n, i].astype(f32)
        gather2[n, row] = total.astype(bf16)
        for i, dev in enumerate(peers):
            spot = gather2.at[n, row]
            back[n, i] = send(spot, spot, sb.at[n, i], rb.at[n, i], dev)

    def take_pieces(n, dst):
        for i in range(len(peers)):
            back[n, i].wait_recv()
        from_pieces(gather2.at[n], dst)

    stages = dict(
        f=send_far, o=send_near, b=send_both, c=second_ring, e=finish, h=pass_on, p=products,
    )
    for word in ORDER.split():
        stages[word[0]](int(word[1:]))
        if not first:
            if word == "o1":
                send_pieces(0, early_ref)
            if word == "c1":
                add_pieces(0, early_ref)
            if word == "p1":
                take_pieces(0, early_grad_ref)
    if not first:
        send_pieces(1, pieces_ref)
        add_pieces(1, pieces_ref)
        take_pieces(1, grad_ref)
    for copy in started:
        copy.wait_send()


def layer(part, weight, acts_t, extra, collective_id):
    first = collective_id == 0
    blk, half, side = part.shape[3:]
    feats, rows = acts_t.shape
    devs = weight.shape[1] // feats
    groups = len(GROUPS)
    vmem = pl.BlockSpec(memory_space=pltpu.VMEM)
    dma = pltpu.SemaphoreType.DMA
    bf16, f32 = jnp.bfloat16, jnp.float32
    grad = (feats, devs * feats)
    pieces = (ROWS, feats // RING, devs * feats // RING)
    scratch = [
        pltpu.VMEM((2, 2, 3, RING, blk // 2, half, side), bf16),
        pltpu.VMEM((2, RING, blk, half, side), bf16),
        pltpu.VMEM((2, 3, blk, half, side), bf16),
        pltpu.VMEM((devs, 2, blk, half, side), bf16),
        pltpu.VMEM(grad, f32),
    ]
    for shape in ((2, 2, 3), (2, 3), (3,), (4,)):
        scratch += [dma(shape + (groups,)), dma(shape + (groups,))]
    out_shape = [jax.ShapeDtypeStruct((feats, rows), bf16)]
    if first:
        out_shape += [jax.ShapeDtypeStruct(pieces, bf16)]
    else:
        out_shape += [jax.ShapeDtypeStruct(grad, f32)] * 2
        scratch += [
            pltpu.VMEM(pieces, bf16),
            pltpu.VMEM((2, ROWS - 1) + pieces[1:], bf16),
            pltpu.VMEM((2,) + pieces, bf16),
        ]
        scratch += [dma((2, ROWS - 1))] * 4
    return pl.pallas_call(
        functools.partial(layer_kernel, first),
        out_shape=out_shape,
        in_specs=[vmem] * 4,
        out_specs=[vmem] * len(out_shape),
        scratch_shapes=scratch,
        compiler_params=pltpu.CompilerParams(
            collective_id=collective_id, has_side_effects=True, vmem_limit_bytes=32 << 20
        ),
    )(part, weight, acts_t, extra)


def per_device(
    node_feats, hidden_act, grad_out, relu_mask, edge_tiles, block_cols, weight_one, weight_two
):
    part, tiles = spread(block_cols, grad_out.T, edge_tiles, True)
    delta_t, pieces = layer(part, weight_two, hidden_act.T, relu_mask.T, 0)
    part = spread(block_cols, delta_t, tiles, False)
    input_grad_t, first_grad, second_grad = layer(part, weight_one, node_feats.T, pieces, 1)
    return (input_grad_t.T, first_grad, second_grad)


def solution(mesh):
    in_specs = (
        P("row", "col"),
        P("row", "col"),
        P("row", "col"),
        P("row", "col"),
        P("row", None, None, None),
        P("row", None),
        P("col", None),
        P("col", None),
    )
    out_specs = (P("row", "col"), P("col", None), P("col", None))
    return jax.shard_map(
        per_device, mesh=mesh, in_specs=in_specs, out_specs=out_specs, check_vma=False
    )
```

```python
import functools
import jax
import jax.numpy as jnp
from jax import lax
from jax.experimental import pallas as pl
from jax.experimental.pallas import tpu as pltpu
from jax.sharding import PartitionSpec as P

RING = 4
ROWS = RING * RING
GROUPS = (4, 4, 4, 2, 2)
ORDER = (
    "f2", "f1", "o1", "o0", "b2", "b1", "f0", "f3", "o2", "c1", "b0", "f4",
    "c2", "o3", "b3", "e1", "c0", "o4", "e2", "b4", "c3", "e0", "c4", "h1",
    "e3", "h2", "e4", "h0", "h3", "p0", "p1", "h4", "p2", "p3", "p4",
)
MESH = pl.DeviceIdType.MESH


def add_terms(acc_ref, cols_ref, vals, tiles, first):
    feats = vals.shape[0]
    side = tiles.shape[2]
    blank = jnp.zeros((feats, side), vals.dtype)
    left = jnp.concatenate(
        [
            jnp.concatenate([vals[:, :side], blank], axis=1),
            jnp.concatenate([blank, vals[:, side:]], axis=1),
        ],
        axis=0,
    )
    for k in range(0, tiles.shape[1], 2):
        right = jnp.concatenate(
            [
                jnp.concatenate([tiles[0, k], tiles[0, k + 1]], axis=1),
                jnp.concatenate([tiles[1, k], tiles[1, k + 1]], axis=1),
            ],
            axis=0,
        )
        term = jnp.dot(left, right, preferred_element_type=jnp.float32)
        for row in range(2):
            for at in range(2):
                acc_ref[cols_ref[first + row, k + at]] += term[
                    row * feats : (row + 1) * feats, at * side : (at + 1) * side
                ]


def hand_out(acc_ref, out_ref):
    per_dev = out_ref.shape[3]
    half = out_ref.shape[4]
    for x in range(RING):
        for y in range(RING):
            got = acc_ref[pl.ds((x * RING + y) * per_dev, per_dev)].astype(out_ref.dtype)
            out_ref[0, x, y] = got[:, :half]
            out_ref[1, y, x] = got[:, half:]


def spread_kernel(cols_ref, vals_ref, tiles_ref, out_ref, acc_ref):
    step = pl.program_id(0)

    @pl.when(step == 0)
    def _():
        acc_ref[...] = jnp.zeros_like(acc_ref)

    add_terms(acc_ref, cols_ref, vals_ref[...], tiles_ref, 2 * step)

    @pl.when(step == pl.num_programs(0) - 1)
    def _():
        hand_out(acc_ref, out_ref)


def stream_kernel(cols_hbm, vals_hbm, tiles_hbm, out_ref, tiles_ref, acc_ref, cols_ref, vals_ref, sems):
    pairs = tiles_ref.shape[0] // 2
    side = tiles_ref.shape[2]
    small = [
        pltpu.make_async_copy(cols_hbm, cols_ref, sems.at[pairs]),
        pltpu.make_async_copy(vals_hbm, vals_ref, sems.at[pairs + 1]),
    ]
    for copy in small:
        copy.start()

    def tiles_copy(i):
        at = pl.ds(2 * i, 2)
        return pltpu.make_async_copy(tiles_hbm.at[at], tiles_ref.at[at], sems.at[i])

    for i in range(pairs):
        tiles_copy(i).start()
    acc_ref[...] = jnp.zeros_like(acc_ref)
    for copy in small:
        copy.wait()

    def body(i, carry):
        tiles_copy(i).wait()
        vals = vals_ref[:, pl.ds(pl.multiple_of(2 * side * i, 2 * side), 2 * side)]
        add_terms(acc_ref, cols_ref, vals, tiles_ref.at[pl.ds(2 * i, 2)], 2 * i)
        return carry

    lax.fori_loop(0, pairs, body, 0)
    hand_out(acc_ref, out_ref)


def spread(block_cols, vals_t, edge_tiles, stream):
    rows, per_row, side, _ = edge_tiles.shape
    feats = vals_t.shape[0]
    out = (2, RING, RING, rows, feats // 2, side)
    acc = pltpu.VMEM((rows * ROWS, feats, side), jnp.float32)
    out_shape = jax.ShapeDtypeStruct(out, jnp.bfloat16)
    if stream:
        hbm = pl.BlockSpec(memory_space=pltpu.HBM)
        return pl.pallas_call(
            stream_kernel,
            out_shape=(out_shape, jax.ShapeDtypeStruct(edge_tiles.shape, edge_tiles.dtype)),
            in_specs=[hbm] * 3,
            out_specs=[pl.BlockSpec(memory_space=pltpu.VMEM)] * 2,
            scratch_shapes=[
                acc,
                pltpu.SMEM(block_cols.shape, jnp.int32),
                pltpu.VMEM(vals_t.shape, vals_t.dtype),
                pltpu.SemaphoreType.DMA((rows // 2 + 2,)),
            ],
            compiler_params=pltpu.CompilerParams(vmem_limit_bytes=30 << 20),
        )(*(pltpu.with_memory_space_constraint(v, pltpu.HBM) for v in (block_cols, vals_t, edge_tiles)))
    return pl.pallas_call(
        spread_kernel,
        out_shape=out_shape,
        grid_spec=pltpu.PrefetchScalarGridSpec(
            num_scalar_prefetch=1,
            grid=(rows // 2,),
            in_specs=[
                pl.BlockSpec((feats, 2 * side), lambda i, c: (0, i)),
                pl.BlockSpec((2, per_row, side, side), lambda i, c: (i, 0, 0, 0)),
            ],
            out_specs=pl.BlockSpec(out, lambda i, c: (0,) * 6),
            scratch_shapes=[acc],
        ),
        compiler_params=pltpu.CompilerParams(vmem_limit_bytes=28 << 20),
    )(block_cols, vals_t, edge_tiles)


def to_pieces(grad, pieces_ref):
    _, tall, wide = pieces_ref.shape
    for p in range(ROWS):
        a, b = p // RING, p % RING
        pieces_ref[p] = grad[a * tall : (a + 1) * tall, b * wide : (b + 1) * wide].astype(pieces_ref.dtype)


def from_pieces(pieces_ref, grad_ref):
    _, tall, wide = pieces_ref.shape
    for p in range(ROWS):
        a, b = p // RING, p % RING
        grad_ref[a * tall : (a + 1) * tall, b * wide : (b + 1) * wide] = pieces_ref[p].astype(grad_ref.dtype)


def layer_kernel(first, *refs):
    if first:
        part_ref, weight_ref, acts_ref, mask_ref, value_ref, pieces_ref = refs[:6]
        in1, mid, in2, full, total_ref, s1, r1, s2, r2, sz, rz, sc, rc = refs[6:]
    else:
        part_ref, weight_ref, acts_ref, early_ref, value_ref, grad_ref, early_grad_ref = refs[:7]
        in1, mid, in2, full, total_ref, s1, r1, s2, r2, sz, rz, sc, rc = refs[7:20]
        pieces_ref, gather1, gather2, sg, rg, sb, rb = refs[20:]
    blk, half, side = part_ref.shape[3:]
    feats = 2 * half
    devs = full.shape[0]
    f32, bf16 = jnp.float32, jnp.bfloat16
    starts = [sum(GROUPS[:g]) for g in range(len(GROUPS))]

    row, col = lax.axis_index("row"), lax.axis_index("col")
    pos = (row // RING, lax.rem(row, RING))
    z, core = col // 2, lax.rem(col, 2)
    step = (1, -1, 2)
    lanes = [(h, d) for h in range(2) for d in range(2)]

    def wrap(v):
        return lax.rem(v + RING, RING)

    def plane(axis, d):
        x, y = pos
        if axis == 0:
            return (wrap(x + step[d]) * RING + y, col)
        return (x * RING + wrap(y + step[d]), col)

    def along(d):
        return (row, wrap(z + step[d]) * 2 + core)

    sibling = (row, z * 2 + 1 - core)
    peers = [(lax.rem(row + off, ROWS), col) for off in range(1, ROWS)]

    barrier = pltpu.get_barrier_semaphore()
    met = [plane(a, d) for a in range(2) for d in range(3)] if first else peers
    met = met + [along(0), along(1), along(2), sibling]
    for dev in met:
        pl.semaphore_signal(barrier, inc=1, device_id=dev, device_id_type=MESH)
    pl.semaphore_wait(barrier, len(met))

    started = []

    def send(src, dst, send_sem, recv_sem, dev):
        copy = pltpu.make_async_remote_copy(
            src_ref=src, dst_ref=dst, send_sem=send_sem, recv_sem=recv_sem,
            device_id=dev, device_id_type=MESH,
        )
        copy.start()
        started.append(copy)
        return copy

    def blocks(g, lo=None):
        if lo is None:
            return pl.ds(starts[g], GROUPS[g])
        return pl.ds(starts[g] + lo * (GROUPS[g] // 2), GROUPS[g] // 2)

    def slots(g):
        return pl.ds(starts[g] // 2, GROUPS[g] // 2)

    far, near, both, direct, hop, hand = ({} for _ in range(6))
    summed = []

    def send_far(g):
        for h, d in lanes:
            far[h, d, g] = send(
                part_ref.at[h, wrap(pos[h] + 2), :, blocks(g, d)],
                in1.at[h, d, 0, :, slots(g)], s1.at[h, d, 0, g], r1.at[h, d, 0, g], plane(h, d))

    def send_near(g):
        for h, d in lanes:
            near[h, d, g] = send(
                part_ref.at[h, wrap(pos[h] + step[d]), :, blocks(g, 1 - d)],
                in1.at[h, d, 1, :, slots(g)], s1.at[h, d, 1, g], r1.at[h, d, 1, g], plane(h, d))

    def send_both(g):
        for h, d in lanes:
            far[h, d, g].wait_recv()
            got = in1.at[h, d, 0, :, slots(g)]
            mine = part_ref[h, wrap(pos[h] + step[d]), :, blocks(g, d)]
            got[...] = (got[...].astype(f32) + mine.astype(f32)).astype(bf16)
            both[h, d, g] = send(
                got, in1.at[h, d, 2, :, slots(g)], s1.at[h, d, 2, g], r1.at[h, d, 2, g], plane(h, d))

    def second_ring(g):
        for h in range(2):
            other = pos[1 - h]
            for lo in range(2):
                both[h, lo, g].wait_recv()
                near[h, 1 - lo, g].wait_recv()
                total = part_ref[h, pos[h], :, blocks(g, lo)].astype(f32)
                total += in1[h, lo, 2, :, slots(g)].astype(f32)
                total += in1[h, 1 - lo, 1, :, slots(g)].astype(f32)
                mid[h, :, blocks(g, lo)] = total.astype(bf16)
            for d in (2, 0, 1):
                direct[h, d, g] = send(
                    mid.at[h, wrap(other + step[d]), blocks(g)],
                    in2.at[h, d, blocks(g)], s2.at[h, d, g], r2.at[h, d, g], plane(1 - h, d))

    def give(c, g, key):
        spot = full.at[c, :, blocks(g)]
        hand[key, g] = send(spot, spot, sc.at[key, g], rc.at[key, g], sibling)

    def finish(g):
        for h in range(2):
            other = pos[1 - h]
            total = mid[h, other, blocks(g)].astype(f32)
            for d in range(3):
                direct[h, d, g].wait_recv()
                total += in2[h, d, blocks(g)].astype(f32)
            full[col, h, blocks(g)] = total.astype(bf16)
        for d in (2, 0, 1):
            spot = full.at[col, :, blocks(g)]
            hop[d, g] = send(spot, spot, sz.at[d, g], rz.at[d, g], along(d))
        give(col, g, 3)

    def pass_on(g):
        for d in (0, 1, 2):
            hop[d, g].wait_recv()
            give(wrap(z - step[d]) * 2 + core, g, d)

    def products(g):
        for key in range(4):
            hand[key, g].wait_recv()
        right = jnp.concatenate(
            [
                jnp.concatenate([full[c, h, starts[g] + b] for c in range(devs) for h in range(2)], axis=0)
                for b in range(GROUPS[g])
            ],
            axis=1,
        )
        at = pl.ds(starts[g] * side, GROUPS[g] * side)
        value = jnp.dot(weight_ref[...], right, preferred_element_type=f32)
        if first:
            value = value * mask_ref[:, at].astype(f32)
        value_ref[:, at] = value.astype(bf16)
        grad = lax.dot_general(
            acts_ref[:, at], right, (((1,), (1,)), ((), ())), preferred_element_type=f32
        )
        if summed:
            grad += total_ref[...]
        summed.append(g)
        if len(summed) < len(GROUPS):
            total_ref[...] = grad
        else:
            to_pieces(grad, pieces_ref)

    out, back = {}, {}

    def send_pieces(n, src):
        for i, dev in enumerate(peers):
            out[n, i] = send(src.at[dev[0]], gather1.at[n, i], sg.at[n, i], rg.at[n, i], dev)

    def add_pieces(n, src):
        total = src[row].astype(f32)
        for i, dev in enumerate(peers):
            out[n, i].wait_recv()
            total += gather1[n, i].astype(f32)
        gather2[n, row] = total.astype(bf16)
        for i, dev in enumerate(peers):
            spot = gather2.at[n, row]
            back[n, i] = send(spot, spot, sb.at[n, i], rb.at[n, i], dev)

    def take_pieces(n, dst):
        for i in range(len(peers)):
            back[n, i].wait_recv()
        from_pieces(gather2.at[n], dst)

    stages = dict(
        f=send_far, o=send_near, b=send_both, c=second_ring, e=finish, h=pass_on, p=products,
    )
    for at, word in enumerate(ORDER):
        stages[word[0]](int(word[1:]))
        if not first:
            if at == len(ORDER) // 4:
                send_pieces(0, early_ref)
            if at == len(ORDER) // 2:
                add_pieces(0, early_ref)
            if at == len(ORDER) - 8:
                take_pieces(0, early_grad_ref)
    if not first:
        send_pieces(1, pieces_ref)
        add_pieces(1, pieces_ref)
        take_pieces(1, grad_ref)
    for copy in started:
        copy.wait_send()


def layer(part, weight, acts_t, extra, collective_id):
    first = collective_id == 0
    blk, half, side = part.shape[3:]
    feats, rows = acts_t.shape
    devs = weight.shape[1] // feats
    groups = len(GROUPS)
    vmem = pl.BlockSpec(memory_space=pltpu.VMEM)
    dma = pltpu.SemaphoreType.DMA
    bf16, f32 = jnp.bfloat16, jnp.float32
    grad = (feats, devs * feats)
    pieces = (ROWS, feats // RING, devs * feats // RING)
    scratch = [
        pltpu.VMEM((2, 2, 3, RING, blk // 2, half, side), bf16),
        pltpu.VMEM((2, RING, blk, half, side), bf16),
        pltpu.VMEM((2, 3, blk, half, side), bf16),
        pltpu.VMEM((devs, 2, blk, half, side), bf16),
        pltpu.VMEM(grad, f32),
    ]
    for shape in ((2, 2, 3), (2, 3), (3,), (4,)):
        scratch += [dma(shape + (groups,)), dma(shape + (groups,))]
    out_shape = [jax.ShapeDtypeStruct((feats, rows), bf16)]
    if first:
        out_shape += [jax.ShapeDtypeStruct(pieces, bf16)]
    else:
        out_shape += [jax.ShapeDtypeStruct(grad, f32)] * 2
        scratch += [
            pltpu.VMEM(pieces, bf16),
            pltpu.VMEM((2, ROWS - 1) + pieces[1:], bf16),
            pltpu.VMEM((2,) + pieces, bf16),
        ]
        scratch += [dma((2, ROWS - 1))] * 4
    return pl.pallas_call(
        functools.partial(layer_kernel, first),
        out_shape=out_shape,
        in_specs=[vmem] * 4,
        out_specs=[vmem] * len(out_shape),
        scratch_shapes=scratch,
        compiler_params=pltpu.CompilerParams(
            collective_id=collective_id, has_side_effects=True, vmem_limit_bytes=32 << 20
        ),
    )(part, weight, acts_t, extra)


def per_device(
    node_feats, hidden_act, grad_out, relu_mask, edge_tiles, block_cols, weight_one, weight_two
):
    part, tiles = spread(block_cols, grad_out.T, edge_tiles, True)
    delta_t, pieces = layer(part, weight_two, hidden_act.T, relu_mask.T, 0)
    part = spread(block_cols, delta_t, tiles, False)
    input_grad_t, first_grad, second_grad = layer(part, weight_one, node_feats.T, pieces, 1)
    return (input_grad_t.T, first_grad, second_grad)


def solution(mesh):
    in_specs = (
        P("row", "col"),
        P("row", "col"),
        P("row", "col"),
        P("row", "col"),
        P("row", None, None, None),
        P("row", None),
        P("col", None),
        P("col", None),
    )
    out_specs = (P("row", "col"), P("col", None), P("col", None))
    return jax.shard_map(
        per_device, mesh=mesh, in_specs=in_specs, out_specs=out_specs, check_vma=False
    )
```

```python
import functools
import jax
import jax.numpy as jnp
from jax import lax
from jax.experimental import pallas as pl
from jax.experimental.pallas import tpu as pltpu
from jax.sharding import PartitionSpec as P

RING = 4
ROWS = RING * RING
GROUPS = (4, 4, 4, 2, 2)
ORDER = (
    "f2", "f1", "o1", "o0", "b2", "b1", "f0", "f3", "o2", "c1", "b0", "f4",
    "c2", "o3", "b3", "e1", "c0", "o4", "e2", "b4", "c3", "e0", "c4", "h1",
    "e3", "h2", "e4", "h0", "h3", "p0", "p1", "h4", "p2", "p3", "p4",
)
MESH = pl.DeviceIdType.MESH


def tile_terms(vals, tiles, use):
    feats = vals.shape[0]
    side = tiles.shape[2]
    blank = jnp.zeros((feats, side), vals.dtype)
    left = jnp.concatenate(
        [
            jnp.concatenate([vals[:, :side], blank], axis=1),
            jnp.concatenate([blank, vals[:, side:]], axis=1),
        ],
        axis=0,
    )
    for k in range(0, tiles.shape[1], 2):
        right = jnp.concatenate(
            [
                jnp.concatenate([tiles[0, k], tiles[0, k + 1]], axis=1),
                jnp.concatenate([tiles[1, k], tiles[1, k + 1]], axis=1),
            ],
            axis=0,
        )
        term = jnp.dot(left, right, preferred_element_type=jnp.float32)
        for row in range(2):
            for at in range(2):
                use(row, k + at, term[row * feats : (row + 1) * feats, at * side : (at + 1) * side])


def stream_kernel(
    cols_hbm, vals_hbm, tiles_hbm, out_ref, tiles_ref, before_ref, last_ref, acc_ref, cols_ref, vals_ref, sems
):
    rows, per_row, side, _ = tiles_ref.shape
    pairs = rows // 2
    small = [
        pltpu.make_async_copy(cols_hbm, cols_ref, sems.at[pairs]),
        pltpu.make_async_copy(vals_hbm, vals_ref, sems.at[pairs + 1]),
    ]
    for copy in small:
        copy.start()

    def tiles_copy(i):
        at = pl.ds(2 * i, 2)
        return pltpu.make_async_copy(tiles_hbm.at[at], tiles_ref.at[at], sems.at[i])

    for i in range(pairs):
        tiles_copy(i).start()

    def clear(i, carry):
        for at in range(8):
            last_ref[8 * i + at] = rows * per_row
        acc_ref[pl.ds(8 * i, 8)] = jnp.zeros((8,) + acc_ref.shape[1:], acc_ref.dtype)
        return carry

    lax.fori_loop(0, acc_ref.shape[0] // 8, clear, 0)
    for copy in small:
        copy.wait()

    def body(i, carry):
        tiles_copy(i).wait()
        vals = vals_ref[:, pl.ds(pl.multiple_of(2 * side * i, 2 * side), 2 * side)]

        def use(row, k, term):
            target = cols_ref[2 * i + row, k]
            before_ref[2 * i + row, k] = last_ref[target]
            last_ref[target] = (2 * i + row) * per_row + k
            acc_ref[target] += term

        tile_terms(vals, tiles_ref.at[pl.ds(2 * i, 2)], use)
        return carry

    lax.fori_loop(0, pairs, body, 0)
    per_dev = out_ref.shape[3]
    half = out_ref.shape[4]
    for x in range(RING):
        for y in range(RING):
            got = acc_ref[pl.ds((x * RING + y) * per_dev, per_dev)].astype(out_ref.dtype)
            out_ref[0, x, y] = got[:, :half]
            out_ref[1, y, x] = got[:, half:]


def stream(block_cols, vals_t, edge_tiles):
    rows, per_row, side, _ = edge_tiles.shape
    feats = vals_t.shape[0]
    hbm = pl.BlockSpec(memory_space=pltpu.HBM)
    vmem = pl.BlockSpec(memory_space=pltpu.VMEM)
    smem = pl.BlockSpec(memory_space=pltpu.SMEM)
    return pl.pallas_call(
        stream_kernel,
        out_shape=(
            jax.ShapeDtypeStruct((2, RING, RING, rows, feats // 2, side), jnp.bfloat16),
            jax.ShapeDtypeStruct(edge_tiles.shape, edge_tiles.dtype),
            jax.ShapeDtypeStruct(block_cols.shape, jnp.int32),
            jax.ShapeDtypeStruct((rows * ROWS,), jnp.int32),
        ),
        in_specs=[hbm] * 3,
        out_specs=[vmem, vmem, smem, smem],
        scratch_shapes=[
            pltpu.VMEM((rows * ROWS, feats, side), jnp.float32),
            pltpu.SMEM(block_cols.shape, jnp.int32),
            pltpu.VMEM(vals_t.shape, vals_t.dtype),
            pltpu.SemaphoreType.DMA((rows // 2 + 2,)),
        ],
        compiler_params=pltpu.CompilerParams(vmem_limit_bytes=20 << 20),
    )(*(pltpu.with_memory_space_constraint(v, pltpu.HBM) for v in (block_cols, vals_t, edge_tiles)))


def to_pieces(grad, pieces_ref):
    _, tall, wide = pieces_ref.shape
    for p in range(ROWS):
        a, b = p // RING, p % RING
        pieces_ref[p] = grad[a * tall : (a + 1) * tall, b * wide : (b + 1) * wide].astype(pieces_ref.dtype)


def from_pieces(pieces_ref, grad_ref):
    _, tall, wide = pieces_ref.shape
    for p in range(ROWS):
        a, b = p // RING, p % RING
        grad_ref[a * tall : (a + 1) * tall, b * wide : (b + 1) * wide] = pieces_ref[p].astype(grad_ref.dtype)


def layers_kernel(
    part_ref, tiles_ref, before_ref, last_ref, weight2_ref, hidden_ref, mask_ref, weight1_ref, feats_ref,
    input_grad_ref, first_ref, second_ref,
    in1s, mids, in2s, fulls, totals, delta_ref, chain_ref, part2_ref, all_pieces, gather1, gather2,
    s1s, r1s, s2s, r2s, szs, rzs, scs, rcs, sg, rg, sb, rb,
):
    blk, half, side = part_ref.shape[3:]
    feats = 2 * half
    devs = fulls.shape[1]
    per_row = tiles_ref.shape[1]
    none = chain_ref.shape[0] - 1
    f32, bf16 = jnp.float32, jnp.bfloat16
    starts = [sum(GROUPS[:g]) for g in range(len(GROUPS))]

    row, col = lax.axis_index("row"), lax.axis_index("col")
    pos = (row // RING, lax.rem(row, RING))
    z, core = col // 2, lax.rem(col, 2)
    step = (1, -1, 2)
    lanes = [(h, d) for h in range(2) for d in range(2)]

    def wrap(v):
        return lax.rem(v + RING, RING)

    def plane(axis, d):
        x, y = pos
        if axis == 0:
            return (wrap(x + step[d]) * RING + y, col)
        return (x * RING + wrap(y + step[d]), col)

    def along(d):
        return (row, wrap(z + step[d]) * 2 + core)

    sibling = (row, z * 2 + 1 - core)
    peers = [(lax.rem(row + off, ROWS), col) for off in range(1, ROWS)]

    barrier = pltpu.get_barrier_semaphore()
    met = peers + [along(0), along(1), along(2), sibling]
    for dev in met:
        pl.semaphore_signal(barrier, inc=1, device_id=dev, device_id_type=MESH)
    pl.semaphore_wait(barrier, len(met))

    started = []

    def send(src, dst, send_sem, recv_sem, dev):
        copy = pltpu.make_async_remote_copy(
            src_ref=src, dst_ref=dst, send_sem=send_sem, recv_sem=recv_sem,
            device_id=dev, device_id_type=MESH,
        )
        copy.start()
        started.append(copy)
        return copy

    def blocks(g, lo=None):
        if lo is None:
            return pl.ds(starts[g], GROUPS[g])
        return pl.ds(starts[g] + lo * (GROUPS[g] // 2), GROUPS[g] // 2)

    def slots(g):
        return pl.ds(starts[g] // 2, GROUPS[g] // 2)

    chain_ref[none] = jnp.zeros((feats, side), f32)

    def chain_group(g):
        def body(i, carry):
            vals = delta_ref[:, pl.ds(pl.multiple_of(2 * side * i, 2 * side), 2 * side)]

            def use(row, k, term):
                chain_ref[(2 * i + row) * per_row + k] = term + chain_ref[before_ref[2 * i + row, k]]

            tile_terms(vals, tiles_ref.at[pl.ds(2 * i, 2)], use)
            return carry

        lax.fori_loop(starts[g] // 2, (starts[g] + GROUPS[g]) // 2, body, 0)

    def chain_ends():
        def body(dev, carry):
            x, y = dev // RING, lax.rem(dev, RING)
            for b in range(blk):
                got = chain_ref[last_ref[dev * blk + b]].astype(bf16)
                part2_ref[0, x, y, b] = got[:half]
                part2_ref[1, y, x, b] = got[half:]
            return carry

        lax.fori_loop(0, ROWS, body, 0)

    def layer_stages(n, part_ref, weight_ref, acts_ref, mask_ref, value_ref, pieces_ref):
        in1, mid, in2, full, total_ref = (ref.at[n] for ref in (in1s, mids, in2s, fulls, totals))
        s1, r1, s2, r2, sz, rz, sc, rc = (ref.at[n] for ref in (s1s, r1s, s2s, r2s, szs, rzs, scs, rcs))
        far, near, both, direct, hop, hand = ({} for _ in range(6))
        summed = []

        def send_far(g):
            for h, d in lanes:
                far[h, d, g] = send(
                    part_ref.at[h, wrap(pos[h] + 2), :, blocks(g, d)],
                    in1.at[h, d, 0, :, slots(g)], s1.at[h, d, 0, g], r1.at[h, d, 0, g], plane(h, d))

        def send_near(g):
            for h, d in lanes:
                near[h, d, g] = send(
                    part_ref.at[h, wrap(pos[h] + step[d]), :, blocks(g, 1 - d)],
                    in1.at[h, d, 1, :, slots(g)], s1.at[h, d, 1, g], r1.at[h, d, 1, g], plane(h, d))

        def send_both(g):
            for h, d in lanes:
                far[h, d, g].wait_recv()
                got = in1.at[h, d, 0, :, slots(g)]
                mine = part_ref[h, wrap(pos[h] + step[d]), :, blocks(g, d)]
                got[...] = (got[...].astype(f32) + mine.astype(f32)).astype(bf16)
                both[h, d, g] = send(
                    got, in1.at[h, d, 2, :, slots(g)], s1.at[h, d, 2, g], r1.at[h, d, 2, g], plane(h, d))

        def second_ring(g):
            for h in range(2):
                other = pos[1 - h]
                for lo in range(2):
                    both[h, lo, g].wait_recv()
                    near[h, 1 - lo, g].wait_recv()
                    total = part_ref[h, pos[h], :, blocks(g, lo)].astype(f32)
                    total += in1[h, lo, 2, :, slots(g)].astype(f32)
                    total += in1[h, 1 - lo, 1, :, slots(g)].astype(f32)
                    mid[h, :, blocks(g, lo)] = total.astype(bf16)
                for d in (2, 0, 1):
                    direct[h, d, g] = send(
                        mid.at[h, wrap(other + step[d]), blocks(g)],
                        in2.at[h, d, blocks(g)], s2.at[h, d, g], r2.at[h, d, g], plane(1 - h, d))

        def give(c, g, key):
            spot = full.at[c, :, blocks(g)]
            hand[key, g] = send(spot, spot, sc.at[key, g], rc.at[key, g], sibling)

        def finish(g):
            for h in range(2):
                other = pos[1 - h]
                total = mid[h, other, blocks(g)].astype(f32)
                for d in range(3):
                    direct[h, d, g].wait_recv()
                    total += in2[h, d, blocks(g)].astype(f32)
                full[col, h, blocks(g)] = total.astype(bf16)
            for d in (2, 0, 1):
                spot = full.at[col, :, blocks(g)]
                hop[d, g] = send(spot, spot, sz.at[d, g], rz.at[d, g], along(d))
            give(col, g, 3)

        def pass_on(g):
            for d in (0, 1, 2):
                hop[d, g].wait_recv()
                give(wrap(z - step[d]) * 2 + core, g, d)

        def products(g):
            for key in range(4):
                hand[key, g].wait_recv()
            right = jnp.concatenate(
                [
                    jnp.concatenate([full[c, h, starts[g] + b] for c in range(devs) for h in range(2)], axis=0)
                    for b in range(GROUPS[g])
                ],
                axis=1,
            )
            at = pl.ds(starts[g] * side, GROUPS[g] * side)
            value = jnp.dot(weight_ref[...], right, preferred_element_type=f32)
            if mask_ref is not None:
                value = value * mask_ref[:, at].astype(f32)
            value_ref[:, at] = value.astype(bf16)
            grad = lax.dot_general(
                acts_ref[:, at], right, (((1,), (1,)), ((), ())), preferred_element_type=f32
            )
            if summed:
                grad += total_ref[...]
            summed.append(g)
            if len(summed) < len(GROUPS):
                total_ref[...] = grad
            else:
                to_pieces(grad, pieces_ref)
            if n == 0:
                chain_group(g)

        return dict(
            f=send_far, o=send_near, b=send_both, c=second_ring, e=finish, h=pass_on, p=products,
        )

    out, back = {}, {}

    def send_pieces(n, src):
        for i, dev in enumerate(peers):
            out[n, i] = send(src.at[dev[0]], gather1.at[n, i], sg.at[n, i], rg.at[n, i], dev)

    def add_pieces(n, src):
        total = src[row].astype(f32)
        for i, dev in enumerate(peers):
            out[n, i].wait_recv()
            total += gather1[n, i].astype(f32)
        gather2[n, row] = total.astype(bf16)
        for i, dev in enumerate(peers):
            spot = gather2.at[n, row]
            back[n, i] = send(spot, spot, sb.at[n, i], rb.at[n, i], dev)

    def take_pieces(n, dst):
        for i in range(len(peers)):
            back[n, i].wait_recv()
        from_pieces(gather2.at[n], dst)

    stages = layer_stages(0, part_ref, weight2_ref, hidden_ref, mask_ref, delta_ref, all_pieces.at[0])
    for word in ORDER:
        stages[word[0]](int(word[1:]))
    chain_ends()
    stages = layer_stages(1, part2_ref, weight1_ref, feats_ref, None, input_grad_ref, all_pieces.at[1])
    for at, word in enumerate(ORDER):
        stages[word[0]](int(word[1:]))
        if at == len(ORDER) // 4:
            send_pieces(0, all_pieces.at[0])
        if at == len(ORDER) // 2:
            add_pieces(0, all_pieces.at[0])
        if at == len(ORDER) - 8:
            take_pieces(0, second_ref)
    send_pieces(1, all_pieces.at[1])
    add_pieces(1, all_pieces.at[1])
    take_pieces(1, first_ref)
    for copy in started:
        copy.wait_send()


def layers(part, tiles, before, last, weight_two, hidden_t, mask_t, weight_one, feats_t):
    blk, half, side = part.shape[3:]
    feats, rows = feats_t.shape
    devs = weight_one.shape[1] // feats
    groups = len(GROUPS)
    vmem = pl.BlockSpec(memory_space=pltpu.VMEM)
    smem = pl.BlockSpec(memory_space=pltpu.SMEM)
    dma = pltpu.SemaphoreType.DMA
    bf16, f32 = jnp.bfloat16, jnp.float32
    grad = (feats, devs * feats)
    pieces = (ROWS, feats // RING, devs * feats // RING)
    scratch = [
        pltpu.VMEM((2, 2, 2, 3, RING, blk // 2, half, side), bf16),
        pltpu.VMEM((2, 2, RING, blk, half, side), bf16),
        pltpu.VMEM((2, 2, 3, blk, half, side), bf16),
        pltpu.VMEM((2, devs, 2, blk, half, side), bf16),
        pltpu.VMEM((2,) + grad, f32),
        pltpu.VMEM((feats, rows), bf16),
        pltpu.VMEM((before.size + 1, feats, side), f32),
        pltpu.VMEM(part.shape, bf16),
        pltpu.VMEM((2,) + pieces, bf16),
        pltpu.VMEM((2, ROWS - 1) + pieces[1:], bf16),
        pltpu.VMEM((2,) + pieces, bf16),
    ]
    for shape in ((2, 2, 3), (2, 3), (3,), (4,)):
        scratch += [dma((2,) + shape + (groups,)), dma((2,) + shape + (groups,))]
    scratch += [dma((2, ROWS - 1))] * 4
    return pl.pallas_call(
        layers_kernel,
        out_shape=(
            jax.ShapeDtypeStruct((feats, rows), bf16),
            jax.ShapeDtypeStruct(grad, f32),
            jax.ShapeDtypeStruct(grad, f32),
        ),
        in_specs=[vmem, vmem, smem, smem] + [vmem] * 5,
        out_specs=[vmem] * 3,
        scratch_shapes=scratch,
        compiler_params=pltpu.CompilerParams(
            collective_id=0, has_side_effects=True, vmem_limit_bytes=36 << 20
        ),
    )(part, tiles, before, last, weight_two, hidden_t, mask_t, weight_one, feats_t)


def per_device(
    node_feats, hidden_act, grad_out, relu_mask, edge_tiles, block_cols, weight_one, weight_two
):
    part, tiles, before, last = stream(block_cols, grad_out.T, edge_tiles)
    input_grad_t, first_grad, second_grad = layers(
        part, tiles, before, last, weight_two, hidden_act.T, relu_mask.T, weight_one, node_feats.T
    )
    return (input_grad_t.T, first_grad, second_grad)


def solution(mesh):
    in_specs = (
        P("row", "col"),
        P("row", "col"),
        P("row", "col"),
        P("row", "col"),
        P("row", None, None, None),
        P("row", None),
        P("col", None),
        P("col", None),
    )
    out_specs = (P("row", "col"), P("col", None), P("col", None))
    return jax.shard_map(
        per_device, mesh=mesh, in_specs=in_specs, out_specs=out_specs, check_vma=False
    )
```

```python
import functools
import jax
import jax.numpy as jnp
from jax import lax
from jax.experimental import pallas as pl
from jax.experimental.pallas import tpu as pltpu
from jax.sharding import PartitionSpec as P

RING = 4
ROWS = RING * RING
GROUPS = (6, 4, 2, 2, 2)
ORDER_ONE = (
    "f0", "f1", "o0", "b0", "b1", "o1", "f3", "c0", "f2", "c1", "o2", "f4",
    "e0", "b2", "o3", "b3", "o4", "b4", "e1", "c2", "c3", "c4", "h0", "e2",
    "e3", "h1", "e4", "p0", "h2", "h3", "p1", "h4", "p2", "p3", "p4",
)
ORDER_TWO = (
    "o3", "f0", "f1", "o0", "b0", "b1", "f2", "f3", "f4", "c0", "o2", "b3",
    "o1", "o4", "b2", "e0", "b4", "c3", "c1", "c2", "c4", "e3", "e1", "h0",
    "e2", "e4", "h1", "a0", "p1", "h2", "p0", "h4", "h3", "p4", "p3", "p2",
)
MESH = pl.DeviceIdType.MESH


def tile_terms(vals, tiles, use):
    feats = vals.shape[0]
    side = tiles.shape[2]
    blank = jnp.zeros((feats, side), vals.dtype)
    left = jnp.concatenate(
        [
            jnp.concatenate([vals[:, :side], blank], axis=1),
            jnp.concatenate([blank, vals[:, side:]], axis=1),
        ],
        axis=0,
    )
    for k in range(0, tiles.shape[1], 2):
        right = jnp.concatenate(
            [
                jnp.concatenate([tiles[0, k], tiles[0, k + 1]], axis=1),
                jnp.concatenate([tiles[1, k], tiles[1, k + 1]], axis=1),
            ],
            axis=0,
        )
        term = jnp.dot(left, right, preferred_element_type=jnp.float32)
        for row in range(2):
            for at in range(2):
                use(row, k + at, term[row * feats : (row + 1) * feats, at * side : (at + 1) * side])


def stream_kernel(
    cols_hbm, vals_hbm, tiles_hbm, out_ref, tiles_ref, before_ref, last_ref, acc_ref, cols_ref, vals_ref, sems
):
    rows, per_row, side, _ = tiles_ref.shape
    pairs = rows // 2
    small = [
        pltpu.make_async_copy(cols_hbm, cols_ref, sems.at[pairs]),
        pltpu.make_async_copy(vals_hbm, vals_ref, sems.at[pairs + 1]),
    ]
    for copy in small:
        copy.start()

    def tiles_copy(i):
        at = pl.ds(2 * i, 2)
        return pltpu.make_async_copy(tiles_hbm.at[at], tiles_ref.at[at], sems.at[i])

    for i in range(pairs):
        tiles_copy(i).start()

    def clear(i, carry):
        for at in range(8):
            last_ref[8 * i + at] = rows * per_row
        acc_ref[pl.ds(8 * i, 8)] = jnp.zeros((8,) + acc_ref.shape[1:], acc_ref.dtype)
        return carry

    lax.fori_loop(0, acc_ref.shape[0] // 8, clear, 0)
    for copy in small:
        copy.wait()

    def body(i, carry):
        tiles_copy(i).wait()
        vals = vals_ref[:, pl.ds(pl.multiple_of(2 * side * i, 2 * side), 2 * side)]

        def use(row, k, term):
            target = cols_ref[2 * i + row, k]
            before_ref[2 * i + row, k] = last_ref[target]
            last_ref[target] = (2 * i + row) * per_row + k
            acc_ref[target] += term

        tile_terms(vals, tiles_ref.at[pl.ds(2 * i, 2)], use)
        return carry

    lax.fori_loop(0, pairs, body, 0)
    per_dev = out_ref.shape[3]
    half = out_ref.shape[4]
    for x in range(RING):
        for y in range(RING):
            got = acc_ref[pl.ds((x * RING + y) * per_dev, per_dev)].astype(out_ref.dtype)
            out_ref[0, x, y] = got[:, :half]
            out_ref[1, y, x] = got[:, half:]


def stream(block_cols, vals_t, edge_tiles):
    rows, per_row, side, _ = edge_tiles.shape
    feats = vals_t.shape[0]
    hbm = pl.BlockSpec(memory_space=pltpu.HBM)
    vmem = pl.BlockSpec(memory_space=pltpu.VMEM)
    smem = pl.BlockSpec(memory_space=pltpu.SMEM)
    return pl.pallas_call(
        stream_kernel,
        out_shape=(
            jax.ShapeDtypeStruct((2, RING, RING, rows, feats // 2, side), jnp.bfloat16),
            jax.ShapeDtypeStruct(edge_tiles.shape, edge_tiles.dtype),
            jax.ShapeDtypeStruct(block_cols.shape, jnp.int32),
            jax.ShapeDtypeStruct((rows * ROWS,), jnp.int32),
        ),
        in_specs=[hbm] * 3,
        out_specs=[vmem, vmem, smem, smem],
        scratch_shapes=[
            pltpu.VMEM((rows * ROWS, feats, side), jnp.float32),
            pltpu.SMEM(block_cols.shape, jnp.int32),
            pltpu.VMEM(vals_t.shape, vals_t.dtype),
            pltpu.SemaphoreType.DMA((rows // 2 + 2,)),
        ],
        compiler_params=pltpu.CompilerParams(vmem_limit_bytes=20 << 20),
    )(*(pltpu.with_memory_space_constraint(v, pltpu.HBM) for v in (block_cols, vals_t, edge_tiles)))


def to_pieces(grad, pieces_ref):
    _, tall, wide = pieces_ref.shape
    for p in range(ROWS):
        a, b = p // RING, p % RING
        pieces_ref[p] = grad[a * tall : (a + 1) * tall, b * wide : (b + 1) * wide].astype(pieces_ref.dtype)


def from_pieces(pieces_ref, grad_ref):
    _, tall, wide = pieces_ref.shape
    for p in range(ROWS):
        a, b = p // RING, p % RING
        grad_ref[a * tall : (a + 1) * tall, b * wide : (b + 1) * wide] = pieces_ref[p].astype(grad_ref.dtype)


def layers_kernel(
    part_ref, tiles_ref, before_ref, last_ref, weight2_ref, hidden_ref, mask_ref, weight1_ref, feats_ref,
    input_grad_ref, first_ref, second_ref,
    in1s, mids, in2s, fulls, totals, delta_ref, chain_ref, part2_ref, all_pieces, gather1, gather2,
    feats_all, reduced, wide_ref,
    s1s, r1s, s2s, r2s, szs, rzs, scs, rcs, sg, rg, sb, rb, sxz, rxz, sxc, rxc, sw, rw,
):
    blk, half, side = part_ref.shape[3:]
    feats = 2 * half
    devs = fulls.shape[1]
    per_row = tiles_ref.shape[1]
    none = chain_ref.shape[0] - 1
    f32, bf16 = jnp.float32, jnp.bfloat16
    starts = [sum(GROUPS[:g]) for g in range(len(GROUPS))]

    row, col = lax.axis_index("row"), lax.axis_index("col")
    pos = (row // RING, lax.rem(row, RING))
    z, core = col // 2, lax.rem(col, 2)
    step = (1, -1, 2)
    lanes = [(h, d) for h in range(2) for d in range(2)]

    def wrap(v):
        return lax.rem(v + RING, RING)

    def plane(axis, d):
        x, y = pos
        if axis == 0:
            return (wrap(x + step[d]) * RING + y, col)
        return (x * RING + wrap(y + step[d]), col)

    def along(d):
        return (row, wrap(z + step[d]) * 2 + core)

    sibling = (row, z * 2 + 1 - core)
    peers = [(lax.rem(row + off, ROWS), col) for off in range(1, ROWS)]

    barrier = pltpu.get_barrier_semaphore()
    met = peers + [along(0), along(1), along(2), sibling]
    for dev in met:
        pl.semaphore_signal(barrier, inc=1, device_id=dev, device_id_type=MESH)
    pl.semaphore_wait(barrier, len(met))

    started = []

    def send(src, dst, send_sem, recv_sem, dev):
        copy = pltpu.make_async_remote_copy(
            src_ref=src, dst_ref=dst, send_sem=send_sem, recv_sem=recv_sem,
            device_id=dev, device_id_type=MESH,
        )
        copy.start()
        started.append(copy)
        return copy

    def blocks(g, lo=None):
        if lo is None:
            return pl.ds(starts[g], GROUPS[g])
        return pl.ds(starts[g] + lo * (GROUPS[g] // 2), GROUPS[g] // 2)

    def slots(g):
        return pl.ds(starts[g] // 2, GROUPS[g] // 2)

    chain_ref[none] = jnp.zeros((feats, side), f32)

    feats_hop, feats_hand = {}, {}

    def gather_feats():
        feats_all[col] = feats_ref[...]
        for d in (2, 0, 1):
            feats_hop[d] = send(feats_ref, feats_all.at[col], sxz.at[d], rxz.at[d], along(d))
        feats_hand[3] = send(feats_ref, feats_all.at[col], sxc.at[3], rxc.at[3], sibling)

    def pass_feats():
        for d in range(3):
            feats_hop[d].wait_recv()
            spot = feats_all.at[wrap(z - step[d]) * 2 + core]
            feats_hand[d] = send(spot, spot, sxc.at[d], rxc.at[d], sibling)

    def chain_group(g):
        def body(i, carry):
            vals = delta_ref[:, pl.ds(pl.multiple_of(2 * side * i, 2 * side), 2 * side)]

            def use(row, k, term):
                chain_ref[(2 * i + row) * per_row + k] = term + chain_ref[before_ref[2 * i + row, k]]

            tile_terms(vals, tiles_ref.at[pl.ds(2 * i, 2)], use)
            return carry

        lax.fori_loop(starts[g] // 2, (starts[g] + GROUPS[g]) // 2, body, 0)

    def chain_ends():
        def body(dev, carry):
            x, y = dev // RING, lax.rem(dev, RING)
            for b in range(blk):
                got = chain_ref[last_ref[dev * blk + b]].astype(bf16)
                part2_ref[0, x, y, b] = got[:half]
                part2_ref[1, y, x, b] = got[half:]
            return carry

        lax.fori_loop(0, ROWS, body, 0)

    out, back = {}, {}

    def send_pieces(n, src):
        for i, dev in enumerate(peers):
            out[n, i] = send(src.at[dev[0]], gather1.at[n, i], sg.at[n, i], rg.at[n, i], dev)

    def piece_sum(n, src):
        total = src[row].astype(f32)
        for i in range(len(peers)):
            out[n, i].wait_recv()
            total += gather1[n, i].astype(f32)
        return total

    def add_pieces(n, src):
        total = piece_sum(n, src)
        gather2[n, row] = total.astype(bf16)
        for i, dev in enumerate(peers):
            spot = gather2.at[n, row]
            back[n, i] = send(spot, spot, sb.at[n, i], rb.at[n, i], dev)

    def take_pieces(n, dst):
        for i in range(len(peers)):
            back[n, i].wait_recv()
        from_pieces(gather2.at[n], dst)

    home = pos[1] == z

    def wide_copy(off, c):
        dev = (lax.rem(row + off, ROWS), pos[1] * 2 + c)
        return pltpu.make_async_remote_copy(
            src_ref=reduced, dst_ref=wide_ref.at[col, pos[0]], send_sem=sw.at[off, c], recv_sem=rw.at[col, pos[0]],
            device_id=dev, device_id_type=MESH,
        )

    def others(act):
        for c in range(2):
            for off in range(1, ROWS):
                act(wide_copy(off, c))

            @pl.when(pos[1] * 2 + c != col)
            def _():
                act(wide_copy(0, c))

    def send_wide():
        reduced[...] = piece_sum(1, all_pieces.at[1]).astype(bf16)
        others(lambda copy: copy.start())

        @pl.when(home)
        def _():
            wide_ref[col, pos[0]] = reduced[...]

    def take_wide():
        def body(i, carry):
            c, a = i // RING, lax.rem(i, RING)

            @pl.when(jnp.logical_not(home & (c == col) & (a == pos[0])))
            def _():
                pltpu.make_async_remote_copy(
                    src_ref=reduced, dst_ref=wide_ref.at[c, a], send_sem=sw.at[0, 0], recv_sem=rw.at[c, a],
                    device_id=sibling, device_id_type=MESH,
                ).wait_recv()

            return carry

        lax.fori_loop(0, devs * RING, body, 0)
        wide = wide_ref[...].reshape(devs * feats, side).astype(f32).T
        first_ref[...] = jnp.where(core == 0, wide[:feats], wide[feats:])
        others(lambda copy: copy.wait_send())

    def layer_stages(n, part_ref, weight_ref, acts_ref, mask_ref, value_ref, pieces_ref):
        in1, mid, in2, full, total_ref = (ref.at[n] for ref in (in1s, mids, in2s, fulls, totals))
        s1, r1, s2, r2, sz, rz, sc, rc = (ref.at[n] for ref in (s1s, r1s, s2s, r2s, szs, rzs, scs, rcs))
        far, near, both, direct, hop, hand = ({} for _ in range(6))
        summed = []

        def send_far(g):
            for h, d in lanes:
                far[h, d, g] = send(
                    part_ref.at[h, wrap(pos[h] + 2), :, blocks(g, d)],
                    in1.at[h, d, 0, :, slots(g)], s1.at[h, d, 0, g], r1.at[h, d, 0, g], plane(h, d))

        def send_near(g):
            for h, d in lanes:
                near[h, d, g] = send(
                    part_ref.at[h, wrap(pos[h] + step[d]), :, blocks(g, 1 - d)],
                    in1.at[h, d, 1, :, slots(g)], s1.at[h, d, 1, g], r1.at[h, d, 1, g], plane(h, d))

        def send_both(g):
            for h, d in lanes:
                far[h, d, g].wait_recv()
                got = in1.at[h, d, 0, :, slots(g)]
                mine = part_ref[h, wrap(pos[h] + step[d]), :, blocks(g, d)]
                got[...] = (got[...].astype(f32) + mine.astype(f32)).astype(bf16)
                both[h, d, g] = send(
                    got, in1.at[h, d, 2, :, slots(g)], s1.at[h, d, 2, g], r1.at[h, d, 2, g], plane(h, d))

        def second_ring(g):
            for h in range(2):
                other = pos[1 - h]
                for lo in range(2):
                    both[h, lo, g].wait_recv()
                    near[h, 1 - lo, g].wait_recv()
                    total = part_ref[h, pos[h], :, blocks(g, lo)].astype(f32)
                    total += in1[h, lo, 2, :, slots(g)].astype(f32)
                    total += in1[h, 1 - lo, 1, :, slots(g)].astype(f32)
                    mid[h, :, blocks(g, lo)] = total.astype(bf16)
                for d in (2, 0, 1):
                    direct[h, d, g] = send(
                        mid.at[h, wrap(other + step[d]), blocks(g)],
                        in2.at[h, d, blocks(g)], s2.at[h, d, g], r2.at[h, d, g], plane(1 - h, d))

        def give(c, g, key):
            spot = full.at[c, :, blocks(g)]
            hand[key, g] = send(spot, spot, sc.at[key, g], rc.at[key, g], sibling)

        def finish(g):
            for h in range(2):
                other = pos[1 - h]
                total = mid[h, other, blocks(g)].astype(f32)
                for d in range(3):
                    direct[h, d, g].wait_recv()
                    total += in2[h, d, blocks(g)].astype(f32)
                full[col, h, blocks(g)] = total.astype(bf16)
            for d in (2, 0, 1):
                spot = full.at[col, :, blocks(g)]
                hop[d, g] = send(spot, spot, sz.at[d, g], rz.at[d, g], along(d))
            give(col, g, 3)
            if n == 1:
                at = pl.ds(starts[g] * side, GROUPS[g] * side)
                left = jnp.concatenate(
                    [
                        jnp.concatenate([full[col, h, starts[g] + b] for h in range(2)], axis=0)
                        for b in range(GROUPS[g])
                    ],
                    axis=1,
                )
                add_grad(g, left, feats_all[:, :, at].reshape(devs * feats, GROUPS[g] * side))

        def pass_on(g):
            for d in (0, 1, 2):
                hop[d, g].wait_recv()
                give(wrap(z - step[d]) * 2 + core, g, d)

        def add_grad(g, left, right):
            grad = lax.dot_general(left, right, (((1,), (1,)), ((), ())), preferred_element_type=f32)
            if summed:
                grad += total_ref[...]
            summed.append(g)
            if len(summed) < len(GROUPS):
                total_ref[...] = grad
            else:
                to_pieces(grad, pieces_ref)
                send_pieces(n, pieces_ref)

        def products(g):
            for key in range(4):
                hand[key, g].wait_recv()
            right = jnp.concatenate(
                [
                    jnp.concatenate([full[c, h, starts[g] + b] for c in range(devs) for h in range(2)], axis=0)
                    for b in range(GROUPS[g])
                ],
                axis=1,
            )
            at = pl.ds(starts[g] * side, GROUPS[g] * side)
            value = jnp.dot(weight_ref[...], right, preferred_element_type=f32)
            if mask_ref is not None:
                value = value * mask_ref[:, at].astype(f32)
            value_ref[:, at] = value.astype(bf16)
            if n == 0:
                add_grad(g, acts_ref[:, at], right)
                chain_group(g)

        return dict(
            f=send_far, o=send_near, b=send_both, c=second_ring, e=finish, h=pass_on, p=products,
        )

    stages = layer_stages(0, part_ref, weight2_ref, hidden_ref, mask_ref, delta_ref, all_pieces.at[0])
    for at, word in enumerate(ORDER_ONE):
        stages[word[0]](int(word[1:]))
        if at == 2:
            gather_feats()
        if at == len(ORDER_ONE) - 6:
            pass_feats()
    chain_ends()
    stages = layer_stages(1, part2_ref, weight1_ref, feats_ref, None, input_grad_ref, all_pieces.at[1])
    for at, word in enumerate(ORDER_TWO):
        if word == "a0":
            send_wide()
        else:
            stages[word[0]](int(word[1:]))
        if at == len(ORDER_TWO) // 4:
            add_pieces(0, all_pieces.at[0])
            for key in range(4):
                feats_hand[key].wait_recv()
        if at == len(ORDER_TWO) // 2:
            take_pieces(0, second_ref)
    take_wide()
    for copy in started:
        copy.wait_send()


def layers(part, tiles, before, last, weight_two, hidden_t, mask_t, weight_one, feats_t):
    blk, half, side = part.shape[3:]
    feats, rows = feats_t.shape
    devs = weight_one.shape[1] // feats
    groups = len(GROUPS)
    vmem = pl.BlockSpec(memory_space=pltpu.VMEM)
    smem = pl.BlockSpec(memory_space=pltpu.SMEM)
    dma = pltpu.SemaphoreType.DMA
    bf16, f32 = jnp.bfloat16, jnp.float32
    grad = (feats, devs * feats)
    pieces = (ROWS, feats // RING, devs * feats // RING)
    scratch = [
        pltpu.VMEM((2, 2, 2, 3, RING, blk // 2, half, side), bf16),
        pltpu.VMEM((2, 2, RING, blk, half, side), bf16),
        pltpu.VMEM((2, 2, 3, blk, half, side), bf16),
        pltpu.VMEM((2, devs, 2, blk, half, side), bf16),
        pltpu.VMEM((2,) + grad, f32),
        pltpu.VMEM((feats, rows), bf16),
        pltpu.VMEM((before.size + 1, feats, side), f32),
        pltpu.VMEM(part.shape, bf16),
        pltpu.VMEM((2,) + pieces, bf16),
        pltpu.VMEM((2, ROWS - 1) + pieces[1:], bf16),
        pltpu.VMEM((2,) + pieces, bf16),
        pltpu.VMEM((devs, feats, rows), bf16),
        pltpu.VMEM(pieces[1:], bf16),
        pltpu.VMEM((devs, RING) + pieces[1:], bf16),
    ]
    for shape in ((2, 2, 3), (2, 3), (3,), (4,)):
        scratch += [dma((2,) + shape + (groups,)), dma((2,) + shape + (groups,))]
    scratch += [dma((2, ROWS - 1))] * 4 + [dma((3,))] * 2 + [dma((4,))] * 2
    scratch += [dma((ROWS, 2)), dma((devs, RING))]
    return pl.pallas_call(
        layers_kernel,
        out_shape=(
            jax.ShapeDtypeStruct((feats, rows), bf16),
            jax.ShapeDtypeStruct(grad, f32),
            jax.ShapeDtypeStruct(grad, f32),
        ),
        in_specs=[vmem, vmem, smem, smem] + [vmem] * 5,
        out_specs=[vmem] * 3,
        scratch_shapes=scratch,
        compiler_params=pltpu.CompilerParams(
            collective_id=0, has_side_effects=True, vmem_limit_bytes=36 << 20
        ),
    )(part, tiles, before, last, weight_two, hidden_t, mask_t, weight_one, feats_t)


def deliver_kernel(*refs):
    *arrays, sems = refs
    count = len(arrays) // 2
    copies = [pltpu.make_async_copy(arrays[i], arrays[count + i], sems.at[i]) for i in range(count)]
    for copy in copies:
        copy.start()
    for copy in copies:
        copy.wait()


def deliver(*arrays):
    return pl.pallas_call(
        deliver_kernel,
        out_shape=[jax.ShapeDtypeStruct(a.shape, a.dtype) for a in arrays],
        in_specs=[pl.BlockSpec(memory_space=pltpu.VMEM)] * len(arrays),
        out_specs=[pl.BlockSpec(memory_space=pl.ANY)] * len(arrays),
        scratch_shapes=[pltpu.SemaphoreType.DMA((len(arrays),))],
    )(*arrays)


def per_device(
    node_feats, hidden_act, grad_out, relu_mask, edge_tiles, block_cols, weight_one, weight_two
):
    part, tiles, before, last = stream(block_cols, grad_out.T, edge_tiles)
    input_grad_t, first_grad, second_grad = deliver(
        *layers(part, tiles, before, last, weight_two, hidden_act.T, relu_mask.T, weight_one, node_feats.T)
    )
    return (input_grad_t.T, first_grad, second_grad)


def solution(mesh):
    in_specs = (
        P("row", "col"),
        P("row", "col"),
        P("row", "col"),
        P("row", "col"),
        P("row", None, None, None),
        P("row", None),
        P("col", None),
        P("col", None),
    )
    out_specs = (P("row", "col"), P("col", None), P("col", None))
    return jax.shard_map(
        per_device, mesh=mesh, in_specs=in_specs, out_specs=out_specs, check_vma=False
    )
```

```python
import functools
import jax
import jax.numpy as jnp
from jax import lax
from jax.experimental import pallas as pl
from jax.experimental.pallas import tpu as pltpu
from jax.sharding import PartitionSpec as P

RING = 4
ROWS = RING * RING
GROUPS = (6, 4, 2, 2, 2)
ORDER_ONE = (
    "f0", "f1", "o0", "b0", "b1", "o1", "f3", "c0", "f2", "c1", "o2", "f4",
    "e0", "b2", "o3", "b3", "o4", "b4", "e1", "c2", "c3", "c4", "h0", "e2",
    "e3", "h1", "e4", "p0", "h2", "h3", "p1", "h4", "p2", "p3", "p4",
)
ORDER_TWO = (
    "o3", "f0", "f1", "o0", "b0", "b1", "f2", "f3", "f4", "c0", "o2", "b3",
    "o1", "o4", "b2", "e0", "b4", "c3", "c1", "c2", "c4", "e3", "e1", "h0",
    "e2", "e4", "h1", "a0", "p1", "h2", "p0", "h4", "h3", "p4", "p3", "p2",
)
MESH = pl.DeviceIdType.MESH


def tile_terms(vals, tiles, use):
    feats = vals.shape[0]
    side = tiles.shape[2]
    blank = jnp.zeros((feats, side), vals.dtype)
    left = jnp.concatenate(
        [
            jnp.concatenate([vals[:, :side], blank], axis=1),
            jnp.concatenate([blank, vals[:, side:]], axis=1),
        ],
        axis=0,
    )
    for k in range(0, tiles.shape[1], 2):
        right = jnp.concatenate(
            [
                jnp.concatenate([tiles[0, k], tiles[0, k + 1]], axis=1),
                jnp.concatenate([tiles[1, k], tiles[1, k + 1]], axis=1),
            ],
            axis=0,
        )
        term = jnp.dot(left, right, preferred_element_type=jnp.float32)
        for row in range(2):
            for at in range(2):
                use(row, k + at, term[row * feats : (row + 1) * feats, at * side : (at + 1) * side])


def stream_kernel(
    cols_hbm, vals_hbm, tiles_hbm, out_ref, tiles_ref, before_ref, last_ref, acc_ref, cols_ref, vals_ref, sems
):
    rows, per_row, side, _ = tiles_ref.shape
    pairs = rows // 2
    small = [
        pltpu.make_async_copy(cols_hbm, cols_ref, sems.at[pairs]),
        pltpu.make_async_copy(vals_hbm, vals_ref, sems.at[pairs + 1]),
    ]
    for copy in small:
        copy.start()

    def tiles_copy(i):
        at = pl.ds(2 * i, 2)
        return pltpu.make_async_copy(tiles_hbm.at[at], tiles_ref.at[at], sems.at[i])

    for i in range(pairs):
        tiles_copy(i).start()

    def clear(i, carry):
        for at in range(8):
            last_ref[8 * i + at] = rows * per_row
        acc_ref[pl.ds(8 * i, 8)] = jnp.zeros((8,) + acc_ref.shape[1:], acc_ref.dtype)
        return carry

    lax.fori_loop(0, acc_ref.shape[0] // 8, clear, 0)
    for copy in small:
        copy.wait()

    def body(i, carry):
        tiles_copy(i).wait()
        vals = vals_ref[:, pl.ds(pl.multiple_of(2 * side * i, 2 * side), 2 * side)]

        def use(row, k, term):
            target = cols_ref[2 * i + row, k]
            before_ref[2 * i + row, k] = last_ref[target]
            last_ref[target] = (2 * i + row) * per_row + k
            acc_ref[target] += term

        tile_terms(vals, tiles_ref.at[pl.ds(2 * i, 2)], use)
        return carry

    lax.fori_loop(0, pairs, body, 0)
    per_dev = out_ref.shape[3]
    half = out_ref.shape[4]
    for x in range(RING):
        for y in range(RING):
            got = acc_ref[pl.ds((x * RING + y) * per_dev, per_dev)].astype(out_ref.dtype)
            out_ref[0, x, y] = got[:, :half]
            out_ref[1, y, x] = got[:, half:]


def stream(block_cols, vals_t, edge_tiles):
    rows, per_row, side, _ = edge_tiles.shape
    feats = vals_t.shape[0]
    hbm = pl.BlockSpec(memory_space=pltpu.HBM)
    vmem = pl.BlockSpec(memory_space=pltpu.VMEM)
    smem = pl.BlockSpec(memory_space=pltpu.SMEM)
    return pl.pallas_call(
        stream_kernel,
        out_shape=(
            jax.ShapeDtypeStruct((2, RING, RING, rows, feats // 2, side), jnp.bfloat16),
            jax.ShapeDtypeStruct(edge_tiles.shape, edge_tiles.dtype),
            jax.ShapeDtypeStruct(block_cols.shape, jnp.int32),
            jax.ShapeDtypeStruct((rows * ROWS,), jnp.int32),
        ),
        in_specs=[hbm] * 3,
        out_specs=[vmem, vmem, smem, smem],
        scratch_shapes=[
            pltpu.VMEM((rows * ROWS, feats, side), jnp.float32),
            pltpu.SMEM(block_cols.shape, jnp.int32),
            pltpu.VMEM(vals_t.shape, vals_t.dtype),
            pltpu.SemaphoreType.DMA((rows // 2 + 2,)),
        ],
        compiler_params=pltpu.CompilerParams(vmem_limit_bytes=20 << 20),
    )(*(pltpu.with_memory_space_constraint(v, pltpu.HBM) for v in (block_cols, vals_t, edge_tiles)))


def to_pieces(grad, pieces_ref):
    _, tall, wide = pieces_ref.shape
    for p in range(ROWS):
        a, b = p // RING, p % RING
        pieces_ref[p] = grad[a * tall : (a + 1) * tall, b * wide : (b + 1) * wide].astype(pieces_ref.dtype)


def from_pieces(pieces_ref, grad_ref):
    _, tall, wide = pieces_ref.shape
    for p in range(ROWS):
        a, b = p // RING, p % RING
        grad_ref[a * tall : (a + 1) * tall, b * wide : (b + 1) * wide] = pieces_ref[p].astype(grad_ref.dtype)


def layers_kernel(
    part_ref, tiles_ref, before_ref, last_ref, weight2_ref, hidden_ref, mask_ref, weight1_ref, feats_ref,
    input_grad_ref, first_ref, second_ref,
    in1s, mids, in2s, fulls, totals, delta_ref, chain_ref, part2_ref, all_pieces, gather1, gather2,
    feats_all, reduced, wide_ref,
    s1s, r1s, s2s, r2s, szs, rzs, scs, rcs, sg, rg, sb, rb, sxz, rxz, sxc, rxc, sw, rw,
):
    blk, half, side = part_ref.shape[3:]
    feats = 2 * half
    devs = fulls.shape[1]
    per_row = tiles_ref.shape[1]
    none = chain_ref.shape[0] - 1
    f32, bf16 = jnp.float32, jnp.bfloat16
    starts = [sum(GROUPS[:g]) for g in range(len(GROUPS))]

    row, col = lax.axis_index("row"), lax.axis_index("col")
    pos = (row // RING, lax.rem(row, RING))
    z, core = col // 2, lax.rem(col, 2)
    step = (1, -1, 2)
    lanes = [(h, d) for h in range(2) for d in range(2)]

    def wrap(v):
        return lax.rem(v + RING, RING)

    def plane(axis, d):
        x, y = pos
        if axis == 0:
            return (wrap(x + step[d]) * RING + y, col)
        return (x * RING + wrap(y + step[d]), col)

    def along(d):
        return (row, wrap(z + step[d]) * 2 + core)

    sibling = (row, z * 2 + 1 - core)
    peers = [(lax.rem(row + off, ROWS), col) for off in range(1, ROWS)]

    barrier = pltpu.get_barrier_semaphore()
    met = peers + [along(0), along(1), along(2), sibling]
    for dev in met:
        pl.semaphore_signal(barrier, inc=1, device_id=dev, device_id_type=MESH)
    pl.semaphore_wait(barrier, len(met))

    started = []

    def send(src, dst, send_sem, recv_sem, dev):
        copy = pltpu.make_async_remote_copy(
            src_ref=src, dst_ref=dst, send_sem=send_sem, recv_sem=recv_sem,
            device_id=dev, device_id_type=MESH,
        )
        copy.start()
        started.append(copy)
        return copy

    def blocks(g, lo=None):
        if lo is None:
            return pl.ds(starts[g], GROUPS[g])
        return pl.ds(starts[g] + lo * (GROUPS[g] // 2), GROUPS[g] // 2)

    def slots(g):
        return pl.ds(starts[g] // 2, GROUPS[g] // 2)

    chain_ref[none] = jnp.zeros((feats, side), f32)
    totals[...] = jnp.zeros_like(totals)

    feats_hop, feats_hand = {}, {}

    def gather_feats():
        feats_all[col] = feats_ref[...]
        for d in (2, 0, 1):
            feats_hop[d] = send(feats_ref, feats_all.at[col], sxz.at[d], rxz.at[d], along(d))
        feats_hand[3] = send(feats_ref, feats_all.at[col], sxc.at[3], rxc.at[3], sibling)

    def pass_feats():
        for d in range(3):
            feats_hop[d].wait_recv()
            spot = feats_all.at[wrap(z - step[d]) * 2 + core]
            feats_hand[d] = send(spot, spot, sxc.at[d], rxc.at[d], sibling)

    def chain_group(g):
        def body(i, carry):
            vals = delta_ref[:, pl.ds(pl.multiple_of(2 * side * i, 2 * side), 2 * side)]

            def use(row, k, term):
                chain_ref[(2 * i + row) * per_row + k] = term + chain_ref[before_ref[2 * i + row, k]]

            tile_terms(vals, tiles_ref.at[pl.ds(2 * i, 2)], use)
            return carry

        lax.fori_loop(starts[g] // 2, (starts[g] + GROUPS[g]) // 2, body, 0)

    def chain_ends():
        def body(dev, carry):
            x, y = dev // RING, lax.rem(dev, RING)
            for b in range(blk):
                got = chain_ref[last_ref[dev * blk + b]].astype(bf16)
                part2_ref[0, x, y, b] = got[:half]
                part2_ref[1, y, x, b] = got[half:]
            return carry

        lax.fori_loop(0, ROWS, body, 0)

    out, back = {}, {}

    def send_pieces(n, src):
        for i, dev in enumerate(peers):
            out[n, i] = send(src.at[dev[0]], gather1.at[n, i], sg.at[n, i], rg.at[n, i], dev)

    def piece_sum(n, src):
        total = src[row].astype(f32)
        for i in range(len(peers)):
            out[n, i].wait_recv()
            total += gather1[n, i].astype(f32)
        return total

    def add_pieces(n, src):
        total = piece_sum(n, src)
        gather2[n, row] = total.astype(bf16)
        for i, dev in enumerate(peers):
            spot = gather2.at[n, row]
            back[n, i] = send(spot, spot, sb.at[n, i], rb.at[n, i], dev)

    def take_pieces(n, dst):
        for i in range(len(peers)):
            back[n, i].wait_recv()
        from_pieces(gather2.at[n], dst)

    home = pos[1] == z

    def wide_copy(off, c):
        dev = (lax.rem(row + off, ROWS), pos[1] * 2 + c)
        return pltpu.make_async_remote_copy(
            src_ref=reduced, dst_ref=wide_ref.at[col, pos[0]], send_sem=sw.at[off, c], recv_sem=rw.at[col, pos[0]],
            device_id=dev, device_id_type=MESH,
        )

    def others(act):
        for c in range(2):
            for off in range(1, ROWS):
                act(wide_copy(off, c))

            @pl.when(pos[1] * 2 + c != col)
            def _():
                act(wide_copy(0, c))

    def send_wide():
        reduced[...] = piece_sum(1, all_pieces.at[1]).astype(bf16)
        others(lambda copy: copy.start())

        @pl.when(home)
        def _():
            wide_ref[col, pos[0]] = reduced[...]

    def take_wide():
        def body(i, carry):
            c, a = i // RING, lax.rem(i, RING)

            @pl.when(jnp.logical_not(home & (c == col) & (a == pos[0])))
            def _():
                pltpu.make_async_remote_copy(
                    src_ref=reduced, dst_ref=wide_ref.at[c, a], send_sem=sw.at[0, 0], recv_sem=rw.at[c, a],
                    device_id=sibling, device_id_type=MESH,
                ).wait_recv()

            return carry

        lax.fori_loop(0, devs * RING, body, 0)
        wide = wide_ref[...].reshape(devs * feats, side).astype(f32).T
        first_ref[...] = jnp.where(core == 0, wide[:feats], wide[feats:])
        others(lambda copy: copy.wait_send())

    def layer_stages(n, part_ref, weight_ref, acts_ref, mask_ref, value_ref, pieces_ref):
        in1, mid, in2, full, total_ref = (ref.at[n] for ref in (in1s, mids, in2s, fulls, totals))
        s1, r1, s2, r2, sz, rz, sc, rc = (ref.at[n] for ref in (s1s, r1s, s2s, r2s, szs, rzs, scs, rcs))
        far, near, both, direct, hop, hand = ({} for _ in range(6))
        summed = []

        def send_far(g):
            for h, d in lanes:
                far[h, d, g] = send(
                    part_ref.at[h, wrap(pos[h] + 2), :, blocks(g, d)],
                    in1.at[h, d, 0, :, slots(g)], s1.at[h, d, 0, g], r1.at[h, d, 0, g], plane(h, d))

        def send_near(g):
            for h, d in lanes:
                near[h, d, g] = send(
                    part_ref.at[h, wrap(pos[h] + step[d]), :, blocks(g, 1 - d)],
                    in1.at[h, d, 1, :, slots(g)], s1.at[h, d, 1, g], r1.at[h, d, 1, g], plane(h, d))

        def send_both(g):
            for h, d in lanes:
                far[h, d, g].wait_recv()
                got = in1.at[h, d, 0, :, slots(g)]
                mine = part_ref.at[h, wrap(pos[h] + step[d]), :, blocks(g, d)]

                def add(q, carry):
                    got[q] = (got[q].astype(f32) + mine[q].astype(f32)).astype(bf16)
                    return carry

                lax.fori_loop(0, RING, add, 0)
                both[h, d, g] = send(
                    got, in1.at[h, d, 2, :, slots(g)], s1.at[h, d, 2, g], r1.at[h, d, 2, g], plane(h, d))

        def second_ring(g):
            for h in range(2):
                other = pos[1 - h]
                for lo in range(2):
                    both[h, lo, g].wait_recv()
                    near[h, 1 - lo, g].wait_recv()

                def add(q, carry):
                    for lo in range(2):
                        total = part_ref[h, pos[h], q, blocks(g, lo)].astype(f32)
                        total += in1[h, lo, 2, q, slots(g)].astype(f32)
                        total += in1[h, 1 - lo, 1, q, slots(g)].astype(f32)
                        mid[h, q, blocks(g, lo)] = total.astype(bf16)
                    return carry

                lax.fori_loop(0, RING, add, 0)
                for d in (2, 0, 1):
                    direct[h, d, g] = send(
                        mid.at[h, wrap(other + step[d]), blocks(g)],
                        in2.at[h, d, blocks(g)], s2.at[h, d, g], r2.at[h, d, g], plane(1 - h, d))

        def give(c, g, key):
            spot = full.at[c, :, blocks(g)]
            hand[key, g] = send(spot, spot, sc.at[key, g], rc.at[key, g], sibling)

        def finish(g):
            for h in range(2):
                other = pos[1 - h]
                total = mid[h, other, blocks(g)].astype(f32)
                for d in range(3):
                    direct[h, d, g].wait_recv()
                    total += in2[h, d, blocks(g)].astype(f32)
                full[col, h, blocks(g)] = total.astype(bf16)
            for d in (2, 0, 1):
                spot = full.at[col, :, blocks(g)]
                hop[d, g] = send(spot, spot, sz.at[d, g], rz.at[d, g], along(d))
            give(col, g, 3)
            if n == 1:
                def pair(i, carry):
                    b, at = pair_at(g, i)
                    left = jnp.concatenate(
                        [
                            jnp.concatenate([full[col, h, b + k] for h in range(2)], axis=0)
                            for k in range(2)
                        ],
                        axis=1,
                    )
                    add_grad(left, feats_all[:, :, at].reshape(devs * feats, 2 * side))
                    return carry

                lax.fori_loop(0, GROUPS[g] // 2, pair, 0)
                count_grad(g)

        def pass_on(g):
            for d in (0, 1, 2):
                hop[d, g].wait_recv()
                give(wrap(z - step[d]) * 2 + core, g, d)

        def pair_at(g, i):
            b = starts[g] + 2 * i
            return b, pl.ds(pl.multiple_of(b * side, 2 * side), 2 * side)

        def add_grad(left, right):
            total_ref[...] += lax.dot_general(
                left, right, (((1,), (1,)), ((), ())), preferred_element_type=f32
            )

        def count_grad(g):
            summed.append(g)
            if len(summed) == len(GROUPS):
                to_pieces(total_ref, pieces_ref)
                send_pieces(n, pieces_ref)

        def products(g):
            for key in range(4):
                hand[key, g].wait_recv()

            def pair(i, carry):
                b, at = pair_at(g, i)
                right = jnp.concatenate(
                    [
                        jnp.concatenate([full[c, h, b + k] for c in range(devs) for h in range(2)], axis=0)
                        for k in range(2)
                    ],
                    axis=1,
                )
                value = jnp.dot(weight_ref[...], right, preferred_element_type=f32)
                if mask_ref is not None:
                    value = value * mask_ref[:, at].astype(f32)
                value_ref[:, at] = value.astype(bf16)
                if n == 0:
                    add_grad(acts_ref[:, at], right)
                return carry

            lax.fori_loop(0, GROUPS[g] // 2, pair, 0)
            if n == 0:
                count_grad(g)
                chain_group(g)

        return dict(
            f=send_far, o=send_near, b=send_both, c=second_ring, e=finish, h=pass_on, p=products,
        )

    stages = layer_stages(0, part_ref, weight2_ref, hidden_ref, mask_ref, delta_ref, all_pieces.at[0])
    for at, word in enumerate(ORDER_ONE):
        stages[word[0]](int(word[1:]))
        if at == 2:
            gather_feats()
        if at == len(ORDER_ONE) - 6:
            pass_feats()
    chain_ends()
    stages = layer_stages(1, part2_ref, weight1_ref, feats_ref, None, input_grad_ref, all_pieces.at[1])
    for at, word in enumerate(ORDER_TWO):
        if word == "a0":
            send_wide()
        else:
            stages[word[0]](int(word[1:]))
        if at == len(ORDER_TWO) // 4:
            add_pieces(0, all_pieces.at[0])
            for key in range(4):
                feats_hand[key].wait_recv()
        if at == len(ORDER_TWO) // 2:
            take_pieces(0, second_ref)
    take_wide()
    for copy in started:
        copy.wait_send()


def layers(part, tiles, before, last, weight_two, hidden_t, mask_t, weight_one, feats_t):
    blk, half, side = part.shape[3:]
    feats, rows = feats_t.shape
    devs = weight_one.shape[1] // feats
    groups = len(GROUPS)
    vmem = pl.BlockSpec(memory_space=pltpu.VMEM)
    smem = pl.BlockSpec(memory_space=pltpu.SMEM)
    dma = pltpu.SemaphoreType.DMA
    bf16, f32 = jnp.bfloat16, jnp.float32
    grad = (feats, devs * feats)
    pieces = (ROWS, feats // RING, devs * feats // RING)
    scratch = [
        pltpu.VMEM((2, 2, 2, 3, RING, blk // 2, half, side), bf16),
        pltpu.VMEM((2, 2, RING, blk, half, side), bf16),
        pltpu.VMEM((2, 2, 3, blk, half, side), bf16),
        pltpu.VMEM((2, devs, 2, blk, half, side), bf16),
        pltpu.VMEM((2,) + grad, f32),
        pltpu.VMEM((feats, rows), bf16),
        pltpu.VMEM((before.size + 1, feats, side), f32),
        pltpu.VMEM(part.shape, bf16),
        pltpu.VMEM((2,) + pieces, bf16),
        pltpu.VMEM((2, ROWS - 1) + pieces[1:], bf16),
        pltpu.VMEM((2,) + pieces, bf16),
        pltpu.VMEM((devs, feats, rows), bf16),
        pltpu.VMEM(pieces[1:], bf16),
        pltpu.VMEM((devs, RING) + pieces[1:], bf16),
    ]
    for shape in ((2, 2, 3), (2, 3), (3,), (4,)):
        scratch += [dma((2,) + shape + (groups,)), dma((2,) + shape + (groups,))]
    scratch += [dma((2, ROWS - 1))] * 4 + [dma((3,))] * 2 + [dma((4,))] * 2
    scratch += [dma((ROWS, 2)), dma((devs, RING))]
    return pl.pallas_call(
        layers_kernel,
        out_shape=(
            jax.ShapeDtypeStruct((feats, rows), bf16),
            jax.ShapeDtypeStruct(grad, f32),
            jax.ShapeDtypeStruct(grad, f32),
        ),
        in_specs=[vmem, vmem, smem, smem] + [vmem] * 5,
        out_specs=[vmem] * 3,
        scratch_shapes=scratch,
        compiler_params=pltpu.CompilerParams(
            collective_id=0, has_side_effects=True, vmem_limit_bytes=36 << 20
        ),
    )(part, tiles, before, last, weight_two, hidden_t, mask_t, weight_one, feats_t)


def per_device(
    node_feats, hidden_act, grad_out, relu_mask, edge_tiles, block_cols, weight_one, weight_two
):
    part, tiles, before, last = stream(block_cols, grad_out.T, edge_tiles)
    input_grad_t, first_grad, second_grad = layers(
        part, tiles, before, last, weight_two, hidden_act.T, relu_mask.T, weight_one, node_feats.T
    )
    return (input_grad_t.T, first_grad, second_grad)


def solution(mesh):
    in_specs = (
        P("row", "col"),
        P("row", "col"),
        P("row", "col"),
        P("row", "col"),
        P("row", None, None, None),
        P("row", None),
        P("col", None),
        P("col", None),
    )
    out_specs = (P("row", "col"), P("col", None), P("col", None))
    return jax.shard_map(
        per_device, mesh=mesh, in_specs=in_specs, out_specs=out_specs, check_vma=False
    )
```

```python
import functools
import jax
import jax.numpy as jnp
from jax import lax
from jax.experimental import pallas as pl
from jax.experimental.pallas import tpu as pltpu
from jax.sharding import PartitionSpec as P

RING = 4
ROWS = RING * RING
GROUPS = (6, 4, 2, 2, 2)
ORDER_ONE = (
    "f0", "f1", "o0", "b0", "b1", "o1", "f3", "c0", "f2", "c1", "o2", "f4",
    "e0", "b2", "o3", "b3", "o4", "b4", "e1", "c2", "c3", "c4", "h0", "e2",
    "e3", "h1", "e4", "p0", "h2", "h3", "p1", "h4", "p2", "p3", "p4",
)
ORDER_TWO = (
    "o3", "f0", "f1", "o0", "b0", "b1", "f2", "f3", "f4", "c0", "o2", "b3",
    "o1", "o4", "b2", "e0", "b4", "c3", "c1", "c2", "c4", "e3", "e1", "h0",
    "e2", "e4", "h1", "a0", "p1", "h2", "p0", "h4", "h3", "p4", "p3", "p2",
)
SENDS = 48
MESH = pl.DeviceIdType.MESH


def tile_terms(vals, tiles, use):
    feats = vals.shape[0]
    side = tiles.shape[2]
    blank = jnp.zeros((feats, side), vals.dtype)
    left = jnp.concatenate(
        [
            jnp.concatenate([vals[:, :side], blank], axis=1),
            jnp.concatenate([blank, vals[:, side:]], axis=1),
        ],
        axis=0,
    )
    for k in range(0, tiles.shape[1], 2):
        right = jnp.concatenate(
            [
                jnp.concatenate([tiles[0, k], tiles[0, k + 1]], axis=1),
                jnp.concatenate([tiles[1, k], tiles[1, k + 1]], axis=1),
            ],
            axis=0,
        )
        term = jnp.dot(left, right, preferred_element_type=jnp.float32)
        for row in range(2):
            for at in range(2):
                use(row, k + at, term[row * feats : (row + 1) * feats, at * side : (at + 1) * side])


def stream_kernel(
    cols_hbm, vals_hbm, tiles_hbm, out_ref, tiles_ref, before_ref, last_ref, acc_ref, cols_ref, vals_ref, sems
):
    rows, per_row, side, _ = tiles_ref.shape
    pairs = rows // 2
    small = [
        pltpu.make_async_copy(cols_hbm, cols_ref, sems.at[pairs]),
        pltpu.make_async_copy(vals_hbm, vals_ref, sems.at[pairs + 1]),
    ]
    for copy in small:
        copy.start()

    def tiles_copy(i):
        at = pl.ds(2 * i, 2)
        return pltpu.make_async_copy(tiles_hbm.at[at], tiles_ref.at[at], sems.at[i])

    for i in range(pairs):
        tiles_copy(i).start()

    def clear(i, carry):
        for at in range(8):
            last_ref[8 * i + at] = rows * per_row
        acc_ref[pl.ds(8 * i, 8)] = jnp.zeros((8,) + acc_ref.shape[1:], acc_ref.dtype)
        return carry

    lax.fori_loop(0, acc_ref.shape[0] // 8, clear, 0)
    for copy in small:
        copy.wait()

    def body(i, carry):
        tiles_copy(i).wait()
        vals = vals_ref[:, pl.ds(pl.multiple_of(2 * side * i, 2 * side), 2 * side)]

        def use(row, k, term):
            target = cols_ref[2 * i + row, k]
            before_ref[2 * i + row, k] = last_ref[target]
            last_ref[target] = (2 * i + row) * per_row + k
            acc_ref[target] += term

        tile_terms(vals, tiles_ref.at[pl.ds(2 * i, 2)], use)
        return carry

    lax.fori_loop(0, pairs, body, 0)
    per_dev = out_ref.shape[3]
    half = out_ref.shape[4]
    for x in range(RING):
        for y in range(RING):
            got = acc_ref[pl.ds((x * RING + y) * per_dev, per_dev)].astype(out_ref.dtype)
            out_ref[0, x, y] = got[:, :half]
            out_ref[1, y, x] = got[:, half:]


def stream(block_cols, vals_t, edge_tiles):
    rows, per_row, side, _ = edge_tiles.shape
    feats = vals_t.shape[0]
    hbm = pl.BlockSpec(memory_space=pltpu.HBM)
    vmem = pl.BlockSpec(memory_space=pltpu.VMEM)
    smem = pl.BlockSpec(memory_space=pltpu.SMEM)
    return pl.pallas_call(
        stream_kernel,
        out_shape=(
            jax.ShapeDtypeStruct((2, RING, RING, rows, feats // 2, side), jnp.bfloat16),
            jax.ShapeDtypeStruct(edge_tiles.shape, edge_tiles.dtype),
            jax.ShapeDtypeStruct(block_cols.shape, jnp.int32),
            jax.ShapeDtypeStruct((rows * ROWS,), jnp.int32),
        ),
        in_specs=[hbm] * 3,
        out_specs=[vmem, vmem, smem, smem],
        scratch_shapes=[
            pltpu.VMEM((rows * ROWS, feats, side), jnp.float32),
            pltpu.SMEM(block_cols.shape, jnp.int32),
            pltpu.VMEM(vals_t.shape, vals_t.dtype),
            pltpu.SemaphoreType.DMA((rows // 2 + 2,)),
        ],
        compiler_params=pltpu.CompilerParams(vmem_limit_bytes=20 << 20),
    )(*(pltpu.with_memory_space_constraint(v, pltpu.HBM) for v in (block_cols, vals_t, edge_tiles)))


def to_pieces(grad, pieces_ref):
    _, tall, wide = pieces_ref.shape
    for p in range(ROWS):
        a, b = p // RING, p % RING
        pieces_ref[p] = grad[a * tall : (a + 1) * tall, b * wide : (b + 1) * wide].astype(pieces_ref.dtype)


def from_pieces(pieces_ref, grad_ref):
    _, tall, wide = pieces_ref.shape
    for p in range(ROWS):
        a, b = p // RING, p % RING
        grad_ref[a * tall : (a + 1) * tall, b * wide : (b + 1) * wide] = pieces_ref[p].astype(grad_ref.dtype)


def layers_kernel(
    part_ref, tiles_ref, before_ref, last_ref, weight2_ref, hidden_ref, mask_ref, weight1_ref, feats_ref,
    input_grad_ref, first_ref, second_ref,
    in1s, mids, in2s, fulls, totals, delta_ref, chain_ref, part2_ref, all_pieces, gather1, gather2,
    feats_all, reduced, wide_ref,
    r1s, r2s, rzs, rcs, rg, rb, rxz, rxc, sw, rw, sent,
):
    blk, half, side = part_ref.shape[3:]
    feats = 2 * half
    devs = fulls.shape[1]
    per_row = tiles_ref.shape[1]
    none = chain_ref.shape[0] - 1
    f32, bf16 = jnp.float32, jnp.bfloat16
    starts = [sum(GROUPS[:g]) for g in range(len(GROUPS))]

    row, col = lax.axis_index("row"), lax.axis_index("col")
    pos = (row // RING, lax.rem(row, RING))
    z, core = col // 2, lax.rem(col, 2)
    step = (1, -1, 2)
    lanes = [(h, d) for h in range(2) for d in range(2)]

    def wrap(v):
        return lax.rem(v + RING, RING)

    def plane(axis, d):
        x, y = pos
        if axis == 0:
            return (wrap(x + step[d]) * RING + y, col)
        return (x * RING + wrap(y + step[d]), col)

    def along(d):
        return (row, wrap(z + step[d]) * 2 + core)

    sibling = (row, z * 2 + 1 - core)
    peers = [(lax.rem(row + off, ROWS), col) for off in range(1, ROWS)]

    barrier = pltpu.get_barrier_semaphore()
    met = peers + [along(0), along(1), along(2), sibling]
    for dev in met:
        pl.semaphore_signal(barrier, inc=1, device_id=dev, device_id_type=MESH)
    pl.semaphore_wait(barrier, len(met))

    started = []

    def send(src, dst, recv_sem, dev):
        slot = len(started) % SENDS
        if len(started) >= SENDS:
            started[-SENDS].wait_send()
        copy = pltpu.make_async_remote_copy(
            src_ref=src, dst_ref=dst, send_sem=sent.at[slot], recv_sem=recv_sem,
            device_id=dev, device_id_type=MESH,
        )
        copy.start()
        started.append(copy)
        return copy

    def arrived(ref, recv_sem):
        pltpu.make_async_remote_copy(
            src_ref=ref, dst_ref=ref, send_sem=sent.at[0], recv_sem=recv_sem,
            device_id=sibling, device_id_type=MESH,
        ).wait_recv()

    def blocks(g, lo=None):
        if lo is None:
            return pl.ds(starts[g], GROUPS[g])
        return pl.ds(starts[g] + lo * (GROUPS[g] // 2), GROUPS[g] // 2)

    def slots(g):
        return pl.ds(starts[g] // 2, GROUPS[g] // 2)

    chain_ref[none] = jnp.zeros((feats, side), f32)
    totals[...] = jnp.zeros_like(totals)

    feats_hop, feats_hand = {}, {}

    def gather_feats():
        feats_all[col] = feats_ref[...]
        for d in (2, 0, 1):
            feats_hop[d] = send(feats_ref, feats_all.at[col], rxz.at[d], along(d))
        feats_hand[3] = send(feats_ref, feats_all.at[col], rxc.at[3], sibling)

    def pass_feats():
        for d in range(3):
            feats_hop[d].wait_recv()
            spot = feats_all.at[wrap(z - step[d]) * 2 + core]
            feats_hand[d] = send(spot, spot, rxc.at[d], sibling)

    def chain_group(g):
        def body(i, carry):
            vals = delta_ref[:, pl.ds(pl.multiple_of(2 * side * i, 2 * side), 2 * side)]

            def use(row, k, term):
                chain_ref[(2 * i + row) * per_row + k] = term + chain_ref[before_ref[2 * i + row, k]]

            tile_terms(vals, tiles_ref.at[pl.ds(2 * i, 2)], use)
            return carry

        lax.fori_loop(starts[g] // 2, (starts[g] + GROUPS[g]) // 2, body, 0)

    def chain_ends():
        def body(dev, carry):
            x, y = dev // RING, lax.rem(dev, RING)
            for b in range(blk):
                got = chain_ref[last_ref[dev * blk + b]].astype(bf16)
                part2_ref[0, x, y, b] = got[:half]
                part2_ref[1, y, x, b] = got[half:]
            return carry

        lax.fori_loop(0, ROWS, body, 0)

    out, back = {}, {}

    def send_pieces(n, src):
        for i, dev in enumerate(peers):
            out[n, i] = send(src.at[dev[0]], gather1.at[n, i], rg.at[n], dev)

    def piece_sum(n, src):
        arrived(gather1.at[n], rg.at[n])
        total = src[row].astype(f32)
        for i in range(len(peers)):
            total += gather1[n, i].astype(f32)
        return total

    def add_pieces(n, src):
        total = piece_sum(n, src)
        gather2[n, row] = total.astype(bf16)
        for i, dev in enumerate(peers):
            spot = gather2.at[n, row]
            back[n, i] = send(spot, spot, rb.at[n, i], dev)

    def take_pieces(n, dst):
        for i in range(len(peers)):
            back[n, i].wait_recv()
        from_pieces(gather2.at[n], dst)

    home = pos[1] == z

    def wide_copy(off, c):
        dev = (lax.rem(row + off, ROWS), pos[1] * 2 + c)
        return pltpu.make_async_remote_copy(
            src_ref=reduced, dst_ref=wide_ref.at[col, pos[0]], send_sem=sw.at[off, c], recv_sem=rw.at[col, pos[0]],
            device_id=dev, device_id_type=MESH,
        )

    def others(act):
        for c in range(2):
            for off in range(1, ROWS):
                act(wide_copy(off, c))

            @pl.when(pos[1] * 2 + c != col)
            def _():
                act(wide_copy(0, c))

    def send_wide():
        reduced[...] = piece_sum(1, all_pieces.at[1]).astype(bf16)
        others(lambda copy: copy.start())

        @pl.when(home)
        def _():
            wide_ref[col, pos[0]] = reduced[...]

    def take_wide():
        def body(i, carry):
            c, a = i // RING, lax.rem(i, RING)

            @pl.when(jnp.logical_not(home & (c == col) & (a == pos[0])))
            def _():
                pltpu.make_async_remote_copy(
                    src_ref=reduced, dst_ref=wide_ref.at[c, a], send_sem=sw.at[0, 0], recv_sem=rw.at[c, a],
                    device_id=sibling, device_id_type=MESH,
                ).wait_recv()

            return carry

        lax.fori_loop(0, devs * RING, body, 0)
        wide = wide_ref[...].reshape(devs * feats, side).astype(f32).T
        first_ref[...] = jnp.where(core == 0, wide[:feats], wide[feats:])
        others(lambda copy: copy.wait_send())

    def layer_stages(n, part_ref, weight_ref, acts_ref, mask_ref, value_ref, pieces_ref):
        in1, mid, in2, full, total_ref = (ref.at[n] for ref in (in1s, mids, in2s, fulls, totals))
        r1, r2, rz, rc = (ref.at[n] for ref in (r1s, r2s, rzs, rcs))
        far, near, both, direct, hop, hand = ({} for _ in range(6))
        summed = []

        def send_far(g):
            for h, d in lanes:
                far[h, d, g] = send(
                    part_ref.at[h, wrap(pos[h] + 2), :, blocks(g, d)],
                    in1.at[h, d, 0, :, slots(g)], r1.at[h, d, g], plane(h, d))

        def send_near(g):
            for h, d in lanes:
                near[h, d, g] = send(
                    part_ref.at[h, wrap(pos[h] + step[d]), :, blocks(g, 1 - d)],
                    in1.at[h, d, 1, :, slots(g)], r1.at[h, 2, g], plane(h, d))

        def send_both(g):
            for h, d in lanes:
                far[h, d, g].wait_recv()
                got = in1.at[h, d, 0, :, slots(g)]
                mine = part_ref.at[h, wrap(pos[h] + step[d]), :, blocks(g, d)]

                def add(q, carry):
                    got[q] = (got[q].astype(f32) + mine[q].astype(f32)).astype(bf16)
                    return carry

                lax.fori_loop(0, RING, add, 0)
                both[h, d, g] = send(
                    got, in1.at[h, d, 2, :, slots(g)], r1.at[h, 2, g], plane(h, d))

        def second_ring(g):
            for h in range(2):
                other = pos[1 - h]
                arrived(in1.at[h, :, pl.ds(1, 2), :, slots(g)], r1.at[h, 2, g])

                def add(q, carry):
                    for lo in range(2):
                        total = part_ref[h, pos[h], q, blocks(g, lo)].astype(f32)
                        total += in1[h, lo, 2, q, slots(g)].astype(f32)
                        total += in1[h, 1 - lo, 1, q, slots(g)].astype(f32)
                        mid[h, q, blocks(g, lo)] = total.astype(bf16)
                    return carry

                lax.fori_loop(0, RING, add, 0)
                for d in (2, 0, 1):
                    direct[h, d, g] = send(
                        mid.at[h, wrap(other + step[d]), blocks(g)],
                        in2.at[h, d, blocks(g)], r2.at[h, g], plane(1 - h, d))

        def give(c, g, key):
            spot = full.at[c, :, blocks(g)]
            hand[key, g] = send(spot, spot, rc.at[key, g], sibling)

        def finish(g):
            for h in range(2):
                other = pos[1 - h]
                total = mid[h, other, blocks(g)].astype(f32)
                arrived(in2.at[h, :, blocks(g)], r2.at[h, g])
                for d in range(3):
                    total += in2[h, d, blocks(g)].astype(f32)
                full[col, h, blocks(g)] = total.astype(bf16)
            for d in (2, 0, 1):
                spot = full.at[col, :, blocks(g)]
                hop[d, g] = send(spot, spot, rz.at[d, g], along(d))
            give(col, g, 3)
            if n == 1:
                def pair(i, carry):
                    b, at = pair_at(g, i)
                    left = jnp.concatenate(
                        [
                            jnp.concatenate([full[col, h, b + k] for h in range(2)], axis=0)
                            for k in range(2)
                        ],
                        axis=1,
                    )
                    add_grad(left, feats_all[:, :, at].reshape(devs * feats, 2 * side))
                    return carry

                lax.fori_loop(0, GROUPS[g] // 2, pair, 0)
                count_grad(g)

        def pass_on(g):
            for d in (0, 1, 2):
                hop[d, g].wait_recv()
                give(wrap(z - step[d]) * 2 + core, g, d)

        def pair_at(g, i):
            b = starts[g] + 2 * i
            return b, pl.ds(pl.multiple_of(b * side, 2 * side), 2 * side)

        def add_grad(left, right):
            total_ref[...] += lax.dot_general(
                left, right, (((1,), (1,)), ((), ())), preferred_element_type=f32
            )

        def count_grad(g):
            summed.append(g)
            if len(summed) == len(GROUPS):
                to_pieces(total_ref, pieces_ref)
                send_pieces(n, pieces_ref)

        def products(g):
            for key in range(4):
                hand[key, g].wait_recv()

            def pair(i, carry):
                b, at = pair_at(g, i)
                right = jnp.concatenate(
                    [
                        jnp.concatenate([full[c, h, b + k] for c in range(devs) for h in range(2)], axis=0)
                        for k in range(2)
                    ],
                    axis=1,
                )
                value = jnp.dot(weight_ref[...], right, preferred_element_type=f32)
                if mask_ref is not None:
                    value = value * mask_ref[:, at].astype(f32)
                value_ref[:, at] = value.astype(bf16)
                if n == 0:
                    add_grad(acts_ref[:, at], right)
                return carry

            lax.fori_loop(0, GROUPS[g] // 2, pair, 0)
            if n == 0:
                count_grad(g)
                chain_group(g)

        return dict(
            f=send_far, o=send_near, b=send_both, c=second_ring, e=finish, h=pass_on, p=products,
        )

    stages = layer_stages(0, part_ref, weight2_ref, hidden_ref, mask_ref, delta_ref, all_pieces.at[0])
    for at, word in enumerate(ORDER_ONE):
        stages[word[0]](int(word[1:]))
        if at == 2:
            gather_feats()
        if at == len(ORDER_ONE) - 6:
            pass_feats()
    chain_ends()
    stages = layer_stages(1, part2_ref, weight1_ref, feats_ref, None, input_grad_ref, all_pieces.at[1])
    for at, word in enumerate(ORDER_TWO):
        if word == "a0":
            send_wide()
        else:
            stages[word[0]](int(word[1:]))
        if at == len(ORDER_TWO) // 4:
            add_pieces(0, all_pieces.at[0])
            for key in range(4):
                feats_hand[key].wait_recv()
        if at == len(ORDER_TWO) // 2:
            take_pieces(0, second_ref)
    take_wide()
    for copy in started[-SENDS:]:
        copy.wait_send()


def layers(part, tiles, before, last, weight_two, hidden_t, mask_t, weight_one, feats_t):
    blk, half, side = part.shape[3:]
    feats, rows = feats_t.shape
    devs = weight_one.shape[1] // feats
    groups = len(GROUPS)
    vmem = pl.BlockSpec(memory_space=pltpu.VMEM)
    smem = pl.BlockSpec(memory_space=pltpu.SMEM)
    dma = pltpu.SemaphoreType.DMA
    bf16, f32 = jnp.bfloat16, jnp.float32
    grad = (feats, devs * feats)
    pieces = (ROWS, feats // RING, devs * feats // RING)
    scratch = [
        pltpu.VMEM((2, 2, 2, 3, RING, blk // 2, half, side), bf16),
        pltpu.VMEM((2, 2, RING, blk, half, side), bf16),
        pltpu.VMEM((2, 2, 3, blk, half, side), bf16),
        pltpu.VMEM((2, devs, 2, blk, half, side), bf16),
        pltpu.VMEM((2,) + grad, f32),
        pltpu.VMEM((feats, rows), bf16),
        pltpu.VMEM((before.size + 1, feats, side), f32),
        pltpu.VMEM(part.shape, bf16),
        pltpu.VMEM((2,) + pieces, bf16),
        pltpu.VMEM((2, ROWS - 1) + pieces[1:], bf16),
        pltpu.VMEM((2,) + pieces, bf16),
        pltpu.VMEM((devs, feats, rows), bf16),
        pltpu.VMEM(pieces[1:], bf16),
        pltpu.VMEM((devs, RING) + pieces[1:], bf16),
    ]
    for shape in ((2, 3), (2,), (3,), (4,)):
        scratch += [dma((2,) + shape + (groups,))]
    scratch += [dma((2,)), dma((2, ROWS - 1)), dma((3,)), dma((4,))]
    scratch += [dma((ROWS, 2)), dma((devs, RING)), dma((SENDS,))]
    return pl.pallas_call(
        layers_kernel,
        out_shape=(
            jax.ShapeDtypeStruct((feats, rows), bf16),
            jax.ShapeDtypeStruct(grad, f32),
            jax.ShapeDtypeStruct(grad, f32),
        ),
        in_specs=[vmem, vmem, smem, smem] + [vmem] * 5,
        out_specs=[vmem] * 3,
        scratch_shapes=scratch,
        compiler_params=pltpu.CompilerParams(
            collective_id=0, has_side_effects=True, vmem_limit_bytes=36 << 20
        ),
    )(part, tiles, before, last, weight_two, hidden_t, mask_t, weight_one, feats_t)


def per_device(
    node_feats, hidden_act, grad_out, relu_mask, edge_tiles, block_cols, weight_one, weight_two
):
    part, tiles, before, last = stream(block_cols, grad_out.T, edge_tiles)
    input_grad_t, first_grad, second_grad = layers(
        part, tiles, before, last, weight_two, hidden_act.T, relu_mask.T, weight_one, node_feats.T
    )
    return (input_grad_t.T, first_grad, second_grad)


def solution(mesh):
    in_specs = (
        P("row", "col"),
        P("row", "col"),
        P("row", "col"),
        P("row", "col"),
        P("row", None, None, None),
        P("row", None),
        P("col", None),
        P("col", None),
    )
    out_specs = (P("row", "col"), P("col", None), P("col", None))
    return jax.shard_map(
        per_device, mesh=mesh, in_specs=in_specs, out_specs=out_specs, check_vma=False
    )
```

```python
import functools
import jax
import jax.numpy as jnp
from jax import lax
from jax.experimental import pallas as pl
from jax.experimental.pallas import tpu as pltpu
from jax.sharding import PartitionSpec as P

RING = 4
ROWS = RING * RING
GROUPS = (6, 4, 2, 2, 2)
ORDER_ONE = (
    "f0", "f1", "o0", "b0", "b1", "o1", "f3", "c0", "f2", "c1", "o2", "f4",
    "e0", "b2", "o3", "b3", "o4", "b4", "e1", "c2", "c3", "c4", "h0", "e2",
    "e3", "h1", "e4", "p0", "h2", "h3", "p1", "h4", "p2", "p3", "p4",
)
ORDER_TWO = (
    "o3", "f0", "f1", "o0", "b0", "b1", "f2", "f3", "f4", "c0", "o2", "b3",
    "o1", "o4", "b2", "e0", "b4", "c3", "c1", "c2", "c4", "e3", "e1", "h0",
    "e2", "e4", "h1", "a0", "p1", "h2", "p0", "h4", "h3", "p4", "p3", "p2",
)
SENDS = 32
MESH = pl.DeviceIdType.MESH


def tile_terms(vals, tiles, use):
    feats = vals.shape[0]
    side = tiles.shape[2]
    blank = jnp.zeros((feats, side), vals.dtype)
    left = jnp.concatenate(
        [
            jnp.concatenate([vals[:, :side], blank], axis=1),
            jnp.concatenate([blank, vals[:, side:]], axis=1),
        ],
        axis=0,
    )
    for k in range(0, tiles.shape[1], 2):
        right = jnp.concatenate(
            [
                jnp.concatenate([tiles[0, k], tiles[0, k + 1]], axis=1),
                jnp.concatenate([tiles[1, k], tiles[1, k + 1]], axis=1),
            ],
            axis=0,
        )
        term = jnp.dot(left, right, preferred_element_type=jnp.float32)
        for row in range(2):
            for at in range(2):
                use(row, k + at, term[row * feats : (row + 1) * feats, at * side : (at + 1) * side])


def stream_kernel(
    cols_hbm, vals_hbm, tiles_hbm, out_ref, tiles_ref, before_ref, last_ref, acc_ref, cols_ref, vals_ref, sems
):
    rows, per_row, side, _ = tiles_ref.shape
    pairs = rows // 2
    small = [
        pltpu.make_async_copy(cols_hbm, cols_ref, sems.at[pairs]),
        pltpu.make_async_copy(vals_hbm, vals_ref, sems.at[pairs + 1]),
    ]
    for copy in small:
        copy.start()

    def tiles_copy(i):
        at = pl.ds(2 * i, 2)
        return pltpu.make_async_copy(tiles_hbm.at[at], tiles_ref.at[at], sems.at[i])

    for i in range(pairs):
        tiles_copy(i).start()

    def clear(i, carry):
        for at in range(8):
            last_ref[8 * i + at] = rows * per_row
        acc_ref[pl.ds(8 * i, 8)] = jnp.zeros((8,) + acc_ref.shape[1:], acc_ref.dtype)
        return carry

    lax.fori_loop(0, acc_ref.shape[0] // 8, clear, 0)
    for copy in small:
        copy.wait()

    def body(i, carry):
        tiles_copy(i).wait()
        vals = vals_ref[:, pl.ds(pl.multiple_of(2 * side * i, 2 * side), 2 * side)]

        def use(row, k, term):
            target = cols_ref[2 * i + row, k]
            before_ref[2 * i + row, k] = last_ref[target]
            last_ref[target] = (2 * i + row) * per_row + k
            acc_ref[target] += term

        tile_terms(vals, tiles_ref.at[pl.ds(2 * i, 2)], use)
        return carry

    lax.fori_loop(0, pairs, body, 0)
    per_dev = out_ref.shape[3]
    half = out_ref.shape[4]
    for x in range(RING):
        for y in range(RING):
            got = acc_ref[pl.ds((x * RING + y) * per_dev, per_dev)].astype(out_ref.dtype)
            out_ref[0, x, y] = got[:, :half]
            out_ref[1, y, x] = got[:, half:]


def stream(block_cols, vals_t, edge_tiles):
    rows, per_row, side, _ = edge_tiles.shape
    feats = vals_t.shape[0]
    hbm = pl.BlockSpec(memory_space=pltpu.HBM)
    vmem = pl.BlockSpec(memory_space=pltpu.VMEM)
    smem = pl.BlockSpec(memory_space=pltpu.SMEM)
    return pl.pallas_call(
        stream_kernel,
        out_shape=(
            jax.ShapeDtypeStruct((2, RING, RING, rows, feats // 2, side), jnp.bfloat16),
            jax.ShapeDtypeStruct(edge_tiles.shape, edge_tiles.dtype),
            jax.ShapeDtypeStruct(block_cols.shape, jnp.int32),
            jax.ShapeDtypeStruct((rows * ROWS,), jnp.int32),
        ),
        in_specs=[hbm] * 3,
        out_specs=[vmem, vmem, smem, smem],
        scratch_shapes=[
            pltpu.VMEM((rows * ROWS, feats, side), jnp.float32),
            pltpu.SMEM(block_cols.shape, jnp.int32),
            pltpu.VMEM(vals_t.shape, vals_t.dtype),
            pltpu.SemaphoreType.DMA((rows // 2 + 2,)),
        ],
        compiler_params=pltpu.CompilerParams(vmem_limit_bytes=20 << 20),
    )(*(pltpu.with_memory_space_constraint(v, pltpu.HBM) for v in (block_cols, vals_t, edge_tiles)))


def to_pieces(grad, pieces_ref):
    _, tall, wide = pieces_ref.shape
    for p in range(ROWS):
        a, b = p // RING, p % RING
        pieces_ref[p] = grad[a * tall : (a + 1) * tall, b * wide : (b + 1) * wide].astype(pieces_ref.dtype)


def from_pieces(pieces_ref, grad_ref):
    _, tall, wide = pieces_ref.shape
    for p in range(ROWS):
        a, b = p // RING, p % RING
        grad_ref[a * tall : (a + 1) * tall, b * wide : (b + 1) * wide] = pieces_ref[p].astype(grad_ref.dtype)


def layers_kernel(
    part_ref, tiles_ref, before_ref, last_ref, weight2_ref, hidden_ref, mask_ref, weight1_ref, feats_ref,
    input_grad_ref, first_ref, second_ref,
    in1s, mids, in2s, fulls, totals, delta_ref, chain_ref, part2_ref, all_pieces, gather1, gather2,
    feats_all, reduced, wide_ref,
    r1s, r2s, rzs, rcs, rg, rb, rxz, rxc, sw, rw, sent,
):
    blk, half, side = part_ref.shape[3:]
    feats = 2 * half
    devs = fulls.shape[1]
    per_row = tiles_ref.shape[1]
    none = chain_ref.shape[0] - 1
    f32, bf16 = jnp.float32, jnp.bfloat16
    starts = [sum(GROUPS[:g]) for g in range(len(GROUPS))]

    row, col = lax.axis_index("row"), lax.axis_index("col")
    pos = (row // RING, lax.rem(row, RING))
    z, core = col // 2, lax.rem(col, 2)
    step = (1, -1, 2)
    lanes = [(h, d) for h in range(2) for d in range(2)]

    def wrap(v):
        return lax.rem(v + RING, RING)

    def plane(axis, d):
        x, y = pos
        if axis == 0:
            return (wrap(x + step[d]) * RING + y, col)
        return (x * RING + wrap(y + step[d]), col)

    def along(d):
        return (row, wrap(z + step[d]) * 2 + core)

    sibling = (row, z * 2 + 1 - core)

    def column(z_at):
        return core * RING + z_at

    held = column(z)
    peers = [(lax.rem(row + off, ROWS), col) for off in range(1, ROWS)]

    barrier = pltpu.get_barrier_semaphore()
    met = peers + [along(0), along(1), along(2), sibling]
    for dev in met:
        pl.semaphore_signal(barrier, inc=1, device_id=dev, device_id_type=MESH)
    pl.semaphore_wait(barrier, len(met))

    started = []

    def send(src, dst, recv_sem, dev):
        slot = len(started) % SENDS
        if len(started) >= SENDS:
            started[-SENDS].wait_send()
        copy = pltpu.make_async_remote_copy(
            src_ref=src, dst_ref=dst, send_sem=sent.at[slot], recv_sem=recv_sem,
            device_id=dev, device_id_type=MESH,
        )
        copy.start()
        started.append(copy)
        return copy

    def arrived(ref, recv_sem):
        pltpu.make_async_remote_copy(
            src_ref=ref, dst_ref=ref, send_sem=sent.at[0], recv_sem=recv_sem,
            device_id=sibling, device_id_type=MESH,
        ).wait_recv()

    def blocks(g, lo=None):
        if lo is None:
            return pl.ds(starts[g], GROUPS[g])
        return pl.ds(starts[g] + lo * (GROUPS[g] // 2), GROUPS[g] // 2)

    def slots(g):
        return pl.ds(starts[g] // 2, GROUPS[g] // 2)

    chain_ref[none] = jnp.zeros((feats, side), f32)
    totals[...] = jnp.zeros_like(totals)

    feats_hop, feats_hand = {}, {}

    def gather_feats():
        feats_all[col] = feats_ref[...]
        for d in (2, 0, 1):
            feats_hop[d] = send(feats_ref, feats_all.at[col], rxz.at[d], along(d))
        feats_hand[3] = send(feats_ref, feats_all.at[col], rxc.at[3], sibling)

    def pass_feats():
        for d in range(3):
            feats_hop[d].wait_recv()
            spot = feats_all.at[wrap(z - step[d]) * 2 + core]
            feats_hand[d] = send(spot, spot, rxc.at[d], sibling)

    def chain_group(g):
        def body(i, carry):
            vals = delta_ref[:, pl.ds(pl.multiple_of(2 * side * i, 2 * side), 2 * side)]

            def use(row, k, term):
                chain_ref[(2 * i + row) * per_row + k] = term + chain_ref[before_ref[2 * i + row, k]]

            tile_terms(vals, tiles_ref.at[pl.ds(2 * i, 2)], use)
            return carry

        lax.fori_loop(starts[g] // 2, (starts[g] + GROUPS[g]) // 2, body, 0)

    def chain_ends():
        def body(dev, carry):
            x, y = dev // RING, lax.rem(dev, RING)
            for b in range(blk):
                got = chain_ref[last_ref[dev * blk + b]].astype(bf16)
                part2_ref[0, x, y, b] = got[:half]
                part2_ref[1, y, x, b] = got[half:]
            return carry

        lax.fori_loop(0, ROWS, body, 0)

    out, back = {}, {}

    def send_pieces(n, src):
        for i, dev in enumerate(peers):
            out[n, i] = send(src.at[dev[0]], gather1.at[n, i], rg.at[n], dev)

    def piece_sum(n, src):
        arrived(gather1.at[n], rg.at[n])
        total = src[row].astype(f32)
        for i in range(len(peers)):
            total += gather1[n, i].astype(f32)
        return total

    def add_pieces(n, src):
        total = piece_sum(n, src)
        gather2[n, row] = total.astype(bf16)
        for i, dev in enumerate(peers):
            spot = gather2.at[n, row]
            back[n, i] = send(spot, spot, rb.at[i], dev)

    def take_pieces(n, dst):
        for i in range(len(peers)):
            back[n, i].wait_recv()
        from_pieces(gather2.at[n], dst)

    home = pos[1] == z

    def wide_copy(c):
        return pltpu.make_async_remote_copy(
            src_ref=reduced, dst_ref=wide_ref.at[col, pos[0]], send_sem=sw.at[c], recv_sem=rw.at[col, pos[0]],
            device_id=(row, pos[1] * 2 + c), device_id_type=MESH,
        )

    def nearby(act):
        for c in range(2):

            @pl.when(pos[1] * 2 + c != col)
            def _():
                act(wide_copy(c))

    def send_wide():
        reduced[...] = piece_sum(1, all_pieces.at[1]).astype(bf16)
        for c in range(2):
            for dev in peers:
                send(reduced, wide_ref.at[col, pos[0]], rw.at[col, pos[0]], (dev[0], pos[1] * 2 + c))
        nearby(lambda copy: copy.start())

        @pl.when(home)
        def _():
            wide_ref[col, pos[0]] = reduced[...]

    def take_wide():
        def body(i, carry):
            c, a = i // RING, lax.rem(i, RING)

            @pl.when(jnp.logical_not(home & (c == col) & (a == pos[0])))
            def _():
                pltpu.make_async_remote_copy(
                    src_ref=reduced, dst_ref=wide_ref.at[c, a], send_sem=sw.at[0], recv_sem=rw.at[c, a],
                    device_id=sibling, device_id_type=MESH,
                ).wait_recv()

            return carry

        lax.fori_loop(0, devs * RING, body, 0)
        wide = wide_ref[...].reshape(devs * feats, side).astype(f32).T
        first_ref[...] = jnp.where(core == 0, wide[:feats], wide[feats:])
        nearby(lambda copy: copy.wait_send())

    def layer_stages(n, part_ref, weight_ref, acts_ref, mask_ref, value_ref, pieces_ref):
        in1, mid, in2, full, total_ref = (ref.at[n] for ref in (in1s, mids, in2s, fulls, totals))
        r1, r2, rz, rc = (ref.at[n] for ref in (r1s, r2s, rzs, rcs))
        far, near, both, direct, hop, hand = ({} for _ in range(6))
        summed = []

        def send_far(g):
            for h, d in lanes:
                far[h, d, g] = send(
                    part_ref.at[h, wrap(pos[h] + 2), :, blocks(g, d)],
                    in1.at[h, d, 0, :, slots(g)], r1.at[h, d, g], plane(h, d))

        def send_near(g):
            for h, d in lanes:
                near[h, d, g] = send(
                    part_ref.at[h, wrap(pos[h] + step[d]), :, blocks(g, 1 - d)],
                    in1.at[h, d, 1, :, slots(g)], r1.at[h, 2, g], plane(h, d))

        def send_both(g):
            for h, d in lanes:
                far[h, d, g].wait_recv()
                got = in1.at[h, d, 0, :, slots(g)]
                mine = part_ref.at[h, wrap(pos[h] + step[d]), :, blocks(g, d)]

                def add(q, carry):
                    got[q] = (got[q].astype(f32) + mine[q].astype(f32)).astype(bf16)
                    return carry

                lax.fori_loop(0, RING, add, 0)
                both[h, d, g] = send(
                    got, in1.at[h, d, 2, :, slots(g)], r1.at[h, 2, g], plane(h, d))

        def second_ring(g):
            for h in range(2):
                other = pos[1 - h]
                arrived(in1.at[h, :, pl.ds(1, 2), :, slots(g)], r1.at[h, 2, g])

                def add(q, carry):
                    for lo in range(2):
                        total = part_ref[h, pos[h], q, blocks(g, lo)].astype(f32)
                        total += in1[h, lo, 2, q, slots(g)].astype(f32)
                        total += in1[h, 1 - lo, 1, q, slots(g)].astype(f32)
                        mid[h, q, blocks(g, lo)] = total.astype(bf16)
                    return carry

                lax.fori_loop(0, RING, add, 0)
                for d in (2, 0, 1):
                    direct[h, d, g] = send(
                        mid.at[h, wrap(other + step[d]), blocks(g)],
                        in2.at[h, d, blocks(g)], r2.at[h, g], plane(1 - h, d))

        def give(c, g, key):
            spot = full.at[c, :, blocks(g)]
            hand[key, g] = send(spot, spot, rc.at[g], sibling)

        def finish(g):
            for h in range(2):
                other = pos[1 - h]
                total = mid[h, other, blocks(g)].astype(f32)
                arrived(in2.at[h, :, blocks(g)], r2.at[h, g])
                for d in range(3):
                    total += in2[h, d, blocks(g)].astype(f32)
                full[held, h, blocks(g)] = total.astype(bf16)
            for d in (2, 0, 1):
                spot = full.at[held, :, blocks(g)]
                hop[d, g] = send(spot, spot, rz.at[d, g], along(d))
            give(held, g, 3)
            if n == 1:
                def pair(i, carry):
                    b, at = pair_at(g, i)
                    left = jnp.concatenate(
                        [
                            jnp.concatenate([full[held, h, b + k] for h in range(2)], axis=0)
                            for k in range(2)
                        ],
                        axis=1,
                    )
                    add_grad(left, feats_all[:, :, at].reshape(devs * feats, 2 * side))
                    return carry

                lax.fori_loop(0, GROUPS[g] // 2, pair, 0)
                count_grad(g)

        def pass_on(g):
            for d in (0, 1, 2):
                hop[d, g].wait_recv()
                give(column(wrap(z - step[d])), g, d)

        def pair_at(g, i):
            b = starts[g] + 2 * i
            return b, pl.ds(pl.multiple_of(b * side, 2 * side), 2 * side)

        def add_grad(left, right):
            total_ref[...] += lax.dot_general(
                left, right, (((1,), (1,)), ((), ())), preferred_element_type=f32
            )

        def count_grad(g):
            summed.append(g)
            if len(summed) == len(GROUPS):
                to_pieces(total_ref, pieces_ref)
                send_pieces(n, pieces_ref)

        def products(g):
            arrived(full.at[pl.ds((1 - core) * RING, RING), :, blocks(g)], rc.at[g])
            order = [c % 2 * RING + c // 2 for c in range(devs)]

            def pair(i, carry):
                b, at = pair_at(g, i)
                right = jnp.concatenate(
                    [
                        jnp.concatenate([full[c, h, b + k] for c in order for h in range(2)], axis=0)
                        for k in range(2)
                    ],
                    axis=1,
                )
                value = jnp.dot(weight_ref[...], right, preferred_element_type=f32)
                if mask_ref is not None:
                    value = value * mask_ref[:, at].astype(f32)
                value_ref[:, at] = value.astype(bf16)
                if n == 0:
                    add_grad(acts_ref[:, at], right)
                return carry

            lax.fori_loop(0, GROUPS[g] // 2, pair, 0)
            if n == 0:
                count_grad(g)
                chain_group(g)

        return dict(
            f=send_far, o=send_near, b=send_both, c=second_ring, e=finish, h=pass_on, p=products,
        )

    stages = layer_stages(0, part_ref, weight2_ref, hidden_ref, mask_ref, delta_ref, all_pieces.at[0])
    for at, word in enumerate(ORDER_ONE):
        stages[word[0]](int(word[1:]))
        if at == 2:
            gather_feats()
        if at == len(ORDER_ONE) - 6:
            pass_feats()
    chain_ends()
    stages = layer_stages(1, part2_ref, weight1_ref, feats_ref, None, input_grad_ref, all_pieces.at[1])
    for at, word in enumerate(ORDER_TWO):
        if word == "a0":
            send_wide()
        else:
            stages[word[0]](int(word[1:]))
        if at == len(ORDER_TWO) // 4:
            add_pieces(0, all_pieces.at[0])
            for key in range(4):
                feats_hand[key].wait_recv()
        if at == len(ORDER_TWO) // 2:
            take_pieces(0, second_ref)
    take_wide()
    for copy in started[-SENDS:]:
        copy.wait_send()


def layers(part, tiles, before, last, weight_two, hidden_t, mask_t, weight_one, feats_t):
    blk, half, side = part.shape[3:]
    feats, rows = feats_t.shape
    devs = weight_one.shape[1] // feats
    groups = len(GROUPS)
    vmem = pl.BlockSpec(memory_space=pltpu.VMEM)
    smem = pl.BlockSpec(memory_space=pltpu.SMEM)
    dma = pltpu.SemaphoreType.DMA
    bf16, f32 = jnp.bfloat16, jnp.float32
    grad = (feats, devs * feats)
    pieces = (ROWS, feats // RING, devs * feats // RING)
    scratch = [
        pltpu.VMEM((2, 2, 2, 3, RING, blk // 2, half, side), bf16),
        pltpu.VMEM((2, 2, RING, blk, half, side), bf16),
        pltpu.VMEM((2, 2, 3, blk, half, side), bf16),
        pltpu.VMEM((2, devs, 2, blk, half, side), bf16),
        pltpu.VMEM((2,) + grad, f32),
        pltpu.VMEM((feats, rows), bf16),
        pltpu.VMEM((before.size + 1, feats, side), f32),
        pltpu.VMEM(part.shape, bf16),
        pltpu.VMEM((2,) + pieces, bf16),
        pltpu.VMEM((2, ROWS - 1) + pieces[1:], bf16),
        pltpu.VMEM((2,) + pieces, bf16),
        pltpu.VMEM((devs, feats, rows), bf16),
        pltpu.VMEM(pieces[1:], bf16),
        pltpu.VMEM((devs, RING) + pieces[1:], bf16),
    ]
    for shape in ((2, 3), (2,), (3,), ()):
        scratch += [dma((2,) + shape + (groups,))]
    scratch += [dma((2,)), dma((ROWS - 1,)), dma((3,)), dma((4,))]
    scratch += [dma((2,)), dma((devs, RING)), dma((SENDS,))]
    return pl.pallas_call(
        layers_kernel,
        out_shape=(
            jax.ShapeDtypeStruct((feats, rows), bf16),
            jax.ShapeDtypeStruct(grad, f32),
            jax.ShapeDtypeStruct(grad, f32),
        ),
        in_specs=[vmem, vmem, smem, smem] + [vmem] * 5,
        out_specs=[vmem] * 3,
        scratch_shapes=scratch,
        compiler_params=pltpu.CompilerParams(
            collective_id=0, has_side_effects=True, vmem_limit_bytes=36 << 20
        ),
    )(part, tiles, before, last, weight_two, hidden_t, mask_t, weight_one, feats_t)


def per_device(
    node_feats, hidden_act, grad_out, relu_mask, edge_tiles, block_cols, weight_one, weight_two
):
    part, tiles, before, last = stream(block_cols, grad_out.T, edge_tiles)
    input_grad_t, first_grad, second_grad = layers(
        part, tiles, before, last, weight_two, hidden_act.T, relu_mask.T, weight_one, node_feats.T
    )
    return (input_grad_t.T, first_grad, second_grad)


def solution(mesh):
    in_specs = (
        P("row", "col"),
        P("row", "col"),
        P("row", "col"),
        P("row", "col"),
        P("row", None, None, None),
        P("row", None),
        P("col", None),
        P("col", None),
    )
    out_specs = (P("row", "col"), P("col", None), P("col", None))
    return jax.shard_map(
        per_device, mesh=mesh, in_specs=in_specs, out_specs=out_specs, check_vma=False
    )
```

```python
import functools
import jax
import jax.numpy as jnp
from jax import lax
from jax.experimental import pallas as pl
from jax.experimental.pallas import tpu as pltpu
from jax.sharding import PartitionSpec as P

RING = 4
ROWS = RING * RING
GROUPS = (4, 4, 4, 2, 2)
ORDER_ONE = (
    "f0", "f1", "o0", "f2", "b0", "f3", "b1", "o1", "c0", "o2", "b2", "c1",
    "f4", "o3", "e0", "b3", "c2", "e1", "b4", "o4", "c3", "e2", "h0", "c4",
    "e3", "h1", "p0", "e4", "h2", "p1", "h3", "p2", "h4", "p3", "p4",
)
ORDER_TWO = (
    "o4", "f0", "f2", "f1", "o2", "o1", "b0", "b2", "f4", "f3", "o0", "b1",
    "b4", "c2", "b3", "o3", "c0", "c1", "c4", "e2", "c3", "e0", "e1", "e4",
    "e3", "h2", "p2", "h0", "a0", "h1", "p0", "h4", "h3", "p4", "p1", "p3",
)
SENDS = 32
MESH = pl.DeviceIdType.MESH


def tile_terms(vals, tiles, use):
    feats = vals.shape[0]
    side = tiles.shape[2]
    blank = jnp.zeros((feats, side), vals.dtype)
    left = jnp.concatenate(
        [
            jnp.concatenate([vals[:, :side], blank], axis=1),
            jnp.concatenate([blank, vals[:, side:]], axis=1),
        ],
        axis=0,
    )
    for k in range(0, tiles.shape[1], 2):
        right = jnp.concatenate(
            [
                jnp.concatenate([tiles[0, k], tiles[0, k + 1]], axis=1),
                jnp.concatenate([tiles[1, k], tiles[1, k + 1]], axis=1),
            ],
            axis=0,
        )
        term = jnp.dot(left, right, preferred_element_type=jnp.float32)
        for row in range(2):
            for at in range(2):
                use(row, k + at, term[row * feats : (row + 1) * feats, at * side : (at + 1) * side])


def stream_kernel(
    cols_hbm, vals_hbm, tiles_hbm, out_ref, tiles_ref, before_ref, last_ref, acc_ref, cols_ref, vals_ref, sems
):
    rows, per_row, side, _ = tiles_ref.shape
    pairs = rows // 2
    small = [
        pltpu.make_async_copy(cols_hbm, cols_ref, sems.at[pairs]),
        pltpu.make_async_copy(vals_hbm, vals_ref, sems.at[pairs + 1]),
    ]
    for copy in small:
        copy.start()

    def tiles_copy(i):
        at = pl.ds(2 * i, 2)
        return pltpu.make_async_copy(tiles_hbm.at[at], tiles_ref.at[at], sems.at[i])

    for i in range(pairs):
        tiles_copy(i).start()

    def clear(i, carry):
        for at in range(8):
            last_ref[8 * i + at] = rows * per_row
        acc_ref[pl.ds(8 * i, 8)] = jnp.zeros((8,) + acc_ref.shape[1:], acc_ref.dtype)
        return carry

    lax.fori_loop(0, acc_ref.shape[0] // 8, clear, 0)
    for copy in small:
        copy.wait()

    def body(i, carry):
        tiles_copy(i).wait()
        vals = vals_ref[:, pl.ds(pl.multiple_of(2 * side * i, 2 * side), 2 * side)]

        def use(row, k, term):
            target = cols_ref[2 * i + row, k]
            before_ref[2 * i + row, k] = last_ref[target]
            last_ref[target] = (2 * i + row) * per_row + k
            acc_ref[target] += term

        tile_terms(vals, tiles_ref.at[pl.ds(2 * i, 2)], use)
        return carry

    lax.fori_loop(0, pairs, body, 0)
    per_dev = out_ref.shape[3]
    half = out_ref.shape[4]
    for x in range(RING):
        for y in range(RING):
            got = acc_ref[pl.ds((x * RING + y) * per_dev, per_dev)].astype(out_ref.dtype)
            out_ref[0, x, y] = got[:, :half]
            out_ref[1, y, x] = got[:, half:]


def stream(block_cols, vals_t, edge_tiles):
    rows, per_row, side, _ = edge_tiles.shape
    feats = vals_t.shape[0]
    hbm = pl.BlockSpec(memory_space=pltpu.HBM)
    vmem = pl.BlockSpec(memory_space=pltpu.VMEM)
    smem = pl.BlockSpec(memory_space=pltpu.SMEM)
    return pl.pallas_call(
        stream_kernel,
        out_shape=(
            jax.ShapeDtypeStruct((2, RING, RING, rows, feats // 2, side), jnp.bfloat16),
            jax.ShapeDtypeStruct(edge_tiles.shape, edge_tiles.dtype),
            jax.ShapeDtypeStruct(block_cols.shape, jnp.int32),
            jax.ShapeDtypeStruct((rows * ROWS,), jnp.int32),
        ),
        in_specs=[hbm] * 3,
        out_specs=[vmem, vmem, smem, smem],
        scratch_shapes=[
            pltpu.VMEM((rows * ROWS, feats, side), jnp.float32),
            pltpu.SMEM(block_cols.shape, jnp.int32),
            pltpu.VMEM(vals_t.shape, vals_t.dtype),
            pltpu.SemaphoreType.DMA((rows // 2 + 2,)),
        ],
        compiler_params=pltpu.CompilerParams(vmem_limit_bytes=20 << 20),
    )(*(pltpu.with_memory_space_constraint(v, pltpu.HBM) for v in (block_cols, vals_t, edge_tiles)))


def to_pieces(grad, pieces_ref):
    _, tall, wide = pieces_ref.shape
    for p in range(ROWS):
        a, b = p // RING, p % RING
        pieces_ref[p] = grad[a * tall : (a + 1) * tall, b * wide : (b + 1) * wide].astype(pieces_ref.dtype)


def from_pieces(pieces_ref, grad_ref):
    _, tall, wide = pieces_ref.shape
    for p in range(ROWS):
        a, b = p // RING, p % RING
        grad_ref[a * tall : (a + 1) * tall, b * wide : (b + 1) * wide] = pieces_ref[p].astype(grad_ref.dtype)


def layers_kernel(
    part_ref, tiles_ref, before_ref, last_ref, weight2_ref, hidden_ref, mask_ref, weight1_ref, feats_ref,
    input_grad_ref, first_ref, second_ref,
    in1s, mids, in2s, fulls, totals, delta_ref, chain_ref, part2_ref, all_pieces, gather1, gather2,
    feats_all, reduced, wide_ref,
    r1s, r2s, rzs, rcs, rg, rb, rxz, rxc, sw, rw, sent,
):
    blk, half, side = part_ref.shape[3:]
    feats = 2 * half
    devs = fulls.shape[1]
    per_row = tiles_ref.shape[1]
    none = chain_ref.shape[0] - 1
    f32, bf16 = jnp.float32, jnp.bfloat16
    starts = [sum(GROUPS[:g]) for g in range(len(GROUPS))]

    row, col = lax.axis_index("row"), lax.axis_index("col")
    pos = (row // RING, lax.rem(row, RING))
    z, core = col // 2, lax.rem(col, 2)
    step = (1, -1, 2)
    lanes = [(h, d) for h in range(2) for d in range(2)]

    def wrap(v):
        return lax.rem(v + RING, RING)

    def plane(axis, d):
        x, y = pos
        if axis == 0:
            return (wrap(x + step[d]) * RING + y, col)
        return (x * RING + wrap(y + step[d]), col)

    def along(d):
        return (row, wrap(z + step[d]) * 2 + core)

    sibling = (row, z * 2 + 1 - core)

    def column(z_at):
        return core * RING + z_at

    held = column(z)
    peers = [(lax.rem(row + off, ROWS), col) for off in range(1, ROWS)]

    barrier = pltpu.get_barrier_semaphore()
    met = peers + [along(0), along(1), along(2), sibling]
    for dev in met:
        pl.semaphore_signal(barrier, inc=1, device_id=dev, device_id_type=MESH)
    pl.semaphore_wait(barrier, len(met))

    started = []

    def send(src, dst, recv_sem, dev):
        slot = len(started) % SENDS
        if len(started) >= SENDS:
            started[-SENDS].wait_send()
        copy = pltpu.make_async_remote_copy(
            src_ref=src, dst_ref=dst, send_sem=sent.at[slot], recv_sem=recv_sem,
            device_id=dev, device_id_type=MESH,
        )
        copy.start()
        started.append(copy)
        return copy

    def arrived(ref, recv_sem):
        pltpu.make_async_remote_copy(
            src_ref=ref, dst_ref=ref, send_sem=sent.at[0], recv_sem=recv_sem,
            device_id=sibling, device_id_type=MESH,
        ).wait_recv()

    def blocks(g, lo=None):
        if lo is None:
            return pl.ds(starts[g], GROUPS[g])
        return pl.ds(starts[g] + lo * (GROUPS[g] // 2), GROUPS[g] // 2)

    def slots(g):
        return pl.ds(starts[g] // 2, GROUPS[g] // 2)

    chain_ref[none] = jnp.zeros((feats, side), f32)
    totals[...] = jnp.zeros_like(totals)

    feats_hop, feats_hand = {}, {}

    def gather_feats():
        feats_all[col] = feats_ref[...]
        for d in (2, 0, 1):
            feats_hop[d] = send(feats_ref, feats_all.at[col], rxz.at[d], along(d))
        feats_hand[3] = send(feats_ref, feats_all.at[col], rxc.at[3], sibling)

    def pass_feats():
        for d in range(3):
            feats_hop[d].wait_recv()
            spot = feats_all.at[wrap(z - step[d]) * 2 + core]
            feats_hand[d] = send(spot, spot, rxc.at[d], sibling)

    def chain_group(g):
        def body(i, carry):
            vals = delta_ref[:, pl.ds(pl.multiple_of(2 * side * i, 2 * side), 2 * side)]

            def use(row, k, term):
                chain_ref[(2 * i + row) * per_row + k] = term + chain_ref[before_ref[2 * i + row, k]]

            tile_terms(vals, tiles_ref.at[pl.ds(2 * i, 2)], use)
            return carry

        lax.fori_loop(starts[g] // 2, (starts[g] + GROUPS[g]) // 2, body, 0)

    def chain_ends():
        def body(dev, carry):
            x, y = dev // RING, lax.rem(dev, RING)
            for b in range(blk):
                got = chain_ref[last_ref[dev * blk + b]].astype(bf16)
                part2_ref[0, x, y, b] = got[:half]
                part2_ref[1, y, x, b] = got[half:]
            return carry

        lax.fori_loop(0, ROWS, body, 0)

    out, back = {}, {}

    def send_pieces(n, src):
        for i, dev in enumerate(peers):
            out[n, i] = send(src.at[dev[0]], gather1.at[n, i], rg.at[n], dev)

    def piece_sum(n, src):
        arrived(gather1.at[n], rg.at[n])
        total = src[row].astype(f32)
        for i in range(len(peers)):
            total += gather1[n, i].astype(f32)
        return total

    def add_pieces(n, src):
        total = piece_sum(n, src)
        gather2[n, row] = total.astype(bf16)
        for i, dev in enumerate(peers):
            spot = gather2.at[n, row]
            back[n, i] = send(spot, spot, rb.at[i], dev)

    def take_pieces(n, dst):
        for i in range(len(peers)):
            back[n, i].wait_recv()
        from_pieces(gather2.at[n], dst)

    home = pos[1] == z

    def wide_copy(c):
        return pltpu.make_async_remote_copy(
            src_ref=reduced, dst_ref=wide_ref.at[col, pos[0]], send_sem=sw.at[c], recv_sem=rw.at[col, pos[0]],
            device_id=(row, pos[1] * 2 + c), device_id_type=MESH,
        )

    def nearby(act):
        for c in range(2):

            @pl.when(pos[1] * 2 + c != col)
            def _():
                act(wide_copy(c))

    def send_wide():
        reduced[...] = piece_sum(1, all_pieces.at[1]).astype(bf16)
        for c in range(2):
            for dev in peers:
                send(reduced, wide_ref.at[col, pos[0]], rw.at[col, pos[0]], (dev[0], pos[1] * 2 + c))
        nearby(lambda copy: copy.start())

        @pl.when(home)
        def _():
            wide_ref[col, pos[0]] = reduced[...]

    def take_wide():
        def body(i, carry):
            c, a = i // RING, lax.rem(i, RING)

            @pl.when(jnp.logical_not(home & (c == col) & (a == pos[0])))
            def _():
                pltpu.make_async_remote_copy(
                    src_ref=reduced, dst_ref=wide_ref.at[c, a], send_sem=sw.at[0], recv_sem=rw.at[c, a],
                    device_id=sibling, device_id_type=MESH,
                ).wait_recv()

            return carry

        lax.fori_loop(0, devs * RING, body, 0)
        wide = wide_ref[...].reshape(devs * feats, side).astype(f32).T
        first_ref[...] = jnp.where(core == 0, wide[:feats], wide[feats:])
        nearby(lambda copy: copy.wait_send())

    def layer_stages(n, part_ref, weight_ref, acts_ref, mask_ref, value_ref, pieces_ref):
        in1, mid, in2, full, total_ref = (ref.at[n] for ref in (in1s, mids, in2s, fulls, totals))
        r1, r2, rz, rc = (ref.at[n] for ref in (r1s, r2s, rzs, rcs))
        far, near, both, direct, hop, hand = ({} for _ in range(6))
        summed = []

        def send_far(g):
            for h, d in lanes:
                far[h, d, g] = send(
                    part_ref.at[h, wrap(pos[h] + 2), :, blocks(g, d)],
                    in1.at[h, d, 0, :, slots(g)], r1.at[h, d, g], plane(h, d))

        def send_near(g):
            for h, d in lanes:
                near[h, d, g] = send(
                    part_ref.at[h, wrap(pos[h] + step[d]), :, blocks(g, 1 - d)],
                    in1.at[h, d, 1, :, slots(g)], r1.at[h, 2, g], plane(h, d))

        def send_both(g):
            for h, d in lanes:
                far[h, d, g].wait_recv()
                got = in1.at[h, d, 0, :, slots(g)]
                mine = part_ref.at[h, wrap(pos[h] + step[d]), :, blocks(g, d)]

                def add(q, carry):
                    got[q] = (got[q].astype(f32) + mine[q].astype(f32)).astype(bf16)
                    return carry

                lax.fori_loop(0, RING, add, 0)
                both[h, d, g] = send(
                    got, in1.at[h, d, 2, :, slots(g)], r1.at[h, 2, g], plane(h, d))

        def second_ring(g):
            for h in range(2):
                other = pos[1 - h]
                arrived(in1.at[h, :, pl.ds(1, 2), :, slots(g)], r1.at[h, 2, g])

                def add(q, carry):
                    for lo in range(2):
                        total = part_ref[h, pos[h], q, blocks(g, lo)].astype(f32)
                        total += in1[h, lo, 2, q, slots(g)].astype(f32)
                        total += in1[h, 1 - lo, 1, q, slots(g)].astype(f32)
                        mid[h, q, blocks(g, lo)] = total.astype(bf16)
                    return carry

                lax.fori_loop(0, RING, add, 0)
                for d in (2, 0, 1):
                    direct[h, d, g] = send(
                        mid.at[h, wrap(other + step[d]), blocks(g)],
                        in2.at[h, d, blocks(g)], r2.at[h, g], plane(1 - h, d))

        def give(c, g, key):
            spot = full.at[c, :, blocks(g)]
            hand[key, g] = send(spot, spot, rc.at[g], sibling)

        def finish(g):
            for h in range(2):
                other = pos[1 - h]
                total = mid[h, other, blocks(g)].astype(f32)
                arrived(in2.at[h, :, blocks(g)], r2.at[h, g])
                for d in range(3):
                    total += in2[h, d, blocks(g)].astype(f32)
                full[held, h, blocks(g)] = total.astype(bf16)
            for d in (2, 0, 1):
                spot = full.at[held, :, blocks(g)]
                hop[d, g] = send(spot, spot, rz.at[d, g], along(d))
            give(held, g, 3)
            if n == 1:
                def pair(i, carry):
                    b, at = pair_at(g, i)
                    left = jnp.concatenate(
                        [
                            jnp.concatenate([full[held, h, b + k] for h in range(2)], axis=0)
                            for k in range(2)
                        ],
                        axis=1,
                    )
                    add_grad(left, feats_all[:, :, at].reshape(devs * feats, 2 * side))
                    return carry

                lax.fori_loop(0, GROUPS[g] // 2, pair, 0)
                count_grad(g)

        def pass_on(g):
            for d in (0, 1, 2):
                hop[d, g].wait_recv()
                give(column(wrap(z - step[d])), g, d)

        def pair_at(g, i):
            b = starts[g] + 2 * i
            return b, pl.ds(pl.multiple_of(b * side, 2 * side), 2 * side)

        def add_grad(left, right):
            total_ref[...] += lax.dot_general(
                left, right, (((1,), (1,)), ((), ())), preferred_element_type=f32
            )

        def count_grad(g):
            summed.append(g)
            if len(summed) == len(GROUPS):
                to_pieces(total_ref, pieces_ref)
                send_pieces(n, pieces_ref)

        def products(g):
            arrived(full.at[pl.ds((1 - core) * RING, RING), :, blocks(g)], rc.at[g])
            order = [c % 2 * RING + c // 2 for c in range(devs)]

            def pair(i, carry):
                b, at = pair_at(g, i)
                right = jnp.concatenate(
                    [
                        jnp.concatenate([full[c, h, b + k] for c in order for h in range(2)], axis=0)
                        for k in range(2)
                    ],
                    axis=1,
                )
                value = jnp.dot(weight_ref[...], right, preferred_element_type=f32)
                if mask_ref is not None:
                    value = value * mask_ref[:, at].astype(f32)
                value_ref[:, at] = value.astype(bf16)
                if n == 0:
                    add_grad(acts_ref[:, at], right)
                return carry

            lax.fori_loop(0, GROUPS[g] // 2, pair, 0)
            if n == 0:
                count_grad(g)
                chain_group(g)

        return dict(
            f=send_far, o=send_near, b=send_both, c=second_ring, e=finish, h=pass_on, p=products,
        )

    stages = layer_stages(0, part_ref, weight2_ref, hidden_ref, mask_ref, delta_ref, all_pieces.at[0])
    for at, word in enumerate(ORDER_ONE):
        stages[word[0]](int(word[1:]))
        if at == 2:
            gather_feats()
        if at == len(ORDER_ONE) - 6:
            pass_feats()
    chain_ends()
    stages = layer_stages(1, part2_ref, weight1_ref, feats_ref, None, input_grad_ref, all_pieces.at[1])
    for at, word in enumerate(ORDER_TWO):
        if word == "a0":
            send_wide()
        else:
            stages[word[0]](int(word[1:]))
        if at == len(ORDER_TWO) // 4:
            add_pieces(0, all_pieces.at[0])
            for key in range(4):
                feats_hand[key].wait_recv()
        if at == len(ORDER_TWO) // 2:
            take_pieces(0, second_ref)
    take_wide()
    for copy in started[-SENDS:]:
        copy.wait_send()


def layers(part, tiles, before, last, weight_two, hidden_t, mask_t, weight_one, feats_t):
    blk, half, side = part.shape[3:]
    feats, rows = feats_t.shape
    devs = weight_one.shape[1] // feats
    groups = len(GROUPS)
    vmem = pl.BlockSpec(memory_space=pltpu.VMEM)
    smem = pl.BlockSpec(memory_space=pltpu.SMEM)
    dma = pltpu.SemaphoreType.DMA
    bf16, f32 = jnp.bfloat16, jnp.float32
    grad = (feats, devs * feats)
    pieces = (ROWS, feats // RING, devs * feats // RING)
    scratch = [
        pltpu.VMEM((2, 2, 2, 3, RING, blk // 2, half, side), bf16),
        pltpu.VMEM((2, 2, RING, blk, half, side), bf16),
        pltpu.VMEM((2, 2, 3, blk, half, side), bf16),
        pltpu.VMEM((2, devs, 2, blk, half, side), bf16),
        pltpu.VMEM((2,) + grad, f32),
        pltpu.VMEM((feats, rows), bf16),
        pltpu.VMEM((before.size + 1, feats, side), f32),
        pltpu.VMEM(part.shape, bf16),
        pltpu.VMEM((2,) + pieces, bf16),
        pltpu.VMEM((2, ROWS - 1) + pieces[1:], bf16),
        pltpu.VMEM((2,) + pieces, bf16),
        pltpu.VMEM((devs, feats, rows), bf16),
        pltpu.VMEM(pieces[1:], bf16),
        pltpu.VMEM((devs, RING) + pieces[1:], bf16),
    ]
    for shape in ((2, 3), (2,), (3,), ()):
        scratch += [dma((2,) + shape + (groups,))]
    scratch += [dma((2,)), dma((ROWS - 1,)), dma((3,)), dma((4,))]
    scratch += [dma((2,)), dma((devs, RING)), dma((SENDS,))]
    return pl.pallas_call(
        layers_kernel,
        out_shape=(
            jax.ShapeDtypeStruct((feats, rows), bf16),
            jax.ShapeDtypeStruct(grad, f32),
            jax.ShapeDtypeStruct(grad, f32),
        ),
        in_specs=[vmem, vmem, smem, smem] + [vmem] * 5,
        out_specs=[vmem] * 3,
        scratch_shapes=scratch,
        compiler_params=pltpu.CompilerParams(
            collective_id=0, has_side_effects=True, vmem_limit_bytes=36 << 20
        ),
    )(part, tiles, before, last, weight_two, hidden_t, mask_t, weight_one, feats_t)


def per_device(
    node_feats, hidden_act, grad_out, relu_mask, edge_tiles, block_cols, weight_one, weight_two
):
    part, tiles, before, last = stream(block_cols, grad_out.T, edge_tiles)
    input_grad_t, first_grad, second_grad = layers(
        part, tiles, before, last, weight_two, hidden_act.T, relu_mask.T, weight_one, node_feats.T
    )
    return (input_grad_t.T, first_grad, second_grad)


def solution(mesh):
    in_specs = (
        P("row", "col"),
        P("row", "col"),
        P("row", "col"),
        P("row", "col"),
        P("row", None, None, None),
        P("row", None),
        P("col", None),
        P("col", None),
    )
    out_specs = (P("row", "col"), P("col", None), P("col", None))
    return jax.shard_map(
        per_device, mesh=mesh, in_specs=in_specs, out_specs=out_specs, check_vma=False
    )
```
